32 devices in a mesh: ctx: 4 (over y, x), fsdp: 8 (over z, core).
Axes of the slice: x: 2, y: 2, z: 4, core: 2. Of those that a mesh axis runs over, the one named last changes fastest.
Arguments:
- tokens: bfloat16 [8, 1024, 2048], P('fsdp', 'ctx'), may hold values from -6 to 6
- block_ids: int32 [8, 1024], P('fsdp'), may hold values from 0 to 7, never falling along the last dimension, each value on 1 to 256 neighbouring positions
- piece_order: int32 [8], replicated, may hold values from 0 to 7, as said below
- norm1_gain: float32 [2048], replicated, may hold values from 0.5 to 1.5
- norm1_bias: float32 [2048], replicated, may hold values from -1 to 1
- w_qkv: bfloat16 [2048, 6144], P('fsdp'), may hold values from -0.125 to 0.125
- w_out: bfloat16 [2048, 2048], P('fsdp'), may hold values from -1 to 1
- norm2_gain: float32 [2048], replicated, may hold values from 0.5 to 1.5
- norm2_bias: float32 [2048], replicated, may hold values from -1 to 1
- w_up: bfloat16 [2048, 8192], P('fsdp'), may hold values from -0.125 to 0.125
- w_down: bfloat16 [2048, 8192], P('fsdp'), may hold values from -0.0625 to 0.0625
- grad_out: bfloat16 [8, 1024, 2048], P('fsdp', 'ctx'), may hold values from -6 to 6
Outputs:
- mixed: bfloat16 [8, 1024, 2048], P('fsdp', 'ctx')
- grad_tokens: bfloat16 [8, 1024, 2048], P('fsdp', 'ctx')
- grad_qkv: float32 [2048, 6144], P(('ctx', 'fsdp'))
- grad_wout: float32 [2048, 2048], P(('ctx', 'fsdp'))
- grad_up: float32 [2048, 8192], P(('ctx', 'fsdp'))
- grad_down: float32 [2048, 8192], P(('ctx', 'fsdp'))
- grad_norm1_gain: float32 [2048], replicated
- grad_norm1_bias: float32 [2048], replicated
- grad_norm2_gain: float32 [2048], replicated
- grad_norm2_bias: float32 [2048], replicated
The draws below stay inside these ranges and needn't reach their ends.
Inputs may be any that keep to these rules, and one draw needn't show every extreme that they name: `block_ids`: within a sequence the block numbers never fall along positions; every block covers 1 to 256 positions and some block exactly 256. `piece_order`: each piece appears once; stored pieces 2c and 2c + 1 hold pieces p and 7 - p for some p.
All inputs are finite; a program needn't handle non-finite values.
Results may differ from the reference program's by a relative error of at most 0.014.
Values may be sent and summed in bfloat16 or wider, within the bound.
A program may use at most 896 MiB of HBM per device.

```python
import math
import jax
import jax.numpy as jnp
import numpy as np
from jax import lax

D = 2048
HEADS = 16
HEAD = 128
FF = 8192
BLOCK = 256
LENGTH = 1024
ROWS = 256
PIECE = 128
PIECES = 8
BATCH = 8
NBLOCKS = 8


def draw_piece_order(key, part):
    key_pairs, key_flip = jax.random.split(jax.random.fold_in(key, 7))
    half_count = PIECES // 2
    pair_first = jax.random.permutation(key_pairs, half_count).astype(jnp.int32)
    flipped = jax.random.randint(key_flip, (half_count,), 0, 2, dtype=jnp.int32)
    pair_second = (PIECES - 1 - pair_first).astype(jnp.int32)
    lead_piece = jnp.where(flipped == 1, pair_second, pair_first)
    tail_piece = jnp.where(flipped == 1, pair_first, pair_second)
    return jnp.stack([lead_piece, tail_piece], axis=1).reshape(PIECES).astype(jnp.int32)


def draw_grad_out(key, part):
    key_main = jax.random.fold_in(jax.random.fold_in(key, 11), 0)
    group_count = PIECES // 2
    stored_rows = jnp.arange(LENGTH, dtype=jnp.int32) // ROWS
    device_pos = stored_rows[None, :] * BATCH + jnp.arange(BATCH, dtype=jnp.int32)[:, None]
    row_ramp = 0.5 + device_pos.astype(jnp.float32) / (group_count * BATCH - 1)
    full_shape = (BATCH, LENGTH, D)
    noise_vals = jnp.clip(jax.random.normal(key_main, full_shape, jnp.float32), -4.0, 4.0)
    scaled = noise_vals * row_ramp[:, :, None]
    return jnp.clip(scaled, -6.0, 6.0).astype(jnp.bfloat16)


def level_of(own_key, extent, cuts, low, top_value):
    gain, own = 1.0, jax.random.fold_in(own_key, 6)
    for position, parts in cuts:
        heights = jnp.exp(jax.random.uniform(jax.random.fold_in(own, position), (parts,), jnp.float32, low / len(cuts), top_value / len(cuts)))
        gain = gain * jnp.repeat(heights, extent[position] // parts).reshape([-1 if axis == position else 1 for axis in range(len(extent))])
    return gain


def profile(amount, total, reach, lean):
    loads = [(1 << 20) // math.isqrt(standing ** lean) + 1 for standing in range(2, amount + 1)]
    surplus, given = total - reach - (amount - 1), [1] * (amount - 1)
    while surplus > 0:
        free = [i for i in range(amount - 1) if given[i] < reach]
        pool, budget = sum([loads[i] for i in free]), surplus
        for i in free:
            addition = min(reach - given[i], max(1, budget * loads[i] // pool), surplus)
            given[i] = given[i] + addition
            surplus = surplus - addition
    return np.array([reach] + given)


def uneven_parts(stream_key, count, total, most, skew):
    if count == 2:
        one = jax.random.randint(stream_key, (), max(1, total - most), min(most, total - 1) + 1)
        return jnp.stack([one, total - one])
    tallies = jnp.asarray(profile(count, total, most, skew), jnp.int32)
    twos = (count - 1) // 2
    giver, taker = tallies[1:1 + 2 * twos:2], tallies[2:2 + 2 * twos:2]
    room = jnp.minimum(giver - 1, most - taker)
    passed = jax.random.randint(jax.random.fold_in(stream_key, 1), (twos,), 0, 1 << 20) % (room + 1)
    tallies = tallies.at[1:1 + 2 * twos:2].set(giver - passed).at[2:2 + 2 * twos:2].set(taker + passed)
    return tallies[jax.random.permutation(jax.random.fold_in(stream_key, 2), count)]


def noise(own_key, shape, spread, reach, cuts=(), kind=jnp.bfloat16):
    result = jax.random.normal(own_key, shape, jnp.float32) * spread
    if len(cuts) > 0:
        result = level_of(own_key, shape, cuts, -0.22, 0.18) * result
    return jnp.clip(result, min=-reach, max=reach).astype(kind)


def setup_inputs(seed: int = 0) -> dict:
    keys = jax.random.split(jax.random.key(seed), 13)
    tokens = noise(keys[0], (BATCH, LENGTH, D), 1.0, 6.0, ((0, 8), (1, 4)))
    block_ids = jax.vmap(lambda own: jnp.searchsorted(jnp.cumsum(uneven_parts(own, NBLOCKS, LENGTH, BLOCK, 2)), jnp.arange(LENGTH), side="right"))(jax.random.split(keys[1], BATCH)).reshape((BATCH, LENGTH)).astype(jnp.int32)
    piece_order = draw_piece_order(jax.random.fold_in(keys[12], 71), 0)
    norm1_gain = jnp.clip(1.0 + 0.1 * jax.random.normal(keys[3], (D,), jnp.float32), 0.5, 1.5)
    norm1_bias = noise(keys[4], (D,), 0.2, 1.0, (), jnp.float32)
    w_qkv = noise(keys[5], (D, 3 * D), D ** -0.5, 0.125, ((0, 8),))
    w_out = noise(keys[6], (D, D), (D // 64) ** -0.5, 1.0, ((0, 8),))
    norm2_gain = jnp.clip(1.0 + 0.1 * jax.random.normal(keys[7], (D,), jnp.float32), 0.5, 1.5)
    norm2_bias = noise(keys[8], (D,), 0.2, 1.0, (), jnp.float32)
    w_up = noise(keys[9], (D, FF), D ** -0.5, 0.125, ((0, 8),))
    w_down = noise(keys[10], (D, FF), FF ** -0.5, 0.0625, ((0, 8),))
    grad_out = draw_grad_out(jax.random.fold_in(keys[12], 71), 0)
    return dict(tokens=tokens, block_ids=block_ids, piece_order=piece_order, norm1_gain=norm1_gain, norm1_bias=norm1_bias, w_qkv=w_qkv, w_out=w_out, norm2_gain=norm2_gain, norm2_bias=norm2_bias, w_up=w_up, w_down=w_down, grad_out=grad_out)


norm_eps = 1e-05

@jax.custom_vjp
def low(v):
    return lax.optimization_barrier(v.astype(jnp.bfloat16)).astype(jnp.float32)

@jax.custom_vjp
def low_back(v):
    return v

def low_keep(v):
    return (low(v), None)

def low_pass(kept, grad):
    return (grad,)

def back_keep(v):
    return (v, None)

def back_low(kept, grad):
    return (low(grad),)
low.defvjp(low_keep, low_pass)
low_back.defvjp(back_keep, back_low)

def normalize(values, norm_gain, norm_bias):
    center = values - lax.optimization_barrier(jnp.mean(values, axis=-1, keepdims=True))
    variance = lax.optimization_barrier(jnp.mean(center * center, axis=-1, keepdims=True))
    return center * lax.rsqrt(variance + norm_eps) * norm_gain + norm_bias

def block_layer(inputs, gain_one, bias_one, w_qkv, w_out, gain_two, bias_two, w_up, w_down, seq_blocks):
    highest = lax.Precision.HIGHEST
    act_one = low(normalize(inputs, gain_one, bias_one))
    projected = low(low_back(jnp.dot(act_one, w_qkv, precision=highest)))
    queries = projected[:, :D].reshape(LENGTH, HEADS, HEAD)
    key_all = projected[:, D:2 * D].reshape(LENGTH, HEADS, HEAD)
    value_all = projected[:, 2 * D:].reshape(LENGTH, HEADS, HEAD)
    block_rows = math.gcd(LENGTH, 512)
    scale_factor = 1.0 / math.sqrt(HEAD)

    def one_block(block_index):
        first_row = block_index * block_rows
        query_rows = lax.dynamic_slice_in_dim(queries, first_row, block_rows, 0)
        query_blocks = lax.dynamic_slice_in_dim(seq_blocks, first_row, block_rows, 0)
        raw_scores = jnp.einsum('qhd,khd->hqk', query_rows, key_all, precision=highest)
        visible = seq_blocks[None, None, :] <= query_blocks[None, :, None]
        scores = jnp.where(visible, low_back(raw_scores) * scale_factor, -jnp.inf)
        attn_prob = low(jax.nn.softmax(scores, axis=-1))
        return jnp.einsum('hqk,khd->qhd', attn_prob, value_all, precision=highest)
    attended = lax.map(jax.checkpoint(one_block), jnp.arange(LENGTH // block_rows, dtype=jnp.int32))
    attended = low(low_back(attended.reshape(LENGTH, D)))
    residual = inputs + low_back(jnp.dot(attended, w_out, precision=highest))
    act_two = low(normalize(residual, gain_two, bias_two))
    pre_act = low_back(jnp.dot(act_two, w_up, precision=highest))
    hidden = low(jax.nn.gelu(pre_act, approximate=True))
    return residual + low_back(jnp.dot(hidden, w_down.T, precision=highest))

def reference(tokens, block_ids, piece_order, norm1_gain, norm1_bias, w_qkv, w_out, norm2_gain, norm2_bias, w_up, w_down, grad_out):
    row_index = jnp.arange(LENGTH, dtype=jnp.int32)
    stored_pos = (piece_order[row_index // PIECE] * PIECE + row_index % PIECE).astype(jnp.int32)
    all_blocks = jnp.take(block_ids, stored_pos, axis=1)
    params = (norm1_gain.astype(jnp.float32), norm1_bias.astype(jnp.float32), w_qkv.astype(jnp.float32), w_out.astype(jnp.float32), norm2_gain.astype(jnp.float32), norm2_bias.astype(jnp.float32), w_up.astype(jnp.float32), w_down.astype(jnp.float32))

    def one_sequence(totals, sequence):
        seq_tokens, seq_blocks, seq_grad = sequence

        def forward(inputs, *weights):
            return block_layer(inputs, *weights, seq_blocks)
        output, pullback = jax.vjp(forward, seq_tokens.astype(jnp.float32), *params)
        gradients = pullback(seq_grad.astype(jnp.float32))
        totals = tuple((summed + extra for summed, extra in zip(totals, gradients[1:])))
        return (totals, (output.astype(jnp.bfloat16), gradients[0].astype(jnp.bfloat16)))
    start_totals = tuple((jnp.zeros(weight_arr.shape, jnp.float32) for weight_arr in params))
    scanned = (tokens, all_blocks, grad_out)
    totals, outputs = lax.scan(one_sequence, start_totals, scanned)
    return (outputs[0], outputs[1], totals[2], totals[3], totals[6], totals[7], totals[0], totals[1], totals[4], totals[5])
```

```python
import functools
import math

import jax
import jax.numpy as jnp
import numpy as np
from jax import lax
from jax.experimental import pallas as pl
from jax.experimental.pallas import tpu as pltpu
from jax.sharding import Mesh, PartitionSpec as P

HEADS = 16
CORES = 2
LANES = 2
MESH = pl.DeviceIdType.MESH
VMEM_LIMIT = 56 << 20
norm_eps = 1e-05
F32 = jnp.float32
BF16 = jnp.bfloat16


def stored_blocks(seq_blocks, piece_order, piece_len):
    pieces = seq_blocks.reshape(seq_blocks.shape[0], -1, piece_len)
    return jnp.take(pieces, piece_order, axis=1).reshape(seq_blocks.shape)


def normalize(values, norm_gain, norm_bias):
    center = values - jnp.mean(values, axis=-1, keepdims=True)
    variance = jnp.mean(center * center, axis=-1, keepdims=True)
    inv_std = lax.rsqrt(variance + norm_eps)
    unit_vals = center * inv_std
    return (unit_vals * norm_gain + norm_bias, unit_vals, inv_std)


def normalize_back(grad_normed, unit_vals, inv_std, norm_gain):
    grad_unit = grad_normed * norm_gain
    mean_first = jnp.mean(grad_unit, axis=-1, keepdims=True)
    mean_second = jnp.mean(grad_unit * unit_vals, axis=-1, keepdims=True)
    return inv_std * (grad_unit - mean_first - unit_vals * mean_second)


def contract_last(left_arr, right_arr):
    return lax.dot_general(
        left_arr, right_arr, (((1,), (1,)), ((), ())), preferred_element_type=F32
    )


def contract_first(left_arr, right_arr):
    return lax.dot_general(
        left_arr, right_arr, (((0,), (0,)), ((), ())), preferred_element_type=F32
    )


def chip_bits(chips):
    return [1 << i for i in range(chips.bit_length() - 1)]


def lane_orders(chips):
    bits = chip_bits(chips)
    return [bits[lane:] + bits[:lane] for lane in range(LANES)]


def greet(chips, me_chip, me_core):
    barrier = pltpu.get_barrier_semaphore()
    bits = chip_bits(chips)
    for bit in bits:
        pl.semaphore_signal(barrier, inc=1, device_id={"ctx": me_chip ^ bit}, device_id_type=MESH)
    pl.semaphore_signal(barrier, inc=1, device_id={"core": 1 - me_core}, device_id_type=MESH)
    pl.semaphore_wait(barrier, len(bits) + 1)


def gather_kernel(chips, pieces, x_ref, o_ref, own_sem, send_sem, recv_sem):
    c, k = lax.axis_index("ctx"), lax.axis_index("core")
    rows = x_ref.shape[0]
    piece_rows = rows // (LANES * pieces)
    bits, orders = chip_bits(chips), lane_orders(chips)

    def place(core, chip, lane, piece):
        return pl.ds((core * chips + chip) * rows + (lane * pieces + piece) * piece_rows, piece_rows)

    local = pltpu.make_async_copy(x_ref, o_ref.at[pl.ds((k * chips + c) * rows, rows)], own_sem)
    local.start()
    greet(chips, c, k)
    started = []

    def send(source, m, lane, piece, step):
        if step < len(bits):
            bit = orders[lane][step]
            device, kind, landing = {"ctx": c ^ bit}, 0, m ^ bit
        else:
            device, kind, landing = {"core": 1 - k}, 1, m
        copy = pltpu.make_async_remote_copy(
            src_ref=source,
            dst_ref=o_ref.at[place(k, c ^ m, lane, piece)],
            send_sem=send_sem.at[step, m, lane, piece],
            recv_sem=recv_sem.at[kind, landing, lane, piece],
            device_id=device,
            device_id_type=MESH,
        )
        copy.start()
        started.append(copy)

    def arrived(kind, m, lane, piece):
        ref = o_ref.at[place(k if kind == 0 else 1 - k, c ^ m, lane, piece)]
        pltpu.make_async_remote_copy(
            src_ref=ref,
            dst_ref=ref,
            send_sem=send_sem.at[0, m, lane, piece],
            recv_sem=recv_sem.at[kind, m, lane, piece],
            device_id={"core": 1 - k},
            device_id_type=MESH,
        ).wait_recv()

    own = [(p, l) for p in range(pieces) for l in range(LANES)]
    for piece, lane in own:
        source = x_ref.at[pl.ds((lane * pieces + piece) * piece_rows, piece_rows)]
        for step in range(len(bits)):
            send(source, 0, lane, piece, step)
    for piece, lane in own:
        source = x_ref.at[pl.ds((lane * pieces + piece) * piece_rows, piece_rows)]
        send(source, 0, lane, piece, len(bits))
    items = sorted(
        (max(i for i, b in enumerate(orders[lane]) if m & b), piece, lane, m)
        for m in range(1, chips)
        for piece, lane in own
    )
    for step, piece, lane, m in items:
        arrived(0, m, lane, piece)
        source = o_ref.at[place(k, c ^ m, lane, piece)]
        for later in range(step + 1, len(bits) + 1):
            send(source, m, lane, piece, later)
    for m in range(chips):
        for piece, lane in own:
            arrived(1, m, lane, piece)
    for copy in started:
        copy.wait_send()
    local.wait()


def plane_gather(x, chips, ident, pieces=2):
    rows, cols = x.shape
    bits = len(chip_bits(chips))
    return pl.pallas_call(
        functools.partial(gather_kernel, chips, pieces),
        name="plane_gather",
        out_shape=jax.ShapeDtypeStruct((CORES * chips * rows, cols), x.dtype),
        in_specs=[pl.BlockSpec(memory_space=pl.ANY)],
        out_specs=pl.BlockSpec(memory_space=pl.ANY),
        scratch_shapes=[
            pltpu.SemaphoreType.DMA,
            pltpu.SemaphoreType.DMA((bits + 1, chips, LANES, pieces)),
            pltpu.SemaphoreType.DMA((2, chips, LANES, pieces)),
        ],
        cost_estimate=pl.CostEstimate(flops=40_000_000_000, bytes_accessed=0, transcendentals=0),
        compiler_params=pltpu.CompilerParams(collective_id=ident, has_side_effects=True),
    )(x)


def scatter_plan(chips):
    orders = lane_orders(chips)
    slots, sends = {}, {}
    for lane in range(LANES):
        count = 0
        for step, bit in enumerate(orders[lane]):
            gone = sum(orders[lane][: step + 1])
            for m in range(chips):
                if m & gone == 0:
                    slots[lane, step, m] = count
                    count += 1
        for m in range(1, chips):
            sends[m, lane] = min(i for i, b in enumerate(orders[lane]) if m & b)
    units = sorted(
        ((m, lane) for m in range(chips) for lane in range(LANES)),
        key=lambda u: (sends.get(u, len(orders[0])), -bin(u[0]).count("1"), u[1], u[0]),
    )
    return orders, slots, sends, units


def product_scatter_kernel(
    chips, transposed, tile, h_ref, w_ref, o_ref, h_v, w_v, own, theirs, from_core, from_chip,
    load_sem, core_send, core_recv, chip_send, chip_recv,
):
    c, k = lax.axis_index("ctx"), lax.axis_index("core")
    rows, cols = o_ref.shape
    half = rows // LANES
    orders, slots, sends, units = scatter_plan(chips)
    w_load = pltpu.make_async_copy(w_ref, w_v, load_sem.at[0])
    h_load = pltpu.make_async_copy(h_ref, h_v, load_sem.at[1])
    w_load.start()
    h_load.start()
    greet(chips, c, k)
    w_load.wait()
    h_load.wait()
    waits = []

    def lane_rows(lane):
        return pl.ds(lane * half, half)

    def compute(m, lane):
        def rows_for(core):
            start = (core * chips + (c ^ m)) * rows + lane * half
            return h_v[pl.ds(pl.multiple_of(start, half), half), :]

        left = jnp.concatenate([rows_for(k), rows_for(1 - k)], axis=0)

        def body(i, carry):
            span = pl.ds(pl.multiple_of(i * tile, tile), tile)
            if transposed:
                part = contract_last(left, w_v[span, :])
            else:
                part = jnp.dot(left, w_v[:, span], preferred_element_type=F32)
            own[m, lane_rows(lane), span] = part[:half].astype(BF16)
            theirs[m, lane_rows(lane), span] = part[half:].astype(BF16)
            return carry

        lax.fori_loop(0, cols // tile, body, 0)
        copy = pltpu.make_async_remote_copy(
            src_ref=theirs.at[m, lane_rows(lane)],
            dst_ref=from_core.at[m, lane_rows(lane)],
            send_sem=core_send.at[m, lane],
            recv_sem=core_recv.at[m, lane],
            device_id={"core": 1 - k},
            device_id_type=MESH,
        )
        copy.start()
        waits.append(copy)
        return copy

    def combine(m, lane, core_copy):
        core_copy.wait_recv()
        total = own[m, lane_rows(lane), :].astype(F32) + from_core[m, lane_rows(lane), :].astype(F32)
        last = sends.get((m, lane), len(orders[lane]))
        for step in range(last):
            slot = slots[lane, step, m]
            landed = from_chip.at[lane, slot]
            pltpu.make_async_remote_copy(
                src_ref=landed,
                dst_ref=landed,
                send_sem=chip_send.at[lane, slot],
                recv_sem=chip_recv.at[lane, slot],
                device_id={"core": 1 - k},
                device_id_type=MESH,
            ).wait_recv()
            total = total + from_chip[lane, slot].astype(F32)
        if m == 0:
            o_ref[lane_rows(lane), :] = total.astype(o_ref.dtype)
            return
        own[m, lane_rows(lane), :] = total.astype(BF16)
        bit = orders[lane][last]
        slot = slots[lane, last, m ^ bit]
        copy = pltpu.make_async_remote_copy(
            src_ref=own.at[m, lane_rows(lane)],
            dst_ref=from_chip.at[lane, slot],
            send_sem=chip_send.at[lane, slot],
            recv_sem=chip_recv.at[lane, slot],
            device_id={"ctx": c ^ bit},
            device_id_type=MESH,
        )
        copy.start()
        waits.append(copy)

    pending = []
    for m, lane in units:
        pending.append((m, lane, compute(m, lane)))
        if len(pending) > 1:
            combine(*pending.pop(0))
    while pending:
        combine(*pending.pop(0))
    for copy in waits:
        copy.wait_send()


def product_scatter(h, w, chips, ident, transposed):
    depth = h.shape[1]
    cols = w.shape[0] if transposed else w.shape[1]
    rows = h.shape[0] // (CORES * chips)
    half = rows // LANES
    return pl.pallas_call(
        functools.partial(product_scatter_kernel, chips, transposed, 512),
        name="product_scatter",
        out_shape=jax.ShapeDtypeStruct((rows, cols), F32),
        in_specs=[pl.BlockSpec(memory_space=pl.ANY)] * 2,
        out_specs=pl.BlockSpec(memory_space=pltpu.VMEM),
        scratch_shapes=[
            pltpu.VMEM(h.shape, BF16),
            pltpu.VMEM(w.shape, BF16),
            pltpu.VMEM((chips, rows, cols), BF16),
            pltpu.VMEM((chips, rows, cols), BF16),
            pltpu.VMEM((chips, rows, cols), BF16),
            pltpu.VMEM((LANES, chips - 1, half, cols), BF16),
            pltpu.SemaphoreType.DMA((2,)),
            pltpu.SemaphoreType.DMA((chips, LANES)),
            pltpu.SemaphoreType.DMA((chips, LANES)),
            pltpu.SemaphoreType.DMA((LANES, chips - 1)),
            pltpu.SemaphoreType.DMA((LANES, chips - 1)),
        ],
        cost_estimate=pl.CostEstimate(flops=45_000_000_000, bytes_accessed=0, transcendentals=0),
        compiler_params=pltpu.CompilerParams(
            collective_id=ident, has_side_effects=True, vmem_limit_bytes=VMEM_LIMIT
        ),
    )(h, w)


def attend_kernel(heads, size, step, p_ref, key_blk, query_blk, o_ref, log_ref):
    length = p_ref.shape[0]
    scale = 1.0 / math.sqrt(size)
    key_block = key_blk[0]
    for head in range(heads):
        keys = p_ref[:, (heads + head) * size : (heads + head + 1) * size]
        values = p_ref[:, (2 * heads + head) * size : (2 * heads + head + 1) * size]
        values_t = values.T
        for first in range(0, length, step):
            span = slice(first, first + step)
            queries = p_ref[span, head * size : (head + 1) * size]
            scores = contract_last(keys, queries) * scale
            scores = jnp.where(key_block <= query_blk[0, :, span], scores, -jnp.inf)
            top = jnp.max(scores, axis=0, keepdims=True)
            weights = jnp.exp(scores - top)
            total = jnp.sum(weights, axis=0, keepdims=True)
            prob = (weights * (1.0 / total)).astype(BF16)
            out_t = jnp.dot(values_t, prob, preferred_element_type=F32)
            o_ref[span, head * size : (head + 1) * size] = out_t.T.astype(BF16)
            log_ref[0, head : head + 1, span] = top + jnp.log(total)


def attend_back_kernel(heads, size, step, p_ref, g_ref, key_blk, query_blk, log_ref, d_ref, dk, dv):
    length = p_ref.shape[0]
    scale = 1.0 / math.sqrt(size)
    key_block = key_blk[0]
    for head in range(heads):
        keys = p_ref[:, (heads + head) * size : (heads + head + 1) * size]
        values = p_ref[:, (2 * heads + head) * size : (2 * heads + head + 1) * size]
        keys_t = keys.T
        for first in range(0, length, step):
            span = slice(first, first + step)
            queries = p_ref[span, head * size : (head + 1) * size]
            grads = g_ref[span, head * size : (head + 1) * size]
            scores = contract_last(keys, queries) * scale
            shifted = jnp.where(
                key_block <= query_blk[0, :, span], scores - log_ref[0, head : head + 1, span], -jnp.inf
            )
            prob = jnp.exp(shifted)
            grad_prob = contract_last(values, grads)
            row_dot = jnp.sum(prob * grad_prob, axis=0, keepdims=True)
            grad_raw = (prob * (grad_prob - row_dot) * scale).astype(BF16)
            dk_part = jnp.dot(grad_raw, queries, preferred_element_type=F32)
            dv_part = jnp.dot(prob.astype(BF16), grads, preferred_element_type=F32)
            if first == 0:
                dk[...] = dk_part
                dv[...] = dv_part
            else:
                dk[...] += dk_part
                dv[...] += dv_part
            dq_t = jnp.dot(keys_t, grad_raw, preferred_element_type=F32)
            d_ref[span, head * size : (head + 1) * size] = dq_t.T.astype(BF16)
        d_ref[:, (heads + head) * size : (heads + head + 1) * size] = dk[...].astype(BF16)
        d_ref[:, (2 * heads + head) * size : (2 * heads + head + 1) * size] = dv[...].astype(BF16)


def attention_specs(length, width, heads):
    wide = pl.BlockSpec((length, 3 * width), lambda s: (s, 0))
    narrow = pl.BlockSpec((length, width), lambda s: (s, 0))
    column = pl.BlockSpec((1, length, 1), lambda s: (s, 0, 0))
    row = pl.BlockSpec((1, 1, length), lambda s: (s, 0, 0))
    logs = pl.BlockSpec((1, heads, length), lambda s: (s, 0, 0))
    return wide, narrow, column, row, logs


def attend(proj, blocks, heads, size):
    length = blocks.shape[1]
    width = heads * size
    wide, narrow, column, row, logs = attention_specs(length, width, heads)
    return pl.pallas_call(
        functools.partial(attend_kernel, heads, size, 256),
        name="attend",
        grid=(blocks.shape[0],),
        out_shape=(
            jax.ShapeDtypeStruct((proj.shape[0], width), BF16),
            jax.ShapeDtypeStruct((blocks.shape[0], heads, length), F32),
        ),
        in_specs=[wide, column, row],
        out_specs=(narrow, logs),
        cost_estimate=pl.CostEstimate(flops=15_000_000_000, bytes_accessed=0, transcendentals=0),
        compiler_params=pltpu.CompilerParams(vmem_limit_bytes=VMEM_LIMIT),
    )(proj, blocks[:, :, None], blocks[:, None, :])


def attend_back(proj, grads, blocks, logsums, heads, size):
    length = blocks.shape[1]
    width = heads * size
    wide, narrow, column, row, logs = attention_specs(length, width, heads)
    return pl.pallas_call(
        functools.partial(attend_back_kernel, heads, size, 256),
        name="attend_back",
        grid=(blocks.shape[0],),
        out_shape=jax.ShapeDtypeStruct(proj.shape, BF16),
        in_specs=[wide, narrow, column, row, logs],
        out_specs=wide,
        scratch_shapes=[pltpu.VMEM((length, size), F32)] * 2,
        cost_estimate=pl.CostEstimate(flops=30_000_000_000, bytes_accessed=0, transcendentals=0),
        compiler_params=pltpu.CompilerParams(vmem_limit_bytes=VMEM_LIMIT),
    )(proj, grads, blocks[:, :, None], blocks[:, None, :], logsums)


def shards(
    tokens,
    block_ids,
    piece_order,
    norm1_gain,
    norm1_bias,
    w_qkv,
    w_out,
    norm2_gain,
    norm2_bias,
    w_up,
    w_down,
    grad_out,
):
    chips, depth = lax.axis_size("ctx"), lax.axis_size("z")
    c, k = lax.axis_index("ctx"), lax.axis_index("core")
    row_count, model_width = tokens.shape[1:]
    hidden_width = w_up.shape[1]
    size = model_width // HEADS
    team = CORES * chips
    heads = HEADS // team
    head_cols = heads * size
    ff_cols = hidden_width // team
    fsdp = ("z", "core")

    def chip_cols(w, width):
        return lax.dynamic_slice_in_dim(w, c * (CORES * width), CORES * width, 1)

    def own_slice(w, width):
        parts = w.reshape(w.shape[0], -1, CORES, width).transpose(2, 0, 1, 3)
        parts = parts.reshape(CORES, w.shape[0], -1)
        full = lax.all_gather(parts, fsdp, axis=0, tiled=False)
        mine = lax.dynamic_index_in_dim(full, k, 1, keepdims=False)
        return mine.reshape(model_width, -1)

    qkv_cols = jnp.concatenate(
        [chip_cols(part, head_cols) for part in jnp.split(w_qkv, 3, axis=1)], axis=1
    )
    my_qkv = own_slice(qkv_cols, head_cols)
    out_cols = model_width // chips
    out_gathered = lax.all_gather(
        lax.dynamic_slice_in_dim(w_out, c * out_cols, out_cols, 1), fsdp, axis=0, tiled=True
    )
    out_rows = lax.all_to_all(out_gathered, "ctx", split_axis=0, concat_axis=1, tiled=True)
    my_out = lax.dynamic_slice_in_dim(out_rows, k * head_cols, head_cols, 0)
    my_up = own_slice(chip_cols(w_up, ff_cols), ff_cols)
    my_down = own_slice(chip_cols(w_down, ff_cols), ff_cols)

    blocks = stored_blocks(block_ids, piece_order, row_count // 2)
    blocks = lax.all_gather(blocks, "core", axis=0, tiled=True)

    inputs = tokens.reshape(row_count, model_width).astype(F32)
    grad_y = grad_out.reshape(row_count, model_width)
    normed_one, unit_one, inv_one = normalize(inputs, norm1_gain, norm1_bias)
    acts_one = plane_gather(normed_one.astype(BF16), chips, 1)
    grads_y = plane_gather(grad_y, chips, 1)
    proj = jnp.dot(acts_one, my_qkv, preferred_element_type=F32).astype(BF16)
    attended, logsums = attend(proj, blocks, heads, size)
    residual = inputs + product_scatter(attended, my_out, chips, 2, False)
    normed_two, unit_two, inv_two = normalize(residual, norm2_gain, norm2_bias)
    acts_two = plane_gather(normed_two.astype(BF16), chips, 1)
    pre_act = jnp.dot(acts_two, my_up, preferred_element_type=F32)
    gelu_tanh = functools.partial(jax.nn.gelu, approximate=True)
    hidden_full, gelu_pull = jax.vjp(gelu_tanh, pre_act)
    hidden = hidden_full.astype(BF16)

    def spread_rows(grad):
        rounded = grad.astype(BF16).reshape(chips, -1, grad.shape[1])
        summed = lax.psum_scatter(rounded, "z", scatter_dimension=1, tiled=True)
        summed = summed.reshape(team, -1, grad.shape[1])
        return lax.all_to_all(summed, ("ctx", "core"), split_axis=0, concat_axis=0, tiled=True)

    def whole_columns(parts, width):
        count = parts.shape[1]
        return (
            parts.reshape(team, count, -1, width)
            .transpose(1, 2, 0, 3)
            .reshape(count, -1)
            .astype(F32)
        )

    grad_down = whole_columns(spread_rows(contract_first(grads_y, hidden)), ff_cols)
    grad_hidden = jnp.dot(grads_y, my_down, preferred_element_type=F32)
    grad_pre = gelu_pull(grad_hidden)[0].astype(BF16)
    grad_up = whole_columns(spread_rows(contract_first(acts_two, grad_pre)), ff_cols)
    grad_act_two = product_scatter(grad_pre, my_up, chips, 3, True)
    grad_res = grad_y.astype(F32) + normalize_back(grad_act_two, unit_two, inv_two, norm2_gain)
    grads_res = plane_gather(grad_res.astype(BF16), chips, 1)
    grad_attended = contract_last(grads_res, my_out).astype(BF16)
    grad_proj = attend_back(proj, grad_attended, blocks, logsums, heads, size)
    grad_qkv = whole_columns(spread_rows(contract_first(acts_one, grad_proj)), head_cols)
    out_part = lax.psum_scatter(
        contract_first(attended, grads_res).astype(BF16), "z", scatter_dimension=0, tiled=True
    )
    moves = [(z * CORES + core, core * depth + z) for z in range(depth) for core in range(CORES)]
    grad_wout = lax.ppermute(out_part, fsdp, moves).astype(F32)
    mixed = residual + product_scatter(hidden, my_down, chips, 3, True)
    grad_act_one = product_scatter(grad_proj, my_qkv, chips, 4, True)
    grad_inputs = grad_res + normalize_back(grad_act_one, unit_one, inv_one, norm1_gain)
    norm_sums = lax.psum(
        (
            jnp.sum(grad_act_one * unit_one, axis=0),
            jnp.sum(grad_act_one, axis=0),
            jnp.sum(grad_act_two * unit_two, axis=0),
            jnp.sum(grad_act_two, axis=0),
        ),
        ("ctx", "z", "core"),
    )
    out_shape = (1, row_count, model_width)
    return (
        mixed.reshape(out_shape).astype(BF16),
        grad_inputs.reshape(out_shape).astype(BF16),
        grad_qkv,
        grad_wout,
        grad_up,
        grad_down,
        *norm_sums,
    )


def solution(mesh):
    chips, across = mesh.shape["ctx"], mesh.shape["fsdp"]
    devices = np.asarray(mesh.devices).reshape(chips, across // CORES, CORES)
    cube = Mesh(devices, ("ctx", "z", "core"))
    fsdp = ("z", "core")
    rows = P(fsdp, "ctx", None)
    weight = P(fsdp, None)
    grad = P(("ctx", "z", "core"), None)
    return jax.shard_map(
        shards,
        mesh=cube,
        in_specs=(rows, weight, P(), P(), P(), weight, weight, P(), P(), weight, weight, rows),
        out_specs=(rows, rows, grad, grad, grad, grad, P(), P(), P(), P()),
        check_vma=False,
    )
```

```python
import functools
import math

import jax
import jax.numpy as jnp
import numpy as np
from jax import lax
from jax.experimental import pallas as pl
from jax.experimental.pallas import tpu as pltpu
from jax.sharding import Mesh, PartitionSpec as P

HEADS = 16
CORES = 2
LANES = 2
MESH = pl.DeviceIdType.MESH
VMEM_LIMIT = 56 << 20
norm_eps = 1e-05
F32 = jnp.float32
BF16 = jnp.bfloat16


def stored_blocks(seq_blocks, piece_order, piece_len):
    pieces = seq_blocks.reshape(seq_blocks.shape[0], -1, piece_len)
    return jnp.take(pieces, piece_order, axis=1).reshape(seq_blocks.shape)


def normalize(values, norm_gain, norm_bias):
    center = values - jnp.mean(values, axis=-1, keepdims=True)
    variance = jnp.mean(center * center, axis=-1, keepdims=True)
    inv_std = lax.rsqrt(variance + norm_eps)
    unit_vals = center * inv_std
    return (unit_vals * norm_gain + norm_bias, unit_vals, inv_std)


def normalize_back(grad_normed, unit_vals, inv_std, norm_gain):
    grad_unit = grad_normed * norm_gain
    mean_first = jnp.mean(grad_unit, axis=-1, keepdims=True)
    mean_second = jnp.mean(grad_unit * unit_vals, axis=-1, keepdims=True)
    return inv_std * (grad_unit - mean_first - unit_vals * mean_second)


def contract_last(left_arr, right_arr):
    return lax.dot_general(
        left_arr, right_arr, (((1,), (1,)), ((), ())), preferred_element_type=F32
    )


def contract_first(left_arr, right_arr):
    return lax.dot_general(
        left_arr, right_arr, (((0,), (0,)), ((), ())), preferred_element_type=F32
    )


def chip_bits(chips):
    return [1 << i for i in range(chips.bit_length() - 1)]


def lane_orders(chips):
    bits = chip_bits(chips)
    return [bits[lane:] + bits[:lane] for lane in range(LANES)]


def greet(chips, me_chip, me_core, others=()):
    barrier = pltpu.get_barrier_semaphore()
    friends = [{"ctx": me_chip ^ bit} for bit in chip_bits(chips)] + [{"core": 1 - me_core}]
    friends += others
    for friend in friends:
        pl.semaphore_signal(barrier, inc=1, device_id=friend, device_id_type=MESH)
    pl.semaphore_wait(barrier, len(friends))


def gather_kernel(chips, pieces, x_ref, o_ref, own_sem, send_sem, recv_sem):
    c, k = lax.axis_index("ctx"), lax.axis_index("core")
    rows = x_ref.shape[0]
    piece_rows = rows // (LANES * pieces)
    bits, orders = chip_bits(chips), lane_orders(chips)

    def place(core, chip, lane, piece):
        return pl.ds((core * chips + chip) * rows + (lane * pieces + piece) * piece_rows, piece_rows)

    local = pltpu.make_async_copy(x_ref, o_ref.at[pl.ds((k * chips + c) * rows, rows)], own_sem)
    local.start()
    greet(chips, c, k)
    started = []

    def send(source, m, lane, piece, step):
        if step < len(bits):
            bit = orders[lane][step]
            device, kind, landing = {"ctx": c ^ bit}, 0, m ^ bit
        else:
            device, kind, landing = {"core": 1 - k}, 1, m
        copy = pltpu.make_async_remote_copy(
            src_ref=source,
            dst_ref=o_ref.at[place(k, c ^ m, lane, piece)],
            send_sem=send_sem.at[step, m, lane, piece],
            recv_sem=recv_sem.at[kind, landing, lane, piece],
            device_id=device,
            device_id_type=MESH,
        )
        copy.start()
        started.append(copy)

    def arrived(kind, m, lane, piece):
        ref = o_ref.at[place(k if kind == 0 else 1 - k, c ^ m, lane, piece)]
        pltpu.make_async_remote_copy(
            src_ref=ref,
            dst_ref=ref,
            send_sem=send_sem.at[0, m, lane, piece],
            recv_sem=recv_sem.at[kind, m, lane, piece],
            device_id={"core": 1 - k},
            device_id_type=MESH,
        ).wait_recv()

    own = [(p, l) for p in range(pieces) for l in range(LANES)]
    for piece, lane in own:
        source = x_ref.at[pl.ds((lane * pieces + piece) * piece_rows, piece_rows)]
        for step in range(len(bits)):
            send(source, 0, lane, piece, step)
    for piece, lane in own:
        source = x_ref.at[pl.ds((lane * pieces + piece) * piece_rows, piece_rows)]
        send(source, 0, lane, piece, len(bits))
    items = sorted(
        (max(i for i, b in enumerate(orders[lane]) if m & b), piece, lane, m)
        for m in range(1, chips)
        for piece, lane in own
    )
    for step, piece, lane, m in items:
        arrived(0, m, lane, piece)
        source = o_ref.at[place(k, c ^ m, lane, piece)]
        for later in range(step + 1, len(bits) + 1):
            send(source, m, lane, piece, later)
    for m in range(chips):
        for piece, lane in own:
            arrived(1, m, lane, piece)
    for copy in started:
        copy.wait_send()
    local.wait()


def plane_gather(x, chips, ident, pieces=2):
    rows, cols = x.shape
    bits = len(chip_bits(chips))
    return pl.pallas_call(
        functools.partial(gather_kernel, chips, pieces),
        name="plane_gather",
        out_shape=jax.ShapeDtypeStruct((CORES * chips * rows, cols), x.dtype),
        in_specs=[pl.BlockSpec(memory_space=pl.ANY)],
        out_specs=pl.BlockSpec(memory_space=pl.ANY),
        scratch_shapes=[
            pltpu.SemaphoreType.DMA,
            pltpu.SemaphoreType.DMA((bits + 1, chips, LANES, pieces)),
            pltpu.SemaphoreType.DMA((2, chips, LANES, pieces)),
        ],
        cost_estimate=pl.CostEstimate(flops=1_000_000_000, bytes_accessed=0, transcendentals=0),
        compiler_params=pltpu.CompilerParams(collective_id=ident, has_side_effects=True),
    )(x)


def pick_kernel(head_cols, ff_cols, q_ref, o_ref, u_ref, d_ref, attn_ref, up_ref, down_ref, sem):
    c = lax.axis_index("ctx")
    width = o_ref.shape[1]
    copies = []

    def move(source, first, target, landing, count):
        first = pl.multiple_of(first, 128)
        copy = pltpu.make_async_copy(
            source.at[:, pl.ds(first, count)],
            target.at[:, pl.ds(landing, count)],
            sem.at[len(copies)],
        )
        copy.start()
        copies.append(copy)

    for core in range(CORES):
        first = (c * CORES + core) * head_cols
        for part in range(3):
            landing = (core * 4 + part) * head_cols
            move(q_ref, part * width + first, attn_ref, landing, head_cols)
        move(o_ref, first, attn_ref, (core * 4 + 3) * head_cols, head_cols)
    for source, target in ((u_ref, up_ref), (d_ref, down_ref)):
        move(source, c * (CORES * ff_cols), target, 0, CORES * ff_cols)
    for copy in copies:
        copy.wait()


def pick_columns(w_qkv, w_out, w_up, w_down, head_cols, ff_cols):
    rows = w_qkv.shape[0]
    in_place = pl.BlockSpec(memory_space=pl.ANY)
    in_vmem = pl.BlockSpec(memory_space=pltpu.VMEM)
    return pl.pallas_call(
        functools.partial(pick_kernel, head_cols, ff_cols),
        name="pick_columns",
        out_shape=[
            jax.ShapeDtypeStruct((rows, CORES * count), BF16)
            for count in (4 * head_cols, ff_cols, ff_cols)
        ],
        in_specs=[in_place] * 4,
        out_specs=[in_vmem] * 3,
        scratch_shapes=[pltpu.SemaphoreType.DMA((4 * CORES + 2,))],
    )(w_qkv, w_out, w_up, w_down)


def scatter_plan(chips):
    orders = lane_orders(chips)
    slots, sends = {}, {}
    for lane in range(LANES):
        count = 0
        for step, bit in enumerate(orders[lane]):
            gone = sum(orders[lane][: step + 1])
            for m in range(chips):
                if m & gone == 0:
                    slots[lane, step, m] = count
                    count += 1
        for m in range(1, chips):
            sends[m, lane] = min(i for i, b in enumerate(orders[lane]) if m & b)
    units = sorted(
        ((m, lane) for m in range(chips) for lane in range(LANES)),
        key=lambda u: (sends.get(u, len(orders[0])), -bin(u[0]).count("1"), u[1], u[0]),
    )
    return orders, slots, sends, units


def exchange_scratch(chips, rows, cols):
    half = rows // LANES
    return [
        pltpu.VMEM((chips, rows, cols), BF16),
        pltpu.VMEM((chips, rows, cols), BF16),
        pltpu.VMEM((chips, rows, cols), BF16),
        pltpu.VMEM((LANES, chips - 1, half, cols), BF16),
        pltpu.SemaphoreType.DMA((chips, LANES)),
        pltpu.SemaphoreType.DMA((chips, LANES)),
        pltpu.SemaphoreType.DMA((LANES, chips - 1)),
        pltpu.SemaphoreType.DMA((LANES, chips - 1)),
    ]


def exchange(chips, scratch, o_ref, compute, fillers=()):
    own, theirs, from_core, from_chip, core_send, core_recv, chip_send, chip_recv = scratch
    c, k = lax.axis_index("ctx"), lax.axis_index("core")
    half = o_ref.shape[0] // LANES
    orders, slots, sends, units = scatter_plan(chips)
    waits = []

    def share(m, lane):
        rows = pl.ds(lane * half, half)
        copy = pltpu.make_async_remote_copy(
            src_ref=theirs.at[m, rows],
            dst_ref=from_core.at[m, rows],
            send_sem=core_send.at[m, lane],
            recv_sem=core_recv.at[m, lane],
            device_id={"core": 1 - k},
            device_id_type=MESH,
        )
        copy.start()
        waits.append(copy)
        return copy

    def combine(m, lane, core_copy):
        rows = pl.ds(lane * half, half)
        core_copy.wait_recv()
        total = own[m, rows, :].astype(F32) + from_core[m, rows, :].astype(F32)
        last = sends.get((m, lane), len(orders[lane]))
        for step in range(last):
            slot = slots[lane, step, m]
            landed = from_chip.at[lane, slot]
            pltpu.make_async_remote_copy(
                src_ref=landed,
                dst_ref=landed,
                send_sem=chip_send.at[lane, slot],
                recv_sem=chip_recv.at[lane, slot],
                device_id={"core": 1 - k},
                device_id_type=MESH,
            ).wait_recv()
            total = total + from_chip[lane, slot].astype(F32)
        if m == 0:
            o_ref[rows, :] = total.astype(o_ref.dtype)
            return
        own[m, rows, :] = total.astype(BF16)
        bit = orders[lane][last]
        slot = slots[lane, last, m ^ bit]
        copy = pltpu.make_async_remote_copy(
            src_ref=own.at[m, rows],
            dst_ref=from_chip.at[lane, slot],
            send_sem=chip_send.at[lane, slot],
            recv_sem=chip_recv.at[lane, slot],
            device_id={"ctx": c ^ bit},
            device_id_type=MESH,
        )
        copy.start()
        waits.append(copy)

    fillers = list(fillers)
    pending = []
    for m, lane in units:
        compute(m, lane)
        pending.append((m, lane, share(m, lane)))
        if len(pending) > 1 and sends.get(pending[0][:2]) == 0:
            combine(*pending.pop(0))
    for level in range(1, len(orders[0]) + 1):
        count = -(-len(fillers) // (len(orders[0]) + 1 - level))
        for filler in fillers[:count]:
            filler()
        fillers = fillers[count:]
        while pending and sends.get(pending[0][:2], len(orders[0])) <= level:
            combine(*pending.pop(0))
    for copy in waits:
        copy.wait_send()


def unit_rows(chips, rows, m, lane):
    c, k = lax.axis_index("ctx"), lax.axis_index("core")
    half = rows // LANES
    starts = [(core * chips + (c ^ m)) * rows + lane * half for core in (k, 1 - k)]
    return [pl.ds(pl.multiple_of(start, half), half) for start in starts]


def product_terms(left, w_v, own, theirs, m, lane, transposed, tile):
    half, cols = left.shape[0] // CORES, own.shape[2]
    rows = pl.ds(lane * half, half)

    def body(i, carry):
        span = pl.ds(pl.multiple_of(i * tile, tile), tile)
        if transposed:
            part = contract_last(left, w_v[span, :])
        else:
            part = jnp.dot(left, w_v[:, span], preferred_element_type=F32)
        own[m, rows, span] = part[:half].astype(BF16)
        theirs[m, rows, span] = part[half:].astype(BF16)
        return carry

    lax.fori_loop(0, cols // tile, body, 0)


def core_window(ref, width):
    stride = ref.shape[1] // CORES
    first = pl.multiple_of(lax.axis_index("core") * stride, 128)
    return ref.at[:, pl.ds(first, width)]


def product_scatter_kernel(chips, transposed, tile, back, *refs):
    refs = list(refs)
    take = lambda count: [refs.pop(0) for _ in range(count)]
    h_ref, w_ref = take(2)
    back_in = take(5) if back else None
    o_ref = take(1)[0]
    back_out = take(1) if back else None
    h_v, w_v = take(2)
    scratch = take(8)
    w_sem, h_sem = take(2)
    back_scratch = take(2) if back else None
    c, k = lax.axis_index("ctx"), lax.axis_index("core")
    rows = o_ref.shape[0]
    _, _, _, units = scatter_plan(chips)
    own, theirs = scratch[:2]
    if transposed:
        w_load = pltpu.make_async_copy(core_window(w_ref, w_v.shape[1]), w_v, w_sem)
    else:
        w_load = pltpu.make_async_copy(w_ref, w_v, w_sem)
    w_load.start()
    loads = {}
    for m, lane in units:
        for side, span in enumerate(unit_rows(chips, rows, m, lane)):
            load = pltpu.make_async_copy(h_ref.at[span], h_v.at[span], h_sem.at[m, lane, side])
            load.start()
            loads[m, lane, side] = load
    greet(chips, c, k)
    fillers = []
    if back:
        fillers = attend_back_parts(*back, *back_in, *back_out, *back_scratch)
    w_load.wait()

    def compute(m, lane):
        spans = unit_rows(chips, rows, m, lane)
        for side in range(CORES):
            loads[m, lane, side].wait()
        left = jnp.concatenate([h_v[span, :] for span in spans], axis=0)
        product_terms(left, w_v, own, theirs, m, lane, transposed, tile)

    exchange(chips, scratch, o_ref, compute, fillers)


def product_scatter(h, w, chips, ident, transposed, back=None):
    depth = h.shape[1]
    cols = w.shape[0] if transposed else w.shape[1]
    rows = h.shape[0] // (CORES * chips)
    in_vmem = pl.BlockSpec(memory_space=pltpu.VMEM)
    in_place = pl.BlockSpec(memory_space=pl.ANY)
    operands, in_specs = [h, w], [in_place] * 2
    out_shape = [jax.ShapeDtypeStruct((rows, cols), F32)]
    back_scratch, sizes = [], None
    if back is not None:
        proj, grads, blocks, logsums, heads, size = back
        operands += [proj, grads, blocks[:, :, None], blocks[:, None, :], logsums]
        in_specs += [in_vmem] * 5
        out_shape.append(jax.ShapeDtypeStruct(proj.shape, BF16))
        back_scratch = [pltpu.VMEM((blocks.shape[1], size), F32)] * 2
        sizes = (heads, size, 256)
    result = pl.pallas_call(
        functools.partial(product_scatter_kernel, chips, transposed, 512, sizes),
        name="product_scatter",
        out_shape=out_shape,
        in_specs=in_specs,
        out_specs=[in_vmem] * len(out_shape),
        scratch_shapes=[
            pltpu.VMEM(h.shape, BF16),
            pltpu.VMEM((cols, depth) if transposed else w.shape, BF16),
            *exchange_scratch(chips, rows, cols),
            pltpu.SemaphoreType.DMA,
            pltpu.SemaphoreType.DMA((chips, LANES, CORES)),
            *back_scratch,
        ],
        cost_estimate=pl.CostEstimate(flops=1_000_000_000, bytes_accessed=0, transcendentals=0),
        compiler_params=pltpu.CompilerParams(
            collective_id=ident, has_side_effects=True, vmem_limit_bytes=VMEM_LIMIT
        ),
    )(*operands)
    return result if len(out_shape) > 1 else result[0]


def gelu_slope(u):
    scale, cubic = math.sqrt(2.0 / math.pi), 0.044715
    square = u * u
    bend = jnp.tanh(scale * u * (1.0 + cubic * square))
    return 0.5 * (1.0 + bend) + 0.5 * u * (1.0 - bend * bend) * scale * (1.0 + 3.0 * cubic * square)


def hidden_back_kernel(
    chips, tile, g_ref, d_ref, p_ref, u_ref, o_ref, e_ref, g_v, p_v, e_v, d_v, u_v, *refs
):
    scratch, (w_sem, load_sem, store_sem) = refs[:8], refs[8:]
    c, k = lax.axis_index("ctx"), lax.axis_index("core")
    rows = o_ref.shape[0]
    _, _, _, units = scatter_plan(chips)
    own, theirs = scratch[:2]
    d_load = pltpu.make_async_copy(core_window(d_ref, d_v.shape[1]), d_v, w_sem.at[0])
    u_load = pltpu.make_async_copy(core_window(u_ref, u_v.shape[1]), u_v, w_sem.at[1])
    d_load.start()
    loads, stores = {}, []
    for place, (m, lane) in enumerate(units):
        if place == 1:
            u_load.start()
        for side, span in enumerate(unit_rows(chips, rows, m, lane)):
            for which, (source, target) in enumerate(((g_ref, g_v), (p_ref, p_v))):
                load = pltpu.make_async_copy(
                    source.at[span], target.at[span], load_sem.at[which, m, lane, side]
                )
                load.start()
                loads.setdefault((m, lane), []).append(load)
    greet(chips, c, k)
    d_load.wait()

    def compute(m, lane):
        spans = unit_rows(chips, rows, m, lane)
        half = rows // LANES
        for load in loads[m, lane]:
            load.wait()
        grads = jnp.concatenate([g_v[span, :] for span in spans], axis=0)

        def body(i, carry):
            cols = pl.ds(pl.multiple_of(i * tile, tile), tile)
            part = jnp.dot(grads, d_v[:, cols], preferred_element_type=F32)
            for side, span in enumerate(spans):
                slope = gelu_slope(p_v[span, cols])
                e_v[span, cols] = (part[side * half : (side + 1) * half] * slope).astype(BF16)
            return carry

        lax.fori_loop(0, e_v.shape[1] // tile, body, 0)
        for side, span in enumerate(spans):
            store = pltpu.make_async_copy(e_v.at[span], e_ref.at[span], store_sem.at[m, lane, side])
            store.start()
            stores.append(store)
        if (m, lane) == units[0]:
            u_load.wait()
        left = jnp.concatenate([e_v[span, :] for span in spans], axis=0)
        product_terms(left, u_v, own, theirs, m, lane, True, 512)

    exchange(chips, scratch, o_ref, compute)
    for store in stores:
        store.wait()


def hidden_back(grads, w_down, pre, w_up, chips, ident):
    cols, width = w_up.shape[0], pre.shape[1]
    rows = grads.shape[0] // (CORES * chips)
    in_place = pl.BlockSpec(memory_space=pl.ANY)
    return pl.pallas_call(
        functools.partial(hidden_back_kernel, chips, 256),
        name="hidden_back",
        out_shape=[
            jax.ShapeDtypeStruct((rows, cols), F32),
            jax.ShapeDtypeStruct((grads.shape[0], width), BF16),
        ],
        in_specs=[in_place] * 4,
        out_specs=[pl.BlockSpec(memory_space=pltpu.VMEM), in_place],
        scratch_shapes=[
            pltpu.VMEM(grads.shape, BF16),
            pltpu.VMEM(pre.shape, pre.dtype),
            pltpu.VMEM(pre.shape, BF16),
            pltpu.VMEM((w_down.shape[0], width), BF16),
            pltpu.VMEM((cols, width), BF16),
            *exchange_scratch(chips, rows, cols),
            pltpu.SemaphoreType.DMA((2,)),
            pltpu.SemaphoreType.DMA((2, chips, LANES, CORES)),
            pltpu.SemaphoreType.DMA((chips, LANES, CORES)),
        ],
        cost_estimate=pl.CostEstimate(flops=1_000_000_000, bytes_accessed=0, transcendentals=0),
        compiler_params=pltpu.CompilerParams(
            collective_id=ident, has_side_effects=True, vmem_limit_bytes=VMEM_LIMIT
        ),
    )(grads, w_down, pre, w_up)


def all_sum_kernel(chips, planes, x_ref, o_ref, landed, send_sem, recv_sem):
    c, z, k = lax.axis_index("ctx"), lax.axis_index("z"), lax.axis_index("core")
    partners = [{"ctx": c ^ bit} for bit in chip_bits(chips)] + [{"core": 1 - k}]
    partners += [{"z": z ^ (2 * bit - 1)} for bit in chip_bits(planes)]
    barrier = pltpu.get_barrier_semaphore()
    for partner in partners:
        pl.semaphore_signal(barrier, inc=1, device_id=partner, device_id_type=MESH)
    o_ref[...] = x_ref[...]
    pl.semaphore_wait(barrier, len(partners))
    for step, partner in enumerate(partners):
        copy = pltpu.make_async_remote_copy(
            src_ref=o_ref,
            dst_ref=landed.at[step],
            send_sem=send_sem.at[step],
            recv_sem=recv_sem.at[step],
            device_id=partner,
            device_id_type=MESH,
        )
        copy.start()
        copy.wait()
        o_ref[...] += landed[step]


def all_sum(x, chips, planes, ident):
    in_vmem = pl.BlockSpec(memory_space=pltpu.VMEM)
    steps = len(chip_bits(chips)) + 1 + len(chip_bits(planes))
    return pl.pallas_call(
        functools.partial(all_sum_kernel, chips, planes),
        name="all_sum",
        out_shape=jax.ShapeDtypeStruct(x.shape, x.dtype),
        in_specs=[in_vmem],
        out_specs=in_vmem,
        scratch_shapes=[
            pltpu.VMEM((steps, *x.shape), x.dtype),
            pltpu.SemaphoreType.DMA((steps,)),
            pltpu.SemaphoreType.DMA((steps,)),
        ],
        compiler_params=pltpu.CompilerParams(collective_id=ident, has_side_effects=True),
    )(x)


def attend_kernel(heads, size, step, p_ref, key_blk, query_blk, o_ref, log_ref):
    length = p_ref.shape[0]
    scale = 1.0 / math.sqrt(size)
    key_block = key_blk[0]
    for head in range(heads):
        keys = p_ref[:, (heads + head) * size : (heads + head + 1) * size]
        values = p_ref[:, (2 * heads + head) * size : (2 * heads + head + 1) * size]
        values_t = values.T
        for first in range(0, length, step):
            span = slice(first, first + step)
            queries = p_ref[span, head * size : (head + 1) * size]
            scores = contract_last(keys, queries) * scale
            scores = jnp.where(key_block <= query_blk[0, :, span], scores, -jnp.inf)
            top = jnp.max(scores, axis=0, keepdims=True)
            weights = jnp.exp(scores - top)
            total = jnp.sum(weights, axis=0, keepdims=True)
            prob = (weights * (1.0 / total)).astype(BF16)
            out_t = jnp.dot(values_t, prob, preferred_element_type=F32)
            o_ref[span, head * size : (head + 1) * size] = out_t.T.astype(BF16)
            log_ref[0, head : head + 1, span] = top + jnp.log(total)


def attend_back_parts(
    heads, size, step, p_ref, g_ref, key_blk, query_blk, log_ref, d_ref, dk, dv
):
    length = key_blk.shape[1]
    scale = 1.0 / math.sqrt(size)

    def part(seq, head):
        whole = pl.ds(seq * length, length)
        at_query, at_key, at_value = [
            slice((j * heads + head) * size, (j * heads + head + 1) * size) for j in range(3)
        ]
        keys, values = p_ref[whole, at_key], p_ref[whole, at_value]
        keys_t = keys.T
        key_block = key_blk[seq]
        for first in range(0, length, step):
            here = slice(first, first + step)
            span = pl.ds(seq * length + first, step)
            queries, grads = p_ref[span, at_query], g_ref[span, at_query]
            scores = contract_last(keys, queries) * scale
            shifted = jnp.where(
                key_block <= query_blk[seq, :, here],
                scores - log_ref[seq, head : head + 1, here],
                -jnp.inf,
            )
            prob = jnp.exp(shifted)
            grad_prob = contract_last(values, grads)
            row_dot = jnp.sum(prob * grad_prob, axis=0, keepdims=True)
            grad_raw = (prob * (grad_prob - row_dot) * scale).astype(BF16)
            dk_part = jnp.dot(grad_raw, queries, preferred_element_type=F32)
            dv_part = jnp.dot(prob.astype(BF16), grads, preferred_element_type=F32)
            if first == 0:
                dk[...] = dk_part
                dv[...] = dv_part
            else:
                dk[...] += dk_part
                dv[...] += dv_part
            dq_t = jnp.dot(keys_t, grad_raw, preferred_element_type=F32)
            d_ref[span, at_query] = dq_t.T.astype(BF16)
        d_ref[whole, at_key] = dk[...].astype(BF16)
        d_ref[whole, at_value] = dv[...].astype(BF16)

    return [
        functools.partial(part, seq, head)
        for seq in range(key_blk.shape[0])
        for head in range(heads)
    ]


def attention_specs(length, width, heads):
    wide = pl.BlockSpec((length, 3 * width), lambda s: (s, 0))
    narrow = pl.BlockSpec((length, width), lambda s: (s, 0))
    column = pl.BlockSpec((1, length, 1), lambda s: (s, 0, 0))
    row = pl.BlockSpec((1, 1, length), lambda s: (s, 0, 0))
    logs = pl.BlockSpec((1, heads, length), lambda s: (s, 0, 0))
    return wide, narrow, column, row, logs


def attend(proj, blocks, heads, size):
    length = blocks.shape[1]
    width = heads * size
    wide, narrow, column, row, logs = attention_specs(length, width, heads)
    return pl.pallas_call(
        functools.partial(attend_kernel, heads, size, 256),
        name="attend",
        grid=(blocks.shape[0],),
        out_shape=(
            jax.ShapeDtypeStruct((proj.shape[0], width), BF16),
            jax.ShapeDtypeStruct((blocks.shape[0], heads, length), F32),
        ),
        in_specs=[wide, column, row],
        out_specs=(narrow, logs),
        cost_estimate=pl.CostEstimate(flops=1_000_000_000, bytes_accessed=0, transcendentals=0),
        compiler_params=pltpu.CompilerParams(vmem_limit_bytes=VMEM_LIMIT),
    )(proj, blocks[:, :, None], blocks[:, None, :])


def shards(
    tokens,
    block_ids,
    piece_order,
    norm1_gain,
    norm1_bias,
    w_qkv,
    w_out,
    norm2_gain,
    norm2_bias,
    w_up,
    w_down,
    grad_out,
):
    chips, depth = lax.axis_size("ctx"), lax.axis_size("z")
    c, k = lax.axis_index("ctx"), lax.axis_index("core")
    row_count, model_width = tokens.shape[1:]
    hidden_width = w_up.shape[1]
    size = model_width // HEADS
    team = CORES * chips
    heads = HEADS // team
    head_cols = heads * size
    ff_cols = hidden_width // team
    fsdp = ("z", "core")

    def core_cols(gathered, width, first=0):
        return lax.dynamic_slice_in_dim(gathered, first + k * width, width, 1)

    def across_z(w):
        return lax.all_gather(w, fsdp, axis=0, tiled=True)

    attn_cols, up_cols, down_cols = pick_columns(w_qkv, w_out, w_up, w_down, head_cols, ff_cols)
    attn_weights = across_z(attn_cols)
    inputs = tokens.reshape(row_count, model_width).astype(F32)
    grad_y = grad_out.reshape(row_count, model_width)
    normed_one, unit_one, inv_one = normalize(inputs, norm1_gain, norm1_bias)
    acts_one = plane_gather(normed_one.astype(BF16), chips, 1)
    acts_one, block_ids, grad_y = lax.optimization_barrier((acts_one, block_ids, grad_y))
    up_weights = across_z(up_cols)
    down_weights = across_z(down_cols)
    blocks = stored_blocks(block_ids, piece_order, row_count // 2)
    blocks = lax.all_gather(blocks, "core", axis=0, tiled=True)

    grads_y = plane_gather(grad_y, chips, 1)
    my_attn = core_cols(attn_weights, 4 * head_cols)
    out_blocks = my_attn[:, 3 * head_cols :]
    my_out = lax.all_to_all(out_blocks, ("ctx", "core"), split_axis=0, concat_axis=1, tiled=True)
    proj = jnp.dot(acts_one, my_attn[:, : 3 * head_cols], preferred_element_type=F32).astype(BF16)
    attended, logsums = attend(proj, blocks, heads, size)
    residual = inputs + product_scatter(attended, my_out, chips, 2, False)
    normed_two, unit_two, inv_two = normalize(residual, norm2_gain, norm2_bias)
    acts_two = plane_gather(normed_two.astype(BF16), chips, 1)
    up_weights, acts_two = lax.optimization_barrier((up_weights, acts_two))
    my_up = core_cols(up_weights, ff_cols)
    pre_act = jnp.dot(acts_two, my_up, preferred_element_type=F32)
    hidden = jax.nn.gelu(pre_act, approximate=True).astype(BF16)

    def sum_planes(grad):
        parts = grad.reshape(chips, -1, grad.shape[1])
        return lax.psum_scatter(parts, "z", scatter_dimension=1, tiled=True)

    def spread_rows(summed):
        summed = summed.reshape(team, -1, summed.shape[2])
        return lax.all_to_all(summed, ("ctx", "core"), split_axis=0, concat_axis=0, tiled=True)

    def whole_columns(parts, width):
        count = parts.shape[1]
        return (
            parts.reshape(team, count, -1, width)
            .transpose(1, 2, 0, 3)
            .reshape(count, -1)
            .astype(F32)
        )

    down_part = contract_first(grads_y, hidden).astype(BF16)
    down_weights, down_part = lax.optimization_barrier((down_weights, down_part))
    down_sum = sum_planes(down_part)
    grad_act_two, grad_pre = hidden_back(grads_y, down_weights, pre_act, up_weights, chips, 3)
    up_part = contract_first(acts_two, grad_pre).astype(BF16)
    grad_act_two, up_part = lax.optimization_barrier((grad_act_two, up_part))
    up_sum = sum_planes(up_part)
    grad_res = grad_y.astype(F32) + normalize_back(grad_act_two, unit_two, inv_two, norm2_gain)
    grads_res = plane_gather(grad_res.astype(BF16), chips, 1)
    grad_attended = contract_last(grads_res, my_out).astype(BF16)
    out_part = contract_first(attended, grads_res).astype(BF16)
    grad_attended, out_part, down_sum = lax.optimization_barrier(
        (grad_attended, out_part, down_sum)
    )
    grad_down = whole_columns(spread_rows(down_sum), ff_cols)
    out_sum = lax.psum_scatter(out_part, "z", scatter_dimension=0, tiled=True)
    mixed_sum, grad_proj = product_scatter(
        hidden, down_weights, chips, 5, True, back=(proj, grad_attended, blocks, logsums, heads, size)
    )
    proj_part = contract_first(acts_one, grad_proj).astype(BF16)
    grad_proj, proj_part, up_sum, out_sum = lax.optimization_barrier(
        (grad_proj, proj_part, up_sum, out_sum)
    )
    proj_sum = sum_planes(proj_part)
    grad_act_one = product_scatter(grad_proj, attn_weights, chips, 4, True)
    mixed = residual + mixed_sum
    norm_parts = jnp.stack(
        [
            jnp.sum(grad_act_one * unit_one, axis=0),
            jnp.sum(grad_act_one, axis=0),
            jnp.sum(grad_act_two * unit_two, axis=0),
            jnp.sum(grad_act_two, axis=0),
        ]
        + [jnp.zeros((model_width,), F32)] * 4
    )
    norm_sums = all_sum(norm_parts, chips, depth, 6)
    grad_up = whole_columns(spread_rows(up_sum), ff_cols)
    moves = [(z * CORES + core, core * depth + z) for z in range(depth) for core in range(CORES)]
    grad_wout = lax.ppermute(out_sum, fsdp, moves).astype(F32)
    grad_qkv = whole_columns(spread_rows(proj_sum), head_cols)
    grad_inputs = grad_res + normalize_back(grad_act_one, unit_one, inv_one, norm1_gain)
    out_shape = (1, row_count, model_width)
    return (
        mixed.reshape(out_shape).astype(BF16),
        grad_inputs.reshape(out_shape).astype(BF16),
        grad_qkv,
        grad_wout,
        grad_up,
        grad_down,
        *norm_sums[:4],
    )


def solution(mesh):
    chips, across = mesh.shape["ctx"], mesh.shape["fsdp"]
    devices = np.asarray(mesh.devices).reshape(chips, across // CORES, CORES)
    cube = Mesh(devices, ("ctx", "z", "core"))
    fsdp = ("z", "core")
    rows = P(fsdp, "ctx", None)
    weight = P(fsdp, None)
    grad = P(("ctx", "z", "core"), None)
    return jax.shard_map(
        shards,
        mesh=cube,
        in_specs=(rows, weight, P(), P(), P(), weight, weight, P(), P(), weight, weight, rows),
        out_specs=(rows, rows, grad, grad, grad, grad, P(), P(), P(), P()),
        check_vma=False,
    )
```

```python
import functools
import math

import jax
import jax.numpy as jnp
import numpy as np
from jax import lax
from jax.experimental import pallas as pl
from jax.experimental.pallas import tpu as pltpu
from jax.sharding import Mesh, PartitionSpec as P

HEADS = 16
CORES = 2
LANES = 2
MESH = pl.DeviceIdType.MESH
VMEM_LIMIT = 56 << 20
norm_eps = 1e-05
F32 = jnp.float32
BF16 = jnp.bfloat16


def stored_blocks(seq_blocks, piece_order, piece_len):
    pieces = seq_blocks.reshape(seq_blocks.shape[0], -1, piece_len)
    return jnp.take(pieces, piece_order, axis=1).reshape(seq_blocks.shape)


def normalize(values, norm_gain, norm_bias):
    center = values - jnp.mean(values, axis=-1, keepdims=True)
    variance = jnp.mean(center * center, axis=-1, keepdims=True)
    inv_std = lax.rsqrt(variance + norm_eps)
    unit_vals = center * inv_std
    return (unit_vals * norm_gain + norm_bias, unit_vals, inv_std)


def normalize_back(grad_normed, unit_vals, inv_std, norm_gain):
    grad_unit = grad_normed * norm_gain
    mean_first = jnp.mean(grad_unit, axis=-1, keepdims=True)
    mean_second = jnp.mean(grad_unit * unit_vals, axis=-1, keepdims=True)
    return inv_std * (grad_unit - mean_first - unit_vals * mean_second)


def contract_last(left_arr, right_arr):
    return lax.dot_general(
        left_arr, right_arr, (((1,), (1,)), ((), ())), preferred_element_type=F32
    )


def contract_first(left_arr, right_arr):
    return lax.dot_general(
        left_arr, right_arr, (((0,), (0,)), ((), ())), preferred_element_type=F32
    )


def chip_bits(chips):
    return [1 << i for i in range(chips.bit_length() - 1)]


def lane_orders(chips):
    bits = chip_bits(chips)
    return [bits[lane:] + bits[:lane] for lane in range(LANES)]


def greet(chips, me_chip, me_core, others=()):
    barrier = pltpu.get_barrier_semaphore()
    friends = [{"ctx": me_chip ^ bit} for bit in chip_bits(chips)] + [{"core": 1 - me_core}]
    friends += others
    for friend in friends:
        pl.semaphore_signal(barrier, inc=1, device_id=friend, device_id_type=MESH)
    pl.semaphore_wait(barrier, len(friends))


def gather_kernel(chips, pieces, x_ref, o_ref, own_sem, send_sem, recv_sem):
    c, k = lax.axis_index("ctx"), lax.axis_index("core")
    rows = x_ref.shape[0]
    piece_rows = rows // (LANES * pieces)
    bits, orders = chip_bits(chips), lane_orders(chips)

    def place(core, chip, lane, piece):
        return pl.ds((core * chips + chip) * rows + (lane * pieces + piece) * piece_rows, piece_rows)

    local = pltpu.make_async_copy(x_ref, o_ref.at[pl.ds((k * chips + c) * rows, rows)], own_sem)
    local.start()
    greet(chips, c, k)
    started = []

    def send(source, m, lane, piece, step):
        if step < len(bits):
            bit = orders[lane][step]
            device, kind, landing = {"ctx": c ^ bit}, 0, m ^ bit
        else:
            device, kind, landing = {"core": 1 - k}, 1, m
        copy = pltpu.make_async_remote_copy(
            src_ref=source,
            dst_ref=o_ref.at[place(k, c ^ m, lane, piece)],
            send_sem=send_sem.at[step, m, lane, piece],
            recv_sem=recv_sem.at[kind, landing, lane, piece],
            device_id=device,
            device_id_type=MESH,
        )
        copy.start()
        started.append(copy)

    def arrived(kind, m, lane, piece):
        ref = o_ref.at[place(k if kind == 0 else 1 - k, c ^ m, lane, piece)]
        pltpu.make_async_remote_copy(
            src_ref=ref,
            dst_ref=ref,
            send_sem=send_sem.at[0, m, lane, piece],
            recv_sem=recv_sem.at[kind, m, lane, piece],
            device_id={"core": 1 - k},
            device_id_type=MESH,
        ).wait_recv()

    own = [(p, l) for p in range(pieces) for l in range(LANES)]
    for piece, lane in own:
        source = x_ref.at[pl.ds((lane * pieces + piece) * piece_rows, piece_rows)]
        for step in range(len(bits)):
            send(source, 0, lane, piece, step)
    for piece, lane in own:
        source = x_ref.at[pl.ds((lane * pieces + piece) * piece_rows, piece_rows)]
        send(source, 0, lane, piece, len(bits))
    items = sorted(
        (max(i for i, b in enumerate(orders[lane]) if m & b), piece, lane, m)
        for m in range(1, chips)
        for piece, lane in own
    )
    for step, piece, lane, m in items:
        arrived(0, m, lane, piece)
        source = o_ref.at[place(k, c ^ m, lane, piece)]
        for later in range(step + 1, len(bits) + 1):
            send(source, m, lane, piece, later)
    for m in range(chips):
        for piece, lane in own:
            arrived(1, m, lane, piece)
    for copy in started:
        copy.wait_send()
    local.wait()


def plane_gather(x, chips, ident, pieces=2):
    rows, cols = x.shape
    bits = len(chip_bits(chips))
    return pl.pallas_call(
        functools.partial(gather_kernel, chips, pieces),
        name="plane_gather",
        out_shape=jax.ShapeDtypeStruct((CORES * chips * rows, cols), x.dtype),
        in_specs=[pl.BlockSpec(memory_space=pl.ANY)],
        out_specs=pl.BlockSpec(memory_space=pl.ANY),
        scratch_shapes=[
            pltpu.SemaphoreType.DMA,
            pltpu.SemaphoreType.DMA((bits + 1, chips, LANES, pieces)),
            pltpu.SemaphoreType.DMA((2, chips, LANES, pieces)),
        ],
        cost_estimate=pl.CostEstimate(flops=1_000_000_000, bytes_accessed=0, transcendentals=0),
        compiler_params=pltpu.CompilerParams(collective_id=ident, has_side_effects=True),
    )(x)


def pick_kernel(head_cols, ff_cols, q_ref, o_ref, u_ref, d_ref, attn_ref, up_ref, down_ref, sem):
    c = lax.axis_index("ctx")
    width = o_ref.shape[1]
    copies = []

    def move(source, first, target, landing, count):
        first = pl.multiple_of(first, 128)
        copy = pltpu.make_async_copy(
            source.at[:, pl.ds(first, count)],
            target.at[:, pl.ds(landing, count)],
            sem.at[len(copies)],
        )
        copy.start()
        copies.append(copy)

    for core in range(CORES):
        first = (c * CORES + core) * head_cols
        for part in range(3):
            landing = (core * 4 + part) * head_cols
            move(q_ref, part * width + first, attn_ref, landing, head_cols)
        move(o_ref, first, attn_ref, (core * 4 + 3) * head_cols, head_cols)
    for source, target in ((u_ref, up_ref), (d_ref, down_ref)):
        move(source, c * (CORES * ff_cols), target, 0, CORES * ff_cols)
    for copy in copies:
        copy.wait()


def pick_columns(w_qkv, w_out, w_up, w_down, head_cols, ff_cols):
    rows = w_qkv.shape[0]
    in_place = pl.BlockSpec(memory_space=pl.ANY)
    in_vmem = pl.BlockSpec(memory_space=pltpu.VMEM)
    return pl.pallas_call(
        functools.partial(pick_kernel, head_cols, ff_cols),
        name="pick_columns",
        out_shape=[
            jax.ShapeDtypeStruct((rows, CORES * count), BF16)
            for count in (4 * head_cols, ff_cols, ff_cols)
        ],
        in_specs=[in_place] * 4,
        out_specs=[in_vmem] * 3,
        scratch_shapes=[pltpu.SemaphoreType.DMA((4 * CORES + 2,))],
    )(w_qkv, w_out, w_up, w_down)


def scatter_plan(chips):
    orders = lane_orders(chips)
    slots, sends = {}, {}
    for lane in range(LANES):
        count = 0
        for step, bit in enumerate(orders[lane]):
            gone = sum(orders[lane][: step + 1])
            for m in range(chips):
                if m & gone == 0:
                    slots[lane, step, m] = count
                    count += 1
        for m in range(1, chips):
            sends[m, lane] = min(i for i, b in enumerate(orders[lane]) if m & b)
    return orders, slots, sends


def block_order(chips):
    return sorted(range(chips), key=lambda m: (-bin(m).count("1"), m))


def exchange_scratch(chips, rows, cols):
    half = rows // LANES
    return [
        pltpu.VMEM((chips, rows, cols), BF16),
        pltpu.VMEM((chips, rows, cols), BF16),
        pltpu.VMEM((chips, rows, cols), BF16),
        pltpu.VMEM((LANES, chips - 1, half, cols), BF16),
        pltpu.SemaphoreType.DMA((chips, LANES)),
        pltpu.SemaphoreType.DMA((chips, LANES)),
        pltpu.SemaphoreType.DMA((LANES, chips - 1)),
        pltpu.SemaphoreType.DMA((LANES, chips - 1)),
    ]


def exchange(chips, scratch, o_ref, compute, fillers=()):
    own, theirs, from_core, from_chip, core_send, core_recv, chip_send, chip_recv = scratch
    c, k = lax.axis_index("ctx"), lax.axis_index("core")
    half = o_ref.shape[0] // LANES
    orders, slots, sends = scatter_plan(chips)
    waits = []

    def share(m, lane):
        rows = pl.ds(lane * half, half)
        copy = pltpu.make_async_remote_copy(
            src_ref=theirs.at[m, rows],
            dst_ref=from_core.at[m, rows],
            send_sem=core_send.at[m, lane],
            recv_sem=core_recv.at[m, lane],
            device_id={"core": 1 - k},
            device_id_type=MESH,
        )
        copy.start()
        waits.append(copy)
        return copy

    def combine(m, lane, core_copy):
        rows = pl.ds(lane * half, half)
        core_copy.wait_recv()
        total = own[m, rows, :].astype(F32) + from_core[m, rows, :].astype(F32)
        last = sends.get((m, lane), len(orders[lane]))
        for step in range(last):
            slot = slots[lane, step, m]
            landed = from_chip.at[lane, slot]
            pltpu.make_async_remote_copy(
                src_ref=landed,
                dst_ref=landed,
                send_sem=chip_send.at[lane, slot],
                recv_sem=chip_recv.at[lane, slot],
                device_id={"core": 1 - k},
                device_id_type=MESH,
            ).wait_recv()
            total = total + from_chip[lane, slot].astype(F32)
        if m == 0:
            o_ref[rows, :] = total.astype(o_ref.dtype)
            return
        own[m, rows, :] = total.astype(BF16)
        bit = orders[lane][last]
        slot = slots[lane, last, m ^ bit]
        copy = pltpu.make_async_remote_copy(
            src_ref=own.at[m, rows],
            dst_ref=from_chip.at[lane, slot],
            send_sem=chip_send.at[lane, slot],
            recv_sem=chip_recv.at[lane, slot],
            device_id={"ctx": c ^ bit},
            device_id_type=MESH,
        )
        copy.start()
        waits.append(copy)

    fillers, pending, last = list(fillers), [], len(orders[0])

    def settle(level):
        for unit in [u for u in pending if sends.get(u[:2], last) <= level]:
            pending.remove(unit)
            combine(*unit)

    for m in block_order(chips):
        compute(m)
        fresh = [(m, lane, share(m, lane)) for lane in range(LANES)]
        settle(0)
        pending += fresh
    settle(0)
    for level in range(1, last + 1):
        count = -(-len(fillers) // (last + 1 - level))
        for filler in fillers[:count]:
            filler()
        fillers = fillers[count:]
        settle(level)
    for copy in waits:
        copy.wait_send()


def block_rows(chips, rows, m):
    c, k = lax.axis_index("ctx"), lax.axis_index("core")
    starts = [(core * chips + (c ^ m)) * rows for core in (k, 1 - k)]
    return [pl.ds(pl.multiple_of(start, rows), rows) for start in starts]


def product_terms(left, w_v, own, theirs, m, transposed, tile):
    rows, cols = own.shape[1:]

    def body(i, carry):
        span = pl.ds(pl.multiple_of(i * tile, tile), tile)
        if transposed:
            part = contract_last(left, w_v[span, :])
        else:
            part = jnp.dot(left, w_v[:, span], preferred_element_type=F32)
        own[m, :, span] = part[:rows].astype(BF16)
        theirs[m, :, span] = part[rows:].astype(BF16)
        return carry

    lax.fori_loop(0, cols // tile, body, 0)


def core_window(ref, width):
    stride = ref.shape[1] // CORES
    first = pl.multiple_of(lax.axis_index("core") * stride, 128)
    return ref.at[:, pl.ds(first, width)]


def product_scatter_kernel(chips, transposed, tile, back, *refs):
    refs = list(refs)
    take = lambda count: [refs.pop(0) for _ in range(count)]
    h_ref, w_ref = take(2)
    back_in = take(5) if back else None
    a_ref = take(1)[0] if back else None
    o_ref = take(1)[0]
    back_out = take(1) if back else None
    q_ref = take(1)[0] if back else None
    h_v, w_v = take(2)
    scratch = take(8)
    w_sem, h_sem = take(2)
    back_scratch = take(2) if back else None
    a_v, a_sem = take(2) if back else (None, None)
    c, k = lax.axis_index("ctx"), lax.axis_index("core")
    rows = o_ref.shape[0]
    own, theirs = scratch[:2]
    if transposed:
        w_load = pltpu.make_async_copy(core_window(w_ref, w_v.shape[1]), w_v, w_sem)
    else:
        w_load = pltpu.make_async_copy(w_ref, w_v, w_sem)
    w_load.start()
    loads = {}
    for m in block_order(chips):
        for side, span in enumerate(block_rows(chips, rows, m)):
            load = pltpu.make_async_copy(h_ref.at[span], h_v.at[span], h_sem.at[m, side])
            load.start()
            loads[m, side] = load
    fillers = []
    if back:
        a_load = pltpu.make_async_copy(a_ref, a_v, a_sem)
        a_load.start()
        fillers = attend_back_parts(*back, *back_in, *back_out, *back_scratch)
        fillers.append(a_load.wait)
        fillers += first_product_parts(a_v, back_out[0], q_ref, tile)
    greet(chips, c, k)
    w_load.wait()

    def compute(m):
        spans = block_rows(chips, rows, m)
        for side in range(CORES):
            loads[m, side].wait()
        left = jnp.concatenate([h_v[span, :] for span in spans], axis=0)
        product_terms(left, w_v, own, theirs, m, transposed, tile)

    exchange(chips, scratch, o_ref, compute, fillers)


def first_product_parts(left, right, target, tile, after=None):
    def part(i):
        span = slice(i * tile, (i + 1) * tile)
        target[span, :] = contract_first(left[:, span], right[...]).astype(BF16)
        if after is not None:
            after(i, span)

    return [functools.partial(part, i) for i in range(left.shape[1] // tile)]


def product_scatter(h, w, chips, ident, transposed, back=None):
    depth = h.shape[1]
    cols = w.shape[0] if transposed else w.shape[1]
    rows = h.shape[0] // (CORES * chips)
    in_vmem = pl.BlockSpec(memory_space=pltpu.VMEM)
    in_place = pl.BlockSpec(memory_space=pl.ANY)
    operands, in_specs = [h, w], [in_place] * 2
    out_shape = [jax.ShapeDtypeStruct((rows, cols), F32)]
    back_scratch, sizes = [], None
    if back is not None:
        proj, grads, blocks, logsums, heads, size, acts = back
        operands += [proj, grads, blocks[:, :, None], blocks[:, None, :], logsums, acts]
        in_specs += [in_vmem] * 5 + [in_place]
        out_shape.append(jax.ShapeDtypeStruct(proj.shape, BF16))
        out_shape.append(jax.ShapeDtypeStruct((acts.shape[1], proj.shape[1]), BF16))
        back_scratch = [
            *[pltpu.VMEM((blocks.shape[1], size), F32)] * 2,
            pltpu.VMEM(acts.shape, BF16),
            pltpu.SemaphoreType.DMA,
        ]
        sizes = (heads, size, 256)
    result = pl.pallas_call(
        functools.partial(product_scatter_kernel, chips, transposed, 512, sizes),
        name="product_scatter",
        out_shape=out_shape,
        in_specs=in_specs,
        out_specs=[in_vmem] * len(out_shape),
        scratch_shapes=[
            pltpu.VMEM(h.shape, BF16),
            pltpu.VMEM((cols, depth) if transposed else w.shape, BF16),
            *exchange_scratch(chips, rows, cols),
            pltpu.SemaphoreType.DMA,
            pltpu.SemaphoreType.DMA((chips, CORES)),
            *back_scratch,
        ],
        cost_estimate=pl.CostEstimate(flops=1_000_000_000, bytes_accessed=0, transcendentals=0),
        compiler_params=pltpu.CompilerParams(
            collective_id=ident, has_side_effects=True, vmem_limit_bytes=VMEM_LIMIT
        ),
    )(*operands)
    return result if len(out_shape) > 1 else result[0]


def gelu_slope(u):
    scale, cubic = math.sqrt(2.0 / math.pi), 0.044715
    square = u * u
    bend = jnp.tanh(scale * u * (1.0 + cubic * square))
    return 0.5 * (1.0 + bend) + 0.5 * u * (1.0 - bend * bend) * scale * (1.0 + 3.0 * cubic * square)


def hidden_back_kernel(
    chips, tile, g_ref, d_ref, p_ref, u_ref, a_ref, o_ref, s_ref, g_v, p_v, e_v, d_v, u_v, *refs
):
    scratch, (w_sem, load_sem, a_sem, store_sem) = refs[:8], refs[8:]
    c, k = lax.axis_index("ctx"), lax.axis_index("core")
    rows = o_ref.shape[0]
    own, theirs = scratch[:2]
    d_load = pltpu.make_async_copy(core_window(d_ref, d_v.shape[1]), d_v, w_sem.at[0])
    u_load = pltpu.make_async_copy(core_window(u_ref, u_v.shape[1]), u_v, w_sem.at[1])
    d_load.start()
    loads, stores = {}, []
    for place, m in enumerate(block_order(chips)):
        if place == 1:
            u_load.start()
        for side, span in enumerate(block_rows(chips, rows, m)):
            for which, (source, target) in enumerate(((g_ref, g_v), (p_ref, p_v))):
                load = pltpu.make_async_copy(
                    source.at[span], target.at[span], load_sem.at[which, m, side]
                )
                load.start()
                loads.setdefault(m, []).append(load)
    greet(chips, c, k)
    d_load.wait()

    def compute(m):
        spans = block_rows(chips, rows, m)
        for load in loads[m]:
            load.wait()
        grads = jnp.concatenate([g_v[span, :] for span in spans], axis=0)

        def body(i, carry):
            cols = pl.ds(pl.multiple_of(i * tile, tile), tile)
            part = jnp.dot(grads, d_v[:, cols], preferred_element_type=F32)
            for side, span in enumerate(spans):
                slope = gelu_slope(p_v[span, cols])
                e_v[span, cols] = (part[side * rows : (side + 1) * rows] * slope).astype(BF16)
            return carry

        lax.fori_loop(0, e_v.shape[1] // tile, body, 0)
        if m == block_order(chips)[0]:
            u_load.wait()
        left = jnp.concatenate([e_v[span, :] for span in spans], axis=0)
        product_terms(left, u_v, own, theirs, m, True, tile)

    a_load = pltpu.make_async_copy(a_ref, g_v, a_sem)

    def store(i, span):
        copy = pltpu.make_async_copy(d_v.at[span], s_ref.at[span], store_sem.at[i])
        copy.start()
        stores.append(copy)

    fillers = [a_load.start, a_load.wait, *first_product_parts(g_v, e_v, d_v, tile, store)]
    exchange(chips, scratch, o_ref, compute, fillers)
    for copy in stores:
        copy.wait()


def hidden_back(grads, w_down, pre, w_up, acts, chips, ident):
    cols, width = w_up.shape[0], pre.shape[1]
    rows = grads.shape[0] // (CORES * chips)
    tile = 512
    in_place = pl.BlockSpec(memory_space=pl.ANY)
    return pl.pallas_call(
        functools.partial(hidden_back_kernel, chips, tile),
        name="hidden_back",
        out_shape=[
            jax.ShapeDtypeStruct((rows, cols), F32),
            jax.ShapeDtypeStruct((cols, width), BF16),
        ],
        in_specs=[in_place] * 5,
        out_specs=[pl.BlockSpec(memory_space=pltpu.VMEM), in_place],
        scratch_shapes=[
            pltpu.VMEM(grads.shape, BF16),
            pltpu.VMEM(pre.shape, pre.dtype),
            pltpu.VMEM(pre.shape, BF16),
            pltpu.VMEM((w_down.shape[0], width), BF16),
            pltpu.VMEM((cols, width), BF16),
            *exchange_scratch(chips, rows, cols),
            pltpu.SemaphoreType.DMA((2,)),
            pltpu.SemaphoreType.DMA((2, chips, CORES)),
            pltpu.SemaphoreType.DMA,
            pltpu.SemaphoreType.DMA((cols // tile,)),
        ],
        cost_estimate=pl.CostEstimate(flops=1_000_000_000, bytes_accessed=0, transcendentals=0),
        compiler_params=pltpu.CompilerParams(
            collective_id=ident, has_side_effects=True, vmem_limit_bytes=VMEM_LIMIT
        ),
    )(grads, w_down, pre, w_up, acts)


def deal_kernel(chips, planes, parts, b_ref, x_ref, o_ref, t_ref, landed, heard, *sems):
    send_sem, recv_sem, sum_send, sum_recv = sems
    c, z, k = lax.axis_index("ctx"), lax.axis_index("z"), lax.axis_index("core")
    team, count, width = landed.shape
    peers = [{"ctx": c ^ m, "core": core} for m in range(1, chips) for core in (k, 1 - k)]
    peers.append({"core": 1 - k})
    lines = [{"z": z ^ mask} for mask in range(1, planes)]
    groups = [[{"ctx": c ^ m} for m in range(1, chips)], [{"core": 1 - k}], lines]
    barrier = pltpu.get_barrier_semaphore()
    for friend in peers + lines:
        pl.semaphore_signal(barrier, inc=1, device_id=friend, device_id_type=MESH)
    me = c * CORES + k
    landed[me] = b_ref[me]
    t_ref[...] = x_ref[...]
    pl.semaphore_wait(barrier, len(peers) + len(lines))
    copies = []
    for place, peer in enumerate(peers):
        target = peer.get("ctx", c) * CORES + peer["core"]
        copy = pltpu.make_async_remote_copy(
            src_ref=b_ref.at[target],
            dst_ref=landed.at[me],
            send_sem=send_sem.at[place],
            recv_sem=recv_sem.at[place],
            device_id=peer,
            device_id_type=MESH,
        )
        copies.append(copy)
    slot = 0
    for group in groups:
        sums = []
        for partner in group:
            sums.append(
                pltpu.make_async_remote_copy(
                    src_ref=t_ref,
                    dst_ref=heard.at[slot],
                    send_sem=sum_send.at[slot],
                    recv_sem=sum_recv.at[slot],
                    device_id=partner,
                    device_id_type=MESH,
                )
            )
            slot += 1
        for total in sums:
            total.start()
        if group is groups[0]:
            for copy in copies:
                copy.start()
        for total in sums:
            total.wait()
        for place in range(slot - len(sums), slot):
            t_ref[...] += heard[place]
    for copy in copies:
        copy.wait()
    piece = width // parts
    whole = o_ref.shape[1] // parts
    for source in range(team):
        for part in range(parts):
            first = part * whole + source * piece
            o_ref[:, first : first + piece] = landed[
                source, :, part * piece : (part + 1) * piece
            ].astype(F32)


def deal(blocks, parts, x, chips, planes, ident):
    team, count, width = blocks.shape
    in_vmem = pl.BlockSpec(memory_space=pltpu.VMEM)
    steps = chips - 1 + 1 + planes - 1
    return pl.pallas_call(
        functools.partial(deal_kernel, chips, planes, parts),
        name="deal",
        out_shape=[
            jax.ShapeDtypeStruct((count, team * width), F32),
            jax.ShapeDtypeStruct(x.shape, F32),
        ],
        in_specs=[in_vmem] * 2,
        out_specs=[in_vmem] * 2,
        scratch_shapes=[
            pltpu.VMEM(blocks.shape, BF16),
            pltpu.VMEM((steps, *x.shape), F32),
            pltpu.SemaphoreType.DMA((team - 1,)),
            pltpu.SemaphoreType.DMA((team - 1,)),
            pltpu.SemaphoreType.DMA((steps,)),
            pltpu.SemaphoreType.DMA((steps,)),
        ],
        compiler_params=pltpu.CompilerParams(collective_id=ident, has_side_effects=True),
    )(blocks, x)


def attend_kernel(heads, size, step, p_ref, key_blk, query_blk, o_ref, log_ref):
    length = p_ref.shape[0]
    scale = 1.0 / math.sqrt(size)
    key_block = key_blk[0]
    for head in range(heads):
        keys = p_ref[:, (heads + head) * size : (heads + head + 1) * size]
        values = p_ref[:, (2 * heads + head) * size : (2 * heads + head + 1) * size]
        values_t = values.T
        for first in range(0, length, step):
            span = slice(first, first + step)
            queries = p_ref[span, head * size : (head + 1) * size]
            scores = contract_last(keys, queries) * scale
            scores = jnp.where(key_block <= query_blk[0, :, span], scores, -jnp.inf)
            top = jnp.max(scores, axis=0, keepdims=True)
            weights = jnp.exp(scores - top)
            total = jnp.sum(weights, axis=0, keepdims=True)
            prob = (weights * (1.0 / total)).astype(BF16)
            out_t = jnp.dot(values_t, prob, preferred_element_type=F32)
            o_ref[span, head * size : (head + 1) * size] = out_t.T.astype(BF16)
            log_ref[0, head : head + 1, span] = top + jnp.log(total)


def attend_back_parts(
    heads, size, step, p_ref, g_ref, key_blk, query_blk, log_ref, d_ref, dk, dv
):
    length = key_blk.shape[1]
    scale = 1.0 / math.sqrt(size)

    def part(seq, head):
        whole = pl.ds(seq * length, length)
        at_query, at_key, at_value = [
            slice((j * heads + head) * size, (j * heads + head + 1) * size) for j in range(3)
        ]
        keys, values = p_ref[whole, at_key], p_ref[whole, at_value]
        keys_t = keys.T
        key_block = key_blk[seq]
        for first in range(0, length, step):
            here = slice(first, first + step)
            span = pl.ds(seq * length + first, step)
            queries, grads = p_ref[span, at_query], g_ref[span, at_query]
            scores = contract_last(keys, queries) * scale
            shifted = jnp.where(
                key_block <= query_blk[seq, :, here],
                scores - log_ref[seq, head : head + 1, here],
                -jnp.inf,
            )
            prob = jnp.exp(shifted)
            grad_prob = contract_last(values, grads)
            row_dot = jnp.sum(prob * grad_prob, axis=0, keepdims=True)
            grad_raw = (prob * (grad_prob - row_dot) * scale).astype(BF16)
            dk_part = jnp.dot(grad_raw, queries, preferred_element_type=F32)
            dv_part = jnp.dot(prob.astype(BF16), grads, preferred_element_type=F32)
            if first == 0:
                dk[...] = dk_part
                dv[...] = dv_part
            else:
                dk[...] += dk_part
                dv[...] += dv_part
            dq_t = jnp.dot(keys_t, grad_raw, preferred_element_type=F32)
            d_ref[span, at_query] = dq_t.T.astype(BF16)
        d_ref[whole, at_key] = dk[...].astype(BF16)
        d_ref[whole, at_value] = dv[...].astype(BF16)

    return [
        functools.partial(part, seq, head)
        for seq in range(key_blk.shape[0])
        for head in range(heads)
    ]


def attention_specs(length, width, heads):
    wide = pl.BlockSpec((length, 3 * width), lambda s: (s, 0))
    narrow = pl.BlockSpec((length, width), lambda s: (s, 0))
    column = pl.BlockSpec((1, length, 1), lambda s: (s, 0, 0))
    row = pl.BlockSpec((1, 1, length), lambda s: (s, 0, 0))
    logs = pl.BlockSpec((1, heads, length), lambda s: (s, 0, 0))
    return wide, narrow, column, row, logs


def attend(proj, blocks, heads, size):
    length = blocks.shape[1]
    width = heads * size
    wide, narrow, column, row, logs = attention_specs(length, width, heads)
    return pl.pallas_call(
        functools.partial(attend_kernel, heads, size, 256),
        name="attend",
        grid=(blocks.shape[0],),
        out_shape=(
            jax.ShapeDtypeStruct((proj.shape[0], width), BF16),
            jax.ShapeDtypeStruct((blocks.shape[0], heads, length), F32),
        ),
        in_specs=[wide, column, row],
        out_specs=(narrow, logs),
        cost_estimate=pl.CostEstimate(flops=1_000_000_000, bytes_accessed=0, transcendentals=0),
        compiler_params=pltpu.CompilerParams(vmem_limit_bytes=VMEM_LIMIT),
    )(proj, blocks[:, :, None], blocks[:, None, :])


def shards(
    tokens,
    block_ids,
    piece_order,
    norm1_gain,
    norm1_bias,
    w_qkv,
    w_out,
    norm2_gain,
    norm2_bias,
    w_up,
    w_down,
    grad_out,
):
    chips, depth = lax.axis_size("ctx"), lax.axis_size("z")
    c, k = lax.axis_index("ctx"), lax.axis_index("core")
    row_count, model_width = tokens.shape[1:]
    hidden_width = w_up.shape[1]
    size = model_width // HEADS
    team = CORES * chips
    heads = HEADS // team
    head_cols = heads * size
    ff_cols = hidden_width // team
    fsdp = ("z", "core")

    def core_cols(gathered, width, first=0):
        return lax.dynamic_slice_in_dim(gathered, first + k * width, width, 1)

    def across_z(w):
        return lax.all_gather(w, fsdp, axis=0, tiled=True)

    attn_cols, up_cols, down_cols = pick_columns(w_qkv, w_out, w_up, w_down, head_cols, ff_cols)
    attn_weights = across_z(attn_cols)
    inputs = tokens.reshape(row_count, model_width).astype(F32)
    grad_y = grad_out.reshape(row_count, model_width)
    normed_one, unit_one, inv_one = normalize(inputs, norm1_gain, norm1_bias)
    acts_one = plane_gather(normed_one.astype(BF16), chips, 1)
    acts_one, block_ids, grad_y = lax.optimization_barrier((acts_one, block_ids, grad_y))
    up_weights = across_z(up_cols)
    down_weights = across_z(down_cols)
    blocks = stored_blocks(block_ids, piece_order, row_count // 2)
    blocks = lax.all_gather(blocks, "core", axis=0, tiled=True)

    grads_y = plane_gather(grad_y, chips, 1)
    my_attn = core_cols(attn_weights, 4 * head_cols)
    out_blocks = my_attn[:, 3 * head_cols :]
    my_out = lax.all_to_all(out_blocks, ("ctx", "core"), split_axis=0, concat_axis=1, tiled=True)
    proj = jnp.dot(acts_one, my_attn[:, : 3 * head_cols], preferred_element_type=F32).astype(BF16)
    attended, logsums = attend(proj, blocks, heads, size)
    residual = inputs + product_scatter(attended, my_out, chips, 2, False)
    normed_two, unit_two, inv_two = normalize(residual, norm2_gain, norm2_bias)
    acts_two = plane_gather(normed_two.astype(BF16), chips, 1)
    up_weights, acts_two = lax.optimization_barrier((up_weights, acts_two))
    my_up = core_cols(up_weights, ff_cols)
    pre_act = jnp.dot(acts_two, my_up, preferred_element_type=F32)
    hidden = jax.nn.gelu(pre_act, approximate=True).astype(BF16)

    def sum_planes(grad):
        parts = grad.reshape(chips, -1, grad.shape[1])
        return lax.psum_scatter(parts, "z", scatter_dimension=1, tiled=True)

    def spread_rows(summed):
        summed = summed.reshape(team, -1, summed.shape[2])
        return lax.all_to_all(summed, ("ctx", "core"), split_axis=0, concat_axis=0, tiled=True)

    def whole_columns(parts, width):
        count = parts.shape[1]
        return (
            parts.reshape(team, count, -1, width)
            .transpose(1, 2, 0, 3)
            .reshape(count, -1)
            .astype(F32)
        )

    down_part = contract_first(grads_y, hidden).astype(BF16)
    down_weights, down_part = lax.optimization_barrier((down_weights, down_part))
    down_sum = sum_planes(down_part)
    grad_act_two, up_part = hidden_back(
        grads_y, down_weights, pre_act, up_weights, acts_two, chips, 3
    )
    up_sum = sum_planes(up_part)
    grad_res = grad_y.astype(F32) + normalize_back(grad_act_two, unit_two, inv_two, norm2_gain)
    grads_res = plane_gather(grad_res.astype(BF16), chips, 1)
    grad_attended = contract_last(grads_res, my_out).astype(BF16)
    out_part = contract_first(attended, grads_res).astype(BF16)
    grad_attended, out_part, down_sum = lax.optimization_barrier(
        (grad_attended, out_part, down_sum)
    )
    down_parts = spread_rows(down_sum)
    out_sum = lax.psum_scatter(out_part, "z", scatter_dimension=0, tiled=True)
    mixed_sum, grad_proj, proj_part = product_scatter(
        hidden, down_weights, chips, 5, True,
        back=(proj, grad_attended, blocks, logsums, heads, size, acts_one),
    )
    mixed = residual + mixed_sum
    grad_proj, proj_part, up_sum, out_sum, down_parts, mixed = lax.optimization_barrier(
        (grad_proj, proj_part, up_sum, out_sum, down_parts, mixed)
    )
    proj_sum = sum_planes(proj_part)
    up_parts = spread_rows(up_sum)
    moves = [(z * CORES + core, core * depth + z) for z in range(depth) for core in range(CORES)]
    out_sum = lax.ppermute(out_sum, fsdp, moves)
    grad_act_one = product_scatter(grad_proj, attn_weights, chips, 4, True)
    norm_parts = jnp.stack(
        [
            jnp.sum(grad_act_one * unit_one, axis=0),
            jnp.sum(grad_act_one, axis=0),
            jnp.sum(grad_act_two * unit_two, axis=0),
            jnp.sum(grad_act_two, axis=0),
        ]
    ).reshape(8, -1)
    norm_parts, up_parts, out_sum = lax.optimization_barrier((norm_parts, up_parts, out_sum))
    grad_down = whole_columns(down_parts, ff_cols)
    grad_up = whole_columns(up_parts, ff_cols)
    grad_wout = out_sum.astype(F32)
    grad_qkv, norm_sums = deal(
        proj_sum.reshape(team, -1, 3 * head_cols), 3, norm_parts, chips, depth, 6
    )
    grad_inputs = grad_res + normalize_back(grad_act_one, unit_one, inv_one, norm1_gain)
    out_shape = (1, row_count, model_width)
    return (
        mixed.reshape(out_shape).astype(BF16),
        grad_inputs.reshape(out_shape).astype(BF16),
        grad_qkv,
        grad_wout,
        grad_up,
        grad_down,
        *norm_sums.reshape(4, model_width),
    )


def solution(mesh):
    chips, across = mesh.shape["ctx"], mesh.shape["fsdp"]
    devices = np.asarray(mesh.devices).reshape(chips, across // CORES, CORES)
    cube = Mesh(devices, ("ctx", "z", "core"))
    fsdp = ("z", "core")
    rows = P(fsdp, "ctx", None)
    weight = P(fsdp, None)
    grad = P(("ctx", "z", "core"), None)
    return jax.shard_map(
        shards,
        mesh=cube,
        in_specs=(rows, weight, P(), P(), P(), weight, weight, P(), P(), weight, weight, rows),
        out_specs=(rows, rows, grad, grad, grad, grad, P(), P(), P(), P()),
        check_vma=False,
    )
```

```python
import functools
import math

import jax
import jax.numpy as jnp
import numpy as np
from jax import lax
from jax.experimental import pallas as pl
from jax.experimental.pallas import tpu as pltpu
from jax.sharding import Mesh, PartitionSpec as P

HEADS = 16
CORES = 2
LANES = 2
MESH = pl.DeviceIdType.MESH
VMEM_LIMIT = 56 << 20
norm_eps = 1e-05
F32 = jnp.float32
BF16 = jnp.bfloat16


def stored_blocks(seq_blocks, piece_order, piece_len):
    pieces = seq_blocks.reshape(seq_blocks.shape[0], -1, piece_len)
    return jnp.take(pieces, piece_order, axis=1).reshape(seq_blocks.shape)


def normalize(values, norm_gain, norm_bias):
    center = values - jnp.mean(values, axis=-1, keepdims=True)
    variance = jnp.mean(center * center, axis=-1, keepdims=True)
    inv_std = lax.rsqrt(variance + norm_eps)
    unit_vals = center * inv_std
    return (unit_vals * norm_gain + norm_bias, unit_vals, inv_std)


def normalize_back(grad_normed, unit_vals, inv_std, norm_gain):
    grad_unit = grad_normed * norm_gain
    mean_first = jnp.mean(grad_unit, axis=-1, keepdims=True)
    mean_second = jnp.mean(grad_unit * unit_vals, axis=-1, keepdims=True)
    return inv_std * (grad_unit - mean_first - unit_vals * mean_second)


def contract_last(left_arr, right_arr):
    return lax.dot_general(
        left_arr, right_arr, (((1,), (1,)), ((), ())), preferred_element_type=F32
    )


def contract_first(left_arr, right_arr):
    return lax.dot_general(
        left_arr, right_arr, (((0,), (0,)), ((), ())), preferred_element_type=F32
    )


def chip_bits(chips):
    return [1 << i for i in range(chips.bit_length() - 1)]


def lane_orders(chips):
    bits = chip_bits(chips)
    return [bits[lane:] + bits[:lane] for lane in range(LANES)]


def greet(chips, me_chip, me_core, others=()):
    barrier = pltpu.get_barrier_semaphore()
    friends = [{"ctx": me_chip ^ bit} for bit in chip_bits(chips)] + [{"core": 1 - me_core}]
    friends += others
    for friend in friends:
        pl.semaphore_signal(barrier, inc=1, device_id=friend, device_id_type=MESH)
    pl.semaphore_wait(barrier, len(friends))


def gather_scratch(chips, pieces):
    bits = len(chip_bits(chips))
    return [
        pltpu.SemaphoreType.DMA((bits + 1, chips, LANES, pieces)),
        pltpu.SemaphoreType.DMA((2, chips, LANES, pieces)),
    ]


def gather(chips, pieces, sems, x_ref, o_ref, fillers=(), on_block=None):
    send_sem, recv_sem = sems
    c, k = lax.axis_index("ctx"), lax.axis_index("core")
    rows = x_ref.shape[0]
    piece_rows = rows // (LANES * pieces)
    bits, orders = chip_bits(chips), lane_orders(chips)
    fillers, started = list(fillers), []

    def place(core, chip, lane, piece):
        return pl.ds((core * chips + chip) * rows + (lane * pieces + piece) * piece_rows, piece_rows)

    def send(source, m, lane, piece, step):
        if step < len(bits):
            bit = orders[lane][step]
            device, kind, landing = {"ctx": c ^ bit}, 0, m ^ bit
        else:
            device, kind, landing = {"core": 1 - k}, 1, m
        copy = pltpu.make_async_remote_copy(
            src_ref=source,
            dst_ref=o_ref.at[place(k, c ^ m, lane, piece)],
            send_sem=send_sem.at[step, m, lane, piece],
            recv_sem=recv_sem.at[kind, landing, lane, piece],
            device_id=device,
            device_id_type=MESH,
        )
        copy.start()
        started.append(copy)

    def arrived(kind, m, lane, piece):
        ref = o_ref.at[place(k if kind == 0 else 1 - k, c ^ m, lane, piece)]
        pltpu.make_async_remote_copy(
            src_ref=ref,
            dst_ref=ref,
            send_sem=send_sem.at[0, m, lane, piece],
            recv_sem=recv_sem.at[kind, m, lane, piece],
            device_id={"core": 1 - k},
            device_id_type=MESH,
        ).wait_recv()

    def finish(m):
        if on_block is not None and m:
            on_block(k, m)
        for piece, lane in own:
            arrived(1, m, lane, piece)
        if on_block is not None:
            on_block(1 - k, m)

    own = [(p, l) for p in range(pieces) for l in range(LANES)]
    for piece, lane in own:
        source = x_ref.at[pl.ds((lane * pieces + piece) * piece_rows, piece_rows)]
        for step in range(len(bits)):
            send(source, 0, lane, piece, step)
    for piece, lane in own:
        source = x_ref.at[pl.ds((lane * pieces + piece) * piece_rows, piece_rows)]
        send(source, 0, lane, piece, len(bits))
    items = sorted(
        (max(i for i, b in enumerate(orders[lane]) if m & b), bin(m).count("1"), piece, lane, m)
        for m in range(1, chips)
        for piece, lane in own
    )
    left = {m: len(own) for m in range(1, chips)}
    if on_block is not None:
        on_block(k, 0)
    done = [0]
    for count, (step, _, piece, lane, m) in enumerate(items):
        if fillers and count % max(1, len(items) // len(fillers)) == 0:
            fillers.pop(0)()
        arrived(0, m, lane, piece)
        source = o_ref.at[place(k, c ^ m, lane, piece)]
        for later in range(step + 1, len(bits) + 1):
            send(source, m, lane, piece, later)
        left[m] -= 1
        if left[m] == 0:
            done.append(m)
            finish(done.pop(0))
    for filler in fillers:
        filler()
    for m in done:
        finish(m)
    for copy in started:
        copy.wait_send()


def gather_kernel(chips, pieces, x_ref, o_ref, own_sem, *sems):
    c, k = lax.axis_index("ctx"), lax.axis_index("core")
    rows = x_ref.shape[0]
    local = pltpu.make_async_copy(x_ref, o_ref.at[pl.ds((k * chips + c) * rows, rows)], own_sem)
    local.start()
    greet(chips, c, k)
    gather(chips, pieces, sems, x_ref, o_ref)
    local.wait()


def plane_gather(x, chips, ident, pieces=2):
    rows, cols = x.shape
    return pl.pallas_call(
        functools.partial(gather_kernel, chips, pieces),
        name="plane_gather",
        out_shape=jax.ShapeDtypeStruct((CORES * chips * rows, cols), x.dtype),
        in_specs=[pl.BlockSpec(memory_space=pl.ANY)],
        out_specs=pl.BlockSpec(memory_space=pl.ANY),
        scratch_shapes=[pltpu.SemaphoreType.DMA, *gather_scratch(chips, pieces)],
        cost_estimate=pl.CostEstimate(flops=1_000_000_000, bytes_accessed=0, transcendentals=0),
        compiler_params=pltpu.CompilerParams(collective_id=ident, has_side_effects=True),
    )(x)


def attended_back_kernel(
    chips, pieces, x_ref, w_ref, h_ref, g_ref, s_ref, x_v, own_sem, *sems
):
    c, k = lax.axis_index("ctx"), lax.axis_index("core")
    rows = x_ref.shape[0]

    def span_of(core, m):
        return pl.ds(pl.multiple_of((core * chips + (c ^ m)) * rows, rows), rows)

    local = pltpu.make_async_copy(x_ref, x_v.at[span_of(k, 0)], own_sem)
    local.start()
    greet(chips, c, k)
    local.wait()

    def on_block(core, m):
        span = span_of(core, m)
        g_ref[span, :] = contract_last(x_v[span, :], w_ref[...]).astype(BF16)

    gather(chips, pieces, sems, x_ref, x_v, (), on_block)
    tile = 512
    for i in range(x_v.shape[1] // tile):
        span = slice(i * tile, (i + 1) * tile)
        s_ref[:, span] = contract_first(h_ref[...], x_v[:, span]).astype(BF16)


def attended_back(x, w, attended, chips, ident, pieces=2):
    rows, cols = x.shape
    total = CORES * chips * rows
    in_place, in_vmem = pl.BlockSpec(memory_space=pl.ANY), pl.BlockSpec(memory_space=pltpu.VMEM)
    return pl.pallas_call(
        functools.partial(attended_back_kernel, chips, pieces),
        name="attended_back",
        out_shape=[
            jax.ShapeDtypeStruct((total, w.shape[0]), BF16),
            jax.ShapeDtypeStruct((attended.shape[1], cols), BF16),
        ],
        in_specs=[in_place] + [in_vmem] * 2,
        out_specs=[in_vmem] * 2,
        scratch_shapes=[
            pltpu.VMEM((total, cols), BF16),
            pltpu.SemaphoreType.DMA,
            *gather_scratch(chips, pieces),
        ],
        cost_estimate=pl.CostEstimate(flops=1_000_000_000, bytes_accessed=0, transcendentals=0),
        compiler_params=pltpu.CompilerParams(
            collective_id=ident, has_side_effects=True, vmem_limit_bytes=VMEM_LIMIT
        ),
    )(x, w, attended)


def pick_kernel(head_cols, ff_cols, q_ref, o_ref, u_ref, d_ref, attn_ref, up_ref, down_ref, sem):
    c = lax.axis_index("ctx")
    width = o_ref.shape[1]
    copies = []

    def move(source, first, target, landing, count):
        first = pl.multiple_of(first, 128)
        copy = pltpu.make_async_copy(
            source.at[:, pl.ds(first, count)],
            target.at[:, pl.ds(landing, count)],
            sem.at[len(copies)],
        )
        copy.start()
        copies.append(copy)

    for core in range(CORES):
        first = (c * CORES + core) * head_cols
        for part in range(3):
            landing = (core * 4 + part) * head_cols
            move(q_ref, part * width + first, attn_ref, landing, head_cols)
        move(o_ref, first, attn_ref, (core * 4 + 3) * head_cols, head_cols)
    for source, target in ((u_ref, up_ref), (d_ref, down_ref)):
        move(source, c * (CORES * ff_cols), target, 0, CORES * ff_cols)
    for copy in copies:
        copy.wait()


def pick_columns(w_qkv, w_out, w_up, w_down, head_cols, ff_cols):
    rows = w_qkv.shape[0]
    in_place = pl.BlockSpec(memory_space=pl.ANY)
    in_vmem = pl.BlockSpec(memory_space=pltpu.VMEM)
    return pl.pallas_call(
        functools.partial(pick_kernel, head_cols, ff_cols),
        name="pick_columns",
        out_shape=[
            jax.ShapeDtypeStruct((rows, CORES * count), BF16)
            for count in (4 * head_cols, ff_cols, ff_cols)
        ],
        in_specs=[in_place] * 4,
        out_specs=[in_vmem] * 3,
        scratch_shapes=[pltpu.SemaphoreType.DMA((4 * CORES + 2,))],
    )(w_qkv, w_out, w_up, w_down)


def scatter_plan(chips):
    orders = lane_orders(chips)
    slots, sends = {}, {}
    for lane in range(LANES):
        count = 0
        for step, bit in enumerate(orders[lane]):
            gone = sum(orders[lane][: step + 1])
            for m in range(chips):
                if m & gone == 0:
                    slots[lane, step, m] = count
                    count += 1
        for m in range(1, chips):
            sends[m, lane] = min(i for i, b in enumerate(orders[lane]) if m & b)
    return orders, slots, sends


def block_order(chips):
    return sorted(range(chips), key=lambda m: (-bin(m).count("1"), m))


def exchange_scratch(chips, rows, cols):
    half = rows // LANES
    return [
        pltpu.VMEM((chips, rows, cols), BF16),
        pltpu.VMEM((chips, rows, cols), BF16),
        pltpu.VMEM((chips, rows, cols), BF16),
        pltpu.VMEM((LANES, chips - 1, half, cols), BF16),
        pltpu.SemaphoreType.DMA((chips, LANES)),
        pltpu.SemaphoreType.DMA((chips, LANES)),
        pltpu.SemaphoreType.DMA((LANES, chips - 1)),
        pltpu.SemaphoreType.DMA((LANES, chips - 1)),
    ]


def exchange(chips, scratch, o_ref, compute, fillers=()):
    own, theirs, from_core, from_chip, core_send, core_recv, chip_send, chip_recv = scratch
    c, k = lax.axis_index("ctx"), lax.axis_index("core")
    half = o_ref.shape[0] // LANES
    orders, slots, sends = scatter_plan(chips)
    waits = []

    def share(m, lane):
        rows = pl.ds(lane * half, half)
        copy = pltpu.make_async_remote_copy(
            src_ref=theirs.at[m, rows],
            dst_ref=from_core.at[m, rows],
            send_sem=core_send.at[m, lane],
            recv_sem=core_recv.at[m, lane],
            device_id={"core": 1 - k},
            device_id_type=MESH,
        )
        copy.start()
        waits.append(copy)
        return copy

    def combine(m, lane, core_copy):
        rows = pl.ds(lane * half, half)
        core_copy.wait_recv()
        total = own[m, rows, :].astype(F32) + from_core[m, rows, :].astype(F32)
        last = sends.get((m, lane), len(orders[lane]))
        for step in range(last):
            slot = slots[lane, step, m]
            landed = from_chip.at[lane, slot]
            pltpu.make_async_remote_copy(
                src_ref=landed,
                dst_ref=landed,
                send_sem=chip_send.at[lane, slot],
                recv_sem=chip_recv.at[lane, slot],
                device_id={"core": 1 - k},
                device_id_type=MESH,
            ).wait_recv()
            total = total + from_chip[lane, slot].astype(F32)
        if m == 0:
            o_ref[rows, :] = total.astype(o_ref.dtype)
            return
        own[m, rows, :] = total.astype(BF16)
        bit = orders[lane][last]
        slot = slots[lane, last, m ^ bit]
        copy = pltpu.make_async_remote_copy(
            src_ref=own.at[m, rows],
            dst_ref=from_chip.at[lane, slot],
            send_sem=chip_send.at[lane, slot],
            recv_sem=chip_recv.at[lane, slot],
            device_id={"ctx": c ^ bit},
            device_id_type=MESH,
        )
        copy.start()
        waits.append(copy)

    fillers, pending, last = list(fillers), [], len(orders[0])

    def settle(level):
        for unit in [u for u in pending if sends.get(u[:2], last) <= level]:
            pending.remove(unit)
            combine(*unit)

    for m in block_order(chips):
        compute(m)
        fresh = [(m, lane, share(m, lane)) for lane in range(LANES)]
        settle(0)
        pending += fresh
    settle(0)
    for level in range(1, last + 1):
        count = -(-len(fillers) // (last + 1 - level))
        for filler in fillers[:count]:
            filler()
        fillers = fillers[count:]
        settle(level)
    for copy in waits:
        copy.wait_send()


def block_rows(chips, rows, m):
    c, k = lax.axis_index("ctx"), lax.axis_index("core")
    starts = [(core * chips + (c ^ m)) * rows for core in (k, 1 - k)]
    return [pl.ds(pl.multiple_of(start, rows), rows) for start in starts]


def product_terms(left, w_v, own, theirs, m, transposed, tile):
    rows, cols = own.shape[1:]

    def body(i, carry):
        span = pl.ds(pl.multiple_of(i * tile, tile), tile)
        if transposed:
            part = contract_last(left, w_v[span, :])
        else:
            part = jnp.dot(left, w_v[:, span], preferred_element_type=F32)
        own[m, :, span] = part[:rows].astype(BF16)
        theirs[m, :, span] = part[rows:].astype(BF16)
        return carry

    lax.fori_loop(0, cols // tile, body, 0)


def core_window(ref, width):
    stride = ref.shape[1] // CORES
    first = pl.multiple_of(lax.axis_index("core") * stride, 128)
    return ref.at[:, pl.ds(first, width)]


def product_scatter_kernel(chips, transposed, tile, back, *refs):
    refs = list(refs)
    take = lambda count: [refs.pop(0) for _ in range(count)]
    h_ref, w_ref = take(2)
    back_in = take(5) if back else None
    a_ref = take(1)[0] if back else None
    o_ref = take(1)[0]
    back_out = take(1) if back else None
    q_ref = take(1)[0] if back else None
    h_v, w_v = take(2)
    scratch = take(8)
    w_sem, h_sem = take(2)
    back_scratch = take(2) if back else None
    a_v, a_sem = take(2) if back else (None, None)
    c, k = lax.axis_index("ctx"), lax.axis_index("core")
    rows = o_ref.shape[0]
    own, theirs = scratch[:2]
    if transposed:
        w_load = pltpu.make_async_copy(core_window(w_ref, w_v.shape[1]), w_v, w_sem)
    else:
        w_load = pltpu.make_async_copy(w_ref, w_v, w_sem)
    w_load.start()
    loads = {}
    for m in block_order(chips):
        for side, span in enumerate(block_rows(chips, rows, m)):
            load = pltpu.make_async_copy(h_ref.at[span], h_v.at[span], h_sem.at[m, side])
            load.start()
            loads[m, side] = load
    fillers = []
    if back:
        a_load = pltpu.make_async_copy(a_ref, a_v, a_sem)
        a_load.start()
        fillers = attend_back_parts(*back, *back_in, *back_out, *back_scratch)
        fillers.append(a_load.wait)
        fillers += first_product_parts(a_v, back_out[0], q_ref, tile)
    greet(chips, c, k)
    w_load.wait()

    def compute(m):
        spans = block_rows(chips, rows, m)
        for side in range(CORES):
            loads[m, side].wait()
        left = jnp.concatenate([h_v[span, :] for span in spans], axis=0)
        product_terms(left, w_v, own, theirs, m, transposed, tile)

    exchange(chips, scratch, o_ref, compute, fillers)


def first_product_parts(left, right, target, tile, after=None):
    def part(i):
        span = slice(i * tile, (i + 1) * tile)
        target[span, :] = contract_first(left[:, span], right[...]).astype(BF16)
        if after is not None:
            after(i, span)

    return [functools.partial(part, i) for i in range(left.shape[1] // tile)]


def product_scatter(h, w, chips, ident, transposed, back=None):
    depth = h.shape[1]
    cols = w.shape[0] if transposed else w.shape[1]
    rows = h.shape[0] // (CORES * chips)
    in_vmem = pl.BlockSpec(memory_space=pltpu.VMEM)
    in_place = pl.BlockSpec(memory_space=pl.ANY)
    operands, in_specs = [h, w], [in_place] * 2
    out_shape = [jax.ShapeDtypeStruct((rows, cols), F32)]
    back_scratch, sizes = [], None
    if back is not None:
        proj, grads, blocks, logsums, heads, size, acts = back
        operands += [proj, grads, blocks[:, :, None], blocks[:, None, :], logsums, acts]
        in_specs += [in_vmem] * 5 + [in_place]
        out_shape.append(jax.ShapeDtypeStruct(proj.shape, BF16))
        out_shape.append(jax.ShapeDtypeStruct((acts.shape[1], proj.shape[1]), BF16))
        back_scratch = [
            *[pltpu.VMEM((blocks.shape[1], size), F32)] * 2,
            pltpu.VMEM(acts.shape, BF16),
            pltpu.SemaphoreType.DMA,
        ]
        sizes = (heads, size, 256)
    result = pl.pallas_call(
        functools.partial(product_scatter_kernel, chips, transposed, 512, sizes),
        name="product_scatter",
        out_shape=out_shape,
        in_specs=in_specs,
        out_specs=[in_vmem] * len(out_shape),
        scratch_shapes=[
            pltpu.VMEM(h.shape, BF16),
            pltpu.VMEM((cols, depth) if transposed else w.shape, BF16),
            *exchange_scratch(chips, rows, cols),
            pltpu.SemaphoreType.DMA,
            pltpu.SemaphoreType.DMA((chips, CORES)),
            *back_scratch,
        ],
        cost_estimate=pl.CostEstimate(flops=1_000_000_000, bytes_accessed=0, transcendentals=0),
        compiler_params=pltpu.CompilerParams(
            collective_id=ident, has_side_effects=True, vmem_limit_bytes=VMEM_LIMIT
        ),
    )(*operands)
    return result if len(out_shape) > 1 else result[0]


def gelu_slope(u):
    scale, cubic = math.sqrt(2.0 / math.pi), 0.044715
    square = u * u
    bend = jnp.tanh(scale * u * (1.0 + cubic * square))
    return 0.5 * (1.0 + bend) + 0.5 * u * (1.0 - bend * bend) * scale * (1.0 + 3.0 * cubic * square)


def hidden_back_kernel(
    chips, tile, g_ref, d_ref, p_ref, u_ref, a_ref, o_ref, s_ref, g_v, p_v, e_v, d_v, u_v, *refs
):
    scratch, (w_sem, load_sem, a_sem, store_sem) = refs[:8], refs[8:]
    c, k = lax.axis_index("ctx"), lax.axis_index("core")
    rows = o_ref.shape[0]
    own, theirs = scratch[:2]
    d_load = pltpu.make_async_copy(core_window(d_ref, d_v.shape[1]), d_v, w_sem.at[0])
    u_load = pltpu.make_async_copy(core_window(u_ref, u_v.shape[1]), u_v, w_sem.at[1])
    d_load.start()
    loads, stores = {}, []
    for place, m in enumerate(block_order(chips)):
        if place == 1:
            u_load.start()
        for side, span in enumerate(block_rows(chips, rows, m)):
            for which, (source, target) in enumerate(((g_ref, g_v), (p_ref, p_v))):
                load = pltpu.make_async_copy(
                    source.at[span], target.at[span], load_sem.at[which, m, side]
                )
                load.start()
                loads.setdefault(m, []).append(load)
    greet(chips, c, k)
    d_load.wait()

    def compute(m):
        spans = block_rows(chips, rows, m)
        for load in loads[m]:
            load.wait()
        grads = jnp.concatenate([g_v[span, :] for span in spans], axis=0)

        def body(i, carry):
            cols = pl.ds(pl.multiple_of(i * tile, tile), tile)
            part = jnp.dot(grads, d_v[:, cols], preferred_element_type=F32)
            for side, span in enumerate(spans):
                slope = gelu_slope(p_v[span, cols])
                e_v[span, cols] = (part[side * rows : (side + 1) * rows] * slope).astype(BF16)
            return carry

        lax.fori_loop(0, e_v.shape[1] // tile, body, 0)
        if m == block_order(chips)[0]:
            u_load.wait()
        left = jnp.concatenate([e_v[span, :] for span in spans], axis=0)
        product_terms(left, u_v, own, theirs, m, True, tile)

    a_load = pltpu.make_async_copy(a_ref, g_v, a_sem)

    def store(i, span):
        copy = pltpu.make_async_copy(d_v.at[span], s_ref.at[span], store_sem.at[i])
        copy.start()
        stores.append(copy)

    fillers = [a_load.start, a_load.wait, *first_product_parts(g_v, e_v, d_v, tile, store)]
    exchange(chips, scratch, o_ref, compute, fillers)
    for copy in stores:
        copy.wait()


def hidden_back(grads, w_down, pre, w_up, acts, chips, ident):
    cols, width = w_up.shape[0], pre.shape[1]
    rows = grads.shape[0] // (CORES * chips)
    tile = 512
    in_place = pl.BlockSpec(memory_space=pl.ANY)
    return pl.pallas_call(
        functools.partial(hidden_back_kernel, chips, tile),
        name="hidden_back",
        out_shape=[
            jax.ShapeDtypeStruct((rows, cols), F32),
            jax.ShapeDtypeStruct((cols, width), BF16),
        ],
        in_specs=[in_place] * 5,
        out_specs=[pl.BlockSpec(memory_space=pltpu.VMEM), in_place],
        scratch_shapes=[
            pltpu.VMEM(grads.shape, BF16),
            pltpu.VMEM(pre.shape, pre.dtype),
            pltpu.VMEM(pre.shape, BF16),
            pltpu.VMEM((w_down.shape[0], width), BF16),
            pltpu.VMEM((cols, width), BF16),
            *exchange_scratch(chips, rows, cols),
            pltpu.SemaphoreType.DMA((2,)),
            pltpu.SemaphoreType.DMA((2, chips, CORES)),
            pltpu.SemaphoreType.DMA,
            pltpu.SemaphoreType.DMA((cols // tile,)),
        ],
        cost_estimate=pl.CostEstimate(flops=1_000_000_000, bytes_accessed=0, transcendentals=0),
        compiler_params=pltpu.CompilerParams(
            collective_id=ident, has_side_effects=True, vmem_limit_bytes=VMEM_LIMIT
        ),
    )(grads, w_down, pre, w_up, acts)


def deal_kernel(chips, planes, b_ref, x_ref, landed, t_ref, heard, *sems):
    send_sem, recv_sem, sum_send, sum_recv = sems
    c, z, k = lax.axis_index("ctx"), lax.axis_index("z"), lax.axis_index("core")
    team, count, width = landed.shape
    peers = [{"ctx": c ^ m, "core": core} for m in range(1, chips) for core in (k, 1 - k)]
    peers.append({"core": 1 - k})
    lines = [{"z": z ^ mask} for mask in range(1, planes)]
    groups = [[{"ctx": c ^ m} for m in range(1, chips)], [{"core": 1 - k}], lines]
    barrier = pltpu.get_barrier_semaphore()
    for friend in peers + lines:
        pl.semaphore_signal(barrier, inc=1, device_id=friend, device_id_type=MESH)
    me = c * CORES + k
    landed[me] = b_ref[me]
    t_ref[...] = x_ref[...]
    pl.semaphore_wait(barrier, len(peers) + len(lines))
    copies = []
    for place, peer in enumerate(peers):
        target = peer.get("ctx", c) * CORES + peer["core"]
        copy = pltpu.make_async_remote_copy(
            src_ref=b_ref.at[target],
            dst_ref=landed.at[me],
            send_sem=send_sem.at[place],
            recv_sem=recv_sem.at[place],
            device_id=peer,
            device_id_type=MESH,
        )
        copies.append(copy)
    slot = 0
    for group in groups:
        sums = []
        for partner in group:
            sums.append(
                pltpu.make_async_remote_copy(
                    src_ref=t_ref,
                    dst_ref=heard.at[slot],
                    send_sem=sum_send.at[slot],
                    recv_sem=sum_recv.at[slot],
                    device_id=partner,
                    device_id_type=MESH,
                )
            )
            slot += 1
        for total in sums:
            total.start()
        if group is groups[0]:
            for copy in copies:
                copy.start()
        for total in sums:
            total.wait()
        for place in range(slot - len(sums), slot):
            t_ref[...] += heard[place]
    for copy in copies:
        copy.wait()


def columns_kernel(counts, *refs):
    blocks, targets = refs[: len(counts)], refs[len(counts) :]
    source = pl.program_id(0)
    for count, block, target in zip(counts, blocks, targets):
        piece = block.shape[2] // count
        whole = target.shape[1] // count
        for part in range(count):
            first = pl.multiple_of(part * whole + source * piece, piece) if count > 1 else 0
            target[:, pl.ds(first, piece)] = block[
                0, :, part * piece : (part + 1) * piece
            ].astype(F32)


def whole_columns(arrays, counts):
    team = arrays[0].shape[0]
    specs = []
    for array, count in zip(arrays, counts):
        rows, width = array.shape[1:]
        if count > 1:
            specs.append(pl.BlockSpec((rows, team * width), lambda i: (0, 0)))
        else:
            specs.append(pl.BlockSpec((rows, width), lambda i: (0, i)))
    return pl.pallas_call(
        functools.partial(columns_kernel, counts),
        name="whole_columns",
        grid=(team,),
        out_shape=[jax.ShapeDtypeStruct((a.shape[1], team * a.shape[2]), F32) for a in arrays],
        in_specs=[pl.BlockSpec((1, *a.shape[1:]), lambda i: (i, 0, 0)) for a in arrays],
        out_specs=specs,
    )(*arrays)


def deal(blocks, x, chips, planes, ident):
    team, count, width = blocks.shape
    in_vmem = pl.BlockSpec(memory_space=pltpu.VMEM)
    steps = chips - 1 + 1 + planes - 1
    return pl.pallas_call(
        functools.partial(deal_kernel, chips, planes),
        name="deal",
        out_shape=[
            jax.ShapeDtypeStruct(blocks.shape, BF16),
            jax.ShapeDtypeStruct(x.shape, F32),
        ],
        in_specs=[in_vmem] * 2,
        out_specs=[in_vmem] * 2,
        scratch_shapes=[
            pltpu.VMEM((steps, *x.shape), F32),
            pltpu.SemaphoreType.DMA((team - 1,)),
            pltpu.SemaphoreType.DMA((team - 1,)),
            pltpu.SemaphoreType.DMA((steps,)),
            pltpu.SemaphoreType.DMA((steps,)),
        ],
        compiler_params=pltpu.CompilerParams(collective_id=ident, has_side_effects=True),
    )(blocks, x)


def attend_kernel(heads, size, step, p_ref, key_blk, query_blk, o_ref, log_ref):
    length = p_ref.shape[0]
    scale = 1.0 / math.sqrt(size)
    key_block = key_blk[0]
    for head in range(heads):
        keys = p_ref[:, (heads + head) * size : (heads + head + 1) * size]
        values = p_ref[:, (2 * heads + head) * size : (2 * heads + head + 1) * size]
        values_t = values.T
        for first in range(0, length, step):
            span = slice(first, first + step)
            queries = p_ref[span, head * size : (head + 1) * size]
            scores = contract_last(keys, queries) * scale
            scores = jnp.where(key_block <= query_blk[0, :, span], scores, -jnp.inf)
            top = jnp.max(scores, axis=0, keepdims=True)
            weights = jnp.exp(scores - top)
            total = jnp.sum(weights, axis=0, keepdims=True)
            prob = (weights * (1.0 / total)).astype(BF16)
            out_t = jnp.dot(values_t, prob, preferred_element_type=F32)
            o_ref[span, head * size : (head + 1) * size] = out_t.T.astype(BF16)
            log_ref[0, head : head + 1, span] = top + jnp.log(total)


def attend_back_parts(
    heads, size, step, p_ref, g_ref, key_blk, query_blk, log_ref, d_ref, dk, dv
):
    length = key_blk.shape[1]
    scale = 1.0 / math.sqrt(size)

    def part(seq, head):
        whole = pl.ds(seq * length, length)
        at_query, at_key, at_value = [
            slice((j * heads + head) * size, (j * heads + head + 1) * size) for j in range(3)
        ]
        keys, values = p_ref[whole, at_key], p_ref[whole, at_value]
        keys_t = keys.T
        key_block = key_blk[seq]
        for first in range(0, length, step):
            here = slice(first, first + step)
            span = pl.ds(seq * length + first, step)
            queries, grads = p_ref[span, at_query], g_ref[span, at_query]
            scores = contract_last(keys, queries) * scale
            shifted = jnp.where(
                key_block <= query_blk[seq, :, here],
                scores - log_ref[seq, head : head + 1, here],
                -jnp.inf,
            )
            prob = jnp.exp(shifted)
            grad_prob = contract_last(values, grads)
            row_dot = jnp.sum(prob * grad_prob, axis=0, keepdims=True)
            grad_raw = (prob * (grad_prob - row_dot) * scale).astype(BF16)
            dk_part = jnp.dot(grad_raw, queries, preferred_element_type=F32)
            dv_part = jnp.dot(prob.astype(BF16), grads, preferred_element_type=F32)
            if first == 0:
                dk[...] = dk_part
                dv[...] = dv_part
            else:
                dk[...] += dk_part
                dv[...] += dv_part
            dq_t = jnp.dot(keys_t, grad_raw, preferred_element_type=F32)
            d_ref[span, at_query] = dq_t.T.astype(BF16)
        d_ref[whole, at_key] = dk[...].astype(BF16)
        d_ref[whole, at_value] = dv[...].astype(BF16)

    return [
        functools.partial(part, seq, head)
        for seq in range(key_blk.shape[0])
        for head in range(heads)
    ]


def attention_specs(length, width, heads):
    wide = pl.BlockSpec((length, 3 * width), lambda s: (s, 0))
    narrow = pl.BlockSpec((length, width), lambda s: (s, 0))
    column = pl.BlockSpec((1, length, 1), lambda s: (s, 0, 0))
    row = pl.BlockSpec((1, 1, length), lambda s: (s, 0, 0))
    logs = pl.BlockSpec((1, heads, length), lambda s: (s, 0, 0))
    return wide, narrow, column, row, logs


def attend(proj, blocks, heads, size):
    length = blocks.shape[1]
    width = heads * size
    wide, narrow, column, row, logs = attention_specs(length, width, heads)
    return pl.pallas_call(
        functools.partial(attend_kernel, heads, size, 256),
        name="attend",
        grid=(blocks.shape[0],),
        out_shape=(
            jax.ShapeDtypeStruct((proj.shape[0], width), BF16),
            jax.ShapeDtypeStruct((blocks.shape[0], heads, length), F32),
        ),
        in_specs=[wide, column, row],
        out_specs=(narrow, logs),
        cost_estimate=pl.CostEstimate(flops=1_000_000_000, bytes_accessed=0, transcendentals=0),
        compiler_params=pltpu.CompilerParams(vmem_limit_bytes=VMEM_LIMIT),
    )(proj, blocks[:, :, None], blocks[:, None, :])


def shards(
    tokens,
    block_ids,
    piece_order,
    norm1_gain,
    norm1_bias,
    w_qkv,
    w_out,
    norm2_gain,
    norm2_bias,
    w_up,
    w_down,
    grad_out,
):
    chips, depth = lax.axis_size("ctx"), lax.axis_size("z")
    c, k = lax.axis_index("ctx"), lax.axis_index("core")
    row_count, model_width = tokens.shape[1:]
    hidden_width = w_up.shape[1]
    size = model_width // HEADS
    team = CORES * chips
    heads = HEADS // team
    head_cols = heads * size
    ff_cols = hidden_width // team
    fsdp = ("z", "core")

    def core_cols(gathered, width, first=0):
        return lax.dynamic_slice_in_dim(gathered, first + k * width, width, 1)

    def across_z(w):
        return lax.all_gather(w, fsdp, axis=0, tiled=True)

    attn_cols, up_cols, down_cols = pick_columns(w_qkv, w_out, w_up, w_down, head_cols, ff_cols)
    attn_weights = across_z(attn_cols)
    inputs = tokens.reshape(row_count, model_width).astype(F32)
    grad_y = grad_out.reshape(row_count, model_width)
    normed_one, unit_one, inv_one = normalize(inputs, norm1_gain, norm1_bias)
    acts_one = plane_gather(normed_one.astype(BF16), chips, 1)
    acts_one, block_ids, grad_y = lax.optimization_barrier((acts_one, block_ids, grad_y))
    up_weights = across_z(up_cols)
    down_weights = across_z(down_cols)
    blocks = stored_blocks(block_ids, piece_order, row_count // 2)
    blocks = lax.all_gather(blocks, "core", axis=0, tiled=True)

    grads_y = plane_gather(grad_y, chips, 1)
    my_attn = core_cols(attn_weights, 4 * head_cols)
    out_blocks = my_attn[:, 3 * head_cols :]
    my_out = lax.all_to_all(out_blocks, ("ctx", "core"), split_axis=0, concat_axis=1, tiled=True)
    proj = jnp.dot(acts_one, my_attn[:, : 3 * head_cols], preferred_element_type=F32).astype(BF16)
    attended, logsums = attend(proj, blocks, heads, size)
    residual = inputs + product_scatter(attended, my_out, chips, 2, False)
    normed_two, unit_two, inv_two = normalize(residual, norm2_gain, norm2_bias)
    acts_two = plane_gather(normed_two.astype(BF16), chips, 1)
    up_weights, acts_two = lax.optimization_barrier((up_weights, acts_two))
    my_up = core_cols(up_weights, ff_cols)
    pre_act = jnp.dot(acts_two, my_up, preferred_element_type=F32)
    hidden = jax.nn.gelu(pre_act, approximate=True).astype(BF16)

    def sum_planes(grad):
        parts = grad.reshape(chips, -1, grad.shape[1])
        return lax.psum_scatter(parts, "z", scatter_dimension=1, tiled=True)

    def spread_rows(summed):
        summed = summed.reshape(team, -1, summed.shape[2])
        return lax.all_to_all(summed, ("ctx", "core"), split_axis=0, concat_axis=0, tiled=True)

    down_part = contract_first(grads_y, hidden).astype(BF16)
    down_weights, down_part = lax.optimization_barrier((down_weights, down_part))
    down_sum = sum_planes(down_part)
    grad_act_two, up_part = hidden_back(
        grads_y, down_weights, pre_act, up_weights, acts_two, chips, 3
    )
    up_sum = sum_planes(up_part)
    grad_res = grad_y.astype(F32) + normalize_back(grad_act_two, unit_two, inv_two, norm2_gain)
    grad_attended, out_part = attended_back(grad_res.astype(BF16), my_out, attended, chips, 7)
    grad_attended, out_part, down_sum = lax.optimization_barrier(
        (grad_attended, out_part, down_sum)
    )
    down_parts = spread_rows(down_sum)
    mixed_sum, grad_proj, proj_part = product_scatter(
        hidden, down_weights, chips, 5, True,
        back=(proj, grad_attended, blocks, logsums, heads, size, acts_one),
    )
    grad_proj, proj_part, up_sum, out_part, down_parts = lax.optimization_barrier(
        (grad_proj, proj_part, up_sum, out_part, down_parts)
    )
    proj_sum = sum_planes(proj_part)
    out_part = out_part.reshape(depth // CORES, CORES, -1, model_width)
    kept, given = [
        lax.dynamic_index_in_dim(out_part, core, 1, keepdims=False) for core in (k, 1 - k)
    ]
    taken = lax.ppermute(given, "core", [(0, 1), (1, 0)])
    up_parts = spread_rows(up_sum)
    kept_first = k == 0
    out_mine = jnp.concatenate(
        [jnp.where(kept_first, kept, taken), jnp.where(kept_first, taken, kept)]
    )
    grad_act_one = product_scatter(grad_proj, attn_weights, chips, 4, True)
    grad_act_one, out_mine, up_parts, proj_sum = lax.optimization_barrier(
        (grad_act_one, out_mine, up_parts, proj_sum)
    )
    grad_wout = lax.psum_scatter(out_mine, "z", scatter_dimension=0, tiled=True)
    grad_wout = grad_wout.reshape(-1, model_width).astype(F32)
    mixed = residual + mixed_sum
    norm_parts = jnp.stack(
        [
            jnp.sum(grad_act_one * unit_one, axis=0),
            jnp.sum(grad_act_one, axis=0),
            jnp.sum(grad_act_two * unit_two, axis=0),
            jnp.sum(grad_act_two, axis=0),
        ]
    ).reshape(8, -1)
    proj_parts, norm_sums = deal(
        proj_sum.reshape(team, -1, 3 * head_cols), norm_parts, chips, depth, 6
    )
    grad_qkv, grad_up, grad_down = whole_columns((proj_parts, up_parts, down_parts), (3, 1, 1))
    grad_inputs = grad_res + normalize_back(grad_act_one, unit_one, inv_one, norm1_gain)
    out_shape = (1, row_count, model_width)
    return (
        mixed.reshape(out_shape).astype(BF16),
        grad_inputs.reshape(out_shape).astype(BF16),
        grad_qkv,
        grad_wout,
        grad_up,
        grad_down,
        *norm_sums.reshape(4, model_width),
    )


def solution(mesh):
    chips, across = mesh.shape["ctx"], mesh.shape["fsdp"]
    devices = np.asarray(mesh.devices).reshape(chips, across // CORES, CORES)
    cube = Mesh(devices, ("ctx", "z", "core"))
    fsdp = ("z", "core")
    rows = P(fsdp, "ctx", None)
    weight = P(fsdp, None)
    grad = P(("ctx", "z", "core"), None)
    return jax.shard_map(
        shards,
        mesh=cube,
        in_specs=(rows, weight, P(), P(), P(), weight, weight, P(), P(), weight, weight, rows),
        out_specs=(rows, rows, grad, grad, grad, grad, P(), P(), P(), P()),
        check_vma=False,
    )
```

```python
import functools
import math

import jax
import jax.numpy as jnp
import numpy as np
from jax import lax
from jax.experimental import pallas as pl
from jax.experimental.pallas import tpu as pltpu
from jax.sharding import Mesh, PartitionSpec as P

HEADS = 16
CORES = 2
LANES = 2
MESH = pl.DeviceIdType.MESH
VMEM_LIMIT = 56 << 20
norm_eps = 1e-05
F32 = jnp.float32
BF16 = jnp.bfloat16


def stored_blocks(seq_blocks, piece_order, piece_len):
    pieces = seq_blocks.reshape(seq_blocks.shape[0], -1, piece_len)
    return jnp.take(pieces, piece_order, axis=1).reshape(seq_blocks.shape)


def normalize(values, norm_gain, norm_bias):
    center = values - jnp.mean(values, axis=-1, keepdims=True)
    variance = jnp.mean(center * center, axis=-1, keepdims=True)
    inv_std = lax.rsqrt(variance + norm_eps)
    unit_vals = center * inv_std
    return (unit_vals * norm_gain + norm_bias, unit_vals, inv_std)


def normalize_back(grad_normed, unit_vals, inv_std, norm_gain):
    grad_unit = grad_normed * norm_gain
    mean_first = jnp.mean(grad_unit, axis=-1, keepdims=True)
    mean_second = jnp.mean(grad_unit * unit_vals, axis=-1, keepdims=True)
    return inv_std * (grad_unit - mean_first - unit_vals * mean_second)


def contract_last(left_arr, right_arr):
    return lax.dot_general(
        left_arr, right_arr, (((1,), (1,)), ((), ())), preferred_element_type=F32
    )


def contract_first(left_arr, right_arr):
    return lax.dot_general(
        left_arr, right_arr, (((0,), (0,)), ((), ())), preferred_element_type=F32
    )


def chip_bits(chips):
    return [1 << i for i in range(chips.bit_length() - 1)]


def lane_orders(chips):
    bits = chip_bits(chips)
    return [bits[lane:] + bits[:lane] for lane in range(LANES)]


def greet(chips, me_chip, me_core, others=()):
    barrier = pltpu.get_barrier_semaphore()
    friends = [{"ctx": me_chip ^ bit} for bit in chip_bits(chips)] + [{"core": 1 - me_core}]
    friends += others
    for friend in friends:
        pl.semaphore_signal(barrier, inc=1, device_id=friend, device_id_type=MESH)
    pl.semaphore_wait(barrier, len(friends))


def gather_scratch(chips, pieces):
    bits = len(chip_bits(chips))
    return [
        pltpu.SemaphoreType.DMA((bits + 1, chips, LANES, pieces)),
        pltpu.SemaphoreType.DMA((2, chips, LANES, pieces)),
    ]


def gather(chips, pieces, sems, x_ref, o_ref, fillers=(), on_block=None):
    send_sem, recv_sem = sems
    c, k = lax.axis_index("ctx"), lax.axis_index("core")
    rows = x_ref.shape[0]
    piece_rows = rows // (LANES * pieces)
    bits, orders = chip_bits(chips), lane_orders(chips)
    fillers, started = list(fillers), []

    def place(core, chip, lane, piece):
        return pl.ds((core * chips + chip) * rows + (lane * pieces + piece) * piece_rows, piece_rows)

    def send(source, m, lane, piece, step):
        if step < len(bits):
            bit = orders[lane][step]
            device, kind, landing = {"ctx": c ^ bit}, 0, m ^ bit
        else:
            device, kind, landing = {"core": 1 - k}, 1, m
        copy = pltpu.make_async_remote_copy(
            src_ref=source,
            dst_ref=o_ref.at[place(k, c ^ m, lane, piece)],
            send_sem=send_sem.at[step, m, lane, piece],
            recv_sem=recv_sem.at[kind, landing, lane, piece],
            device_id=device,
            device_id_type=MESH,
        )
        copy.start()
        started.append(copy)

    def arrived(kind, m, lane, piece):
        ref = o_ref.at[place(k if kind == 0 else 1 - k, c ^ m, lane, piece)]
        pltpu.make_async_remote_copy(
            src_ref=ref,
            dst_ref=ref,
            send_sem=send_sem.at[0, m, lane, piece],
            recv_sem=recv_sem.at[kind, m, lane, piece],
            device_id={"core": 1 - k},
            device_id_type=MESH,
        ).wait_recv()

    def finish(m):
        if on_block is not None and m:
            on_block(k, m)
        for piece, lane in own:
            arrived(1, m, lane, piece)
        if on_block is not None:
            on_block(1 - k, m)

    own = [(p, l) for p in range(pieces) for l in range(LANES)]
    for piece, lane in own:
        source = x_ref.at[pl.ds((lane * pieces + piece) * piece_rows, piece_rows)]
        for step in range(len(bits)):
            send(source, 0, lane, piece, step)
    for piece, lane in own:
        source = x_ref.at[pl.ds((lane * pieces + piece) * piece_rows, piece_rows)]
        send(source, 0, lane, piece, len(bits))
    items = sorted(
        (max(i for i, b in enumerate(orders[lane]) if m & b), bin(m).count("1"), piece, lane, m)
        for m in range(1, chips)
        for piece, lane in own
    )
    left = {m: len(own) for m in range(1, chips)}
    if on_block is not None:
        on_block(k, 0)
    done = [0]
    for count, (step, _, piece, lane, m) in enumerate(items):
        if fillers and count % max(1, len(items) // len(fillers)) == 0:
            fillers.pop(0)()
        arrived(0, m, lane, piece)
        source = o_ref.at[place(k, c ^ m, lane, piece)]
        for later in range(step + 1, len(bits) + 1):
            send(source, m, lane, piece, later)
        left[m] -= 1
        if left[m] == 0:
            done.append(m)
            finish(done.pop(0))
    for filler in fillers:
        filler()
    for m in done:
        finish(m)
    for copy in started:
        copy.wait_send()


def gather_kernel(chips, pieces, x_ref, o_ref, own_sem, *sems):
    c, k = lax.axis_index("ctx"), lax.axis_index("core")
    rows = x_ref.shape[0]
    local = pltpu.make_async_copy(x_ref, o_ref.at[pl.ds((k * chips + c) * rows, rows)], own_sem)
    local.start()
    greet(chips, c, k)
    gather(chips, pieces, sems, x_ref, o_ref)
    local.wait()


def plane_gather(x, chips, ident, pieces=2):
    rows, cols = x.shape
    return pl.pallas_call(
        functools.partial(gather_kernel, chips, pieces),
        name="plane_gather",
        out_shape=jax.ShapeDtypeStruct((CORES * chips * rows, cols), x.dtype),
        in_specs=[pl.BlockSpec(memory_space=pl.ANY)],
        out_specs=pl.BlockSpec(memory_space=pl.ANY),
        scratch_shapes=[pltpu.SemaphoreType.DMA, *gather_scratch(chips, pieces)],
        cost_estimate=pl.CostEstimate(flops=1_000_000_000, bytes_accessed=0, transcendentals=0),
        compiler_params=pltpu.CompilerParams(collective_id=ident, has_side_effects=True),
    )(x)


def attended_back_kernel(
    chips, pieces, x_ref, w_ref, h_ref, g_ref, s_ref, x_v, own_sem, *sems
):
    c, k = lax.axis_index("ctx"), lax.axis_index("core")
    rows = x_ref.shape[0]

    def span_of(core, m):
        return pl.ds(pl.multiple_of((core * chips + (c ^ m)) * rows, rows), rows)

    local = pltpu.make_async_copy(x_ref, x_v.at[span_of(k, 0)], own_sem)
    local.start()
    greet(chips, c, k)
    local.wait()

    def on_block(core, m):
        span = span_of(core, m)
        g_ref[span, :] = contract_last(x_v[span, :], w_ref[...]).astype(BF16)

    gather(chips, pieces, sems, x_ref, x_v, (), on_block)
    tile = 512
    for i in range(x_v.shape[1] // tile):
        span = slice(i * tile, (i + 1) * tile)
        s_ref[:, span] = contract_first(h_ref[...], x_v[:, span]).astype(BF16)


def attended_back(x, w, attended, chips, ident, pieces=2):
    rows, cols = x.shape
    total = CORES * chips * rows
    in_place, in_vmem = pl.BlockSpec(memory_space=pl.ANY), pl.BlockSpec(memory_space=pltpu.VMEM)
    return pl.pallas_call(
        functools.partial(attended_back_kernel, chips, pieces),
        name="attended_back",
        out_shape=[
            jax.ShapeDtypeStruct((total, w.shape[0]), BF16),
            jax.ShapeDtypeStruct((attended.shape[1], cols), BF16),
        ],
        in_specs=[in_place] + [in_vmem] * 2,
        out_specs=[in_vmem] * 2,
        scratch_shapes=[
            pltpu.VMEM((total, cols), BF16),
            pltpu.SemaphoreType.DMA,
            *gather_scratch(chips, pieces),
        ],
        cost_estimate=pl.CostEstimate(flops=1_000_000_000, bytes_accessed=0, transcendentals=0),
        compiler_params=pltpu.CompilerParams(
            collective_id=ident, has_side_effects=True, vmem_limit_bytes=VMEM_LIMIT
        ),
    )(x, w, attended)


def pick_kernel(pieces, *refs):
    sources, (target, sem) = refs[:-2], refs[-2:]
    c = lax.axis_index("ctx")
    copies, landing = [], 0
    for place, (which, first, step, count) in enumerate(pieces):
        first = pl.multiple_of(first + c * step, 128)
        copy = pltpu.make_async_copy(
            sources[which].at[:, pl.ds(first, count)],
            target.at[:, pl.ds(landing, count)],
            sem.at[place],
        )
        copy.start()
        copies.append(copy)
        landing += count
    for copy in copies:
        copy.wait()


def pick_columns(weights, pieces):
    return pl.pallas_call(
        functools.partial(pick_kernel, pieces),
        name="pick_columns",
        out_shape=jax.ShapeDtypeStruct((weights[0].shape[0], sum(p[3] for p in pieces)), BF16),
        in_specs=[pl.BlockSpec(memory_space=pl.ANY)] * len(weights),
        out_specs=pl.BlockSpec(memory_space=pltpu.VMEM),
        scratch_shapes=[pltpu.SemaphoreType.DMA((len(pieces),))],
    )(*weights)


def scatter_plan(chips):
    orders = lane_orders(chips)
    slots, sends = {}, {}
    for lane in range(LANES):
        count = 0
        for step, bit in enumerate(orders[lane]):
            gone = sum(orders[lane][: step + 1])
            for m in range(chips):
                if m & gone == 0:
                    slots[lane, step, m] = count
                    count += 1
        for m in range(1, chips):
            sends[m, lane] = min(i for i, b in enumerate(orders[lane]) if m & b)
    return orders, slots, sends


def block_order(chips):
    return sorted(range(chips), key=lambda m: (-bin(m).count("1"), m))


def exchange_scratch(chips, rows, cols):
    half = rows // LANES
    return [
        pltpu.VMEM((chips, rows, cols), BF16),
        pltpu.VMEM((chips, rows, cols), BF16),
        pltpu.VMEM((chips, rows, cols), BF16),
        pltpu.VMEM((LANES, chips - 1, half, cols), BF16),
        pltpu.SemaphoreType.DMA((chips, LANES)),
        pltpu.SemaphoreType.DMA((chips, LANES)),
        pltpu.SemaphoreType.DMA((LANES, chips - 1)),
        pltpu.SemaphoreType.DMA((LANES, chips - 1)),
    ]


def exchange(chips, scratch, o_ref, compute, fillers=()):
    own, theirs, from_core, from_chip, core_send, core_recv, chip_send, chip_recv = scratch
    c, k = lax.axis_index("ctx"), lax.axis_index("core")
    half = o_ref.shape[0] // LANES
    orders, slots, sends = scatter_plan(chips)
    waits = []

    def share(m, lane):
        rows = pl.ds(lane * half, half)
        copy = pltpu.make_async_remote_copy(
            src_ref=theirs.at[m, rows],
            dst_ref=from_core.at[m, rows],
            send_sem=core_send.at[m, lane],
            recv_sem=core_recv.at[m, lane],
            device_id={"core": 1 - k},
            device_id_type=MESH,
        )
        copy.start()
        waits.append(copy)
        return copy

    def combine(m, lane, core_copy):
        rows = pl.ds(lane * half, half)
        core_copy.wait_recv()
        total = own[m, rows, :].astype(F32) + from_core[m, rows, :].astype(F32)
        last = sends.get((m, lane), len(orders[lane]))
        for step in range(last):
            slot = slots[lane, step, m]
            landed = from_chip.at[lane, slot]
            pltpu.make_async_remote_copy(
                src_ref=landed,
                dst_ref=landed,
                send_sem=chip_send.at[lane, slot],
                recv_sem=chip_recv.at[lane, slot],
                device_id={"core": 1 - k},
                device_id_type=MESH,
            ).wait_recv()
            total = total + from_chip[lane, slot].astype(F32)
        if m == 0:
            o_ref[rows, :] = total.astype(o_ref.dtype)
            return
        own[m, rows, :] = total.astype(BF16)
        bit = orders[lane][last]
        slot = slots[lane, last, m ^ bit]
        copy = pltpu.make_async_remote_copy(
            src_ref=own.at[m, rows],
            dst_ref=from_chip.at[lane, slot],
            send_sem=chip_send.at[lane, slot],
            recv_sem=chip_recv.at[lane, slot],
            device_id={"ctx": c ^ bit},
            device_id_type=MESH,
        )
        copy.start()
        waits.append(copy)

    fillers, pending, last = list(fillers), [], len(orders[0])

    def settle(level):
        for unit in [u for u in pending if sends.get(u[:2], last) <= level]:
            pending.remove(unit)
            combine(*unit)

    for m in block_order(chips):
        if m == 0:
            settle(0)
        compute(m)
        fresh = [(m, lane, share(m, lane)) for lane in range(LANES)]
        settle(0)
        pending += fresh
    settle(0)
    for level in range(1, last + 1):
        count = -(-len(fillers) // (last + 1 - level))
        for filler in fillers[:count]:
            filler()
        fillers = fillers[count:]
        settle(level)
    for copy in waits:
        copy.wait_send()


def block_rows(chips, rows, m):
    c, k = lax.axis_index("ctx"), lax.axis_index("core")
    starts = [(core * chips + (c ^ m)) * rows for core in (k, 1 - k)]
    return [pl.ds(pl.multiple_of(start, rows), rows) for start in starts]


def block_place(rows, m, side=None):
    if side is None:
        return slice(m * CORES * rows, (m + 1) * CORES * rows)
    return pl.ds((m * CORES + side) * rows, rows)


def product_terms(left, w_v, own, theirs, m, transposed, tile):
    rows, cols = own.shape[1:]

    def body(i, carry):
        span = pl.ds(pl.multiple_of(i * tile, tile), tile)
        if transposed:
            part = contract_last(left, w_v[span, :])
        else:
            part = jnp.dot(left, w_v[:, span], preferred_element_type=F32)
        own[m, :, span] = part[:rows].astype(BF16)
        theirs[m, :, span] = part[rows:].astype(BF16)
        return carry

    lax.fori_loop(0, cols // tile, body, 0)


def core_window(ref, width):
    stride = ref.shape[1] // CORES
    first = pl.multiple_of(lax.axis_index("core") * stride, 128)
    return ref.at[:, pl.ds(first, width)]


def product_scatter_kernel(chips, transposed, tile, back, *refs):
    refs = list(refs)
    take = lambda count: [refs.pop(0) for _ in range(count)]
    h_ref, w_ref = take(2)
    back_in = take(6) if back else None
    o_ref = take(1)[0]
    back_out = take(2) if back else None
    h_v, w_v = take(2)
    scratch = take(8)
    w_sem, h_sem = take(2)
    back_scratch = take(8) if back else None
    c, k = lax.axis_index("ctx"), lax.axis_index("core")
    rows = o_ref.shape[0]
    own, theirs = scratch[:2]
    if transposed:
        w_load = pltpu.make_async_copy(core_window(w_ref, w_v.shape[1]), w_v, w_sem)
    else:
        w_load = pltpu.make_async_copy(w_ref, w_v, w_sem)
    w_load.start()
    loads = {}
    for m in block_order(chips):
        for side, span in enumerate(block_rows(chips, rows, m)):
            load = pltpu.make_async_copy(
                h_ref.at[span], h_v.at[block_place(rows, m, side)], h_sem.at[m, side]
            )
            load.start()
            loads[m, side] = load
    fillers, stores = [], []
    if back:
        p_ref, g_ref, key_blk, query_blk, log_ref, a_ref = back_in
        p_v, g_v, a_v, d_v, q_v, dk, dv, back_sem = back_scratch
        copies = [
            pltpu.make_async_copy(source, target, back_sem.at[place])
            for place, (source, target) in enumerate(
                ((p_ref, p_v), (g_ref, g_v), (a_ref, a_v), (d_v, back_out[0]), (q_v, back_out[1]))
            )
        ]
        stores = copies[3:]
        for copy in copies[:3]:
            copy.start()
        parts = attend_back_parts(*back, p_v, g_v, key_blk, query_blk, log_ref, d_v, dk, dv)
        products = first_product_parts(a_v, d_v, q_v, tile)

        def first_part():
            copies[0].wait()
            copies[1].wait()
            parts[0]()

        def first_product():
            copies[2].wait()
            stores[0].start()
            products[0]()

        def last_product():
            products[-1]()
            stores[1].start()

        fillers = [first_part, *parts[1:], first_product, *products[1:-1], last_product]
    greet(chips, c, k)
    w_load.wait()

    def compute(m):
        for side in range(CORES):
            loads[m, side].wait()
        product_terms(h_v[block_place(rows, m), :], w_v, own, theirs, m, transposed, tile)

    exchange(chips, scratch, o_ref, compute, fillers)
    for store in stores:
        store.wait()


def first_product_parts(left, right, target, tile, after=None):
    def part(i):
        span = slice(i * tile, (i + 1) * tile)
        target[span, :] = contract_first(left[:, span], right[...]).astype(BF16)
        if after is not None:
            after(i, span)

    return [functools.partial(part, i) for i in range(left.shape[1] // tile)]


def product_scatter(h, w, chips, ident, transposed, back=None):
    depth = h.shape[1]
    cols = w.shape[0] if transposed else w.shape[1]
    rows = h.shape[0] // (CORES * chips)
    in_vmem = pl.BlockSpec(memory_space=pltpu.VMEM)
    in_place = pl.BlockSpec(memory_space=pl.ANY)
    operands, in_specs = [h, w], [in_place] * 2
    out_shape = [jax.ShapeDtypeStruct((rows, cols), F32)]
    out_specs, back_scratch, sizes = [in_vmem], [], None
    if back is not None:
        proj, grads, blocks, logsums, heads, size, acts = back
        operands += [proj, grads, blocks[:, :, None], blocks[:, None, :], logsums, acts]
        in_specs += [in_place] * 2 + [in_vmem] * 3 + [in_place]
        out_specs += [in_place] * 2
        out_shape.append(jax.ShapeDtypeStruct(proj.shape, BF16))
        out_shape.append(jax.ShapeDtypeStruct((acts.shape[1], proj.shape[1]), BF16))
        back_scratch = [
            pltpu.VMEM(proj.shape, BF16),
            pltpu.VMEM(grads.shape, BF16),
            pltpu.VMEM(acts.shape, BF16),
            pltpu.VMEM(proj.shape, BF16),
            pltpu.VMEM((acts.shape[1], proj.shape[1]), BF16),
            *[pltpu.VMEM((blocks.shape[1], size), F32)] * 2,
            pltpu.SemaphoreType.DMA((5,)),
        ]
        sizes = (heads, size, 256)
    result = pl.pallas_call(
        functools.partial(product_scatter_kernel, chips, transposed, 512, sizes),
        name="product_scatter",
        out_shape=out_shape,
        in_specs=in_specs,
        out_specs=out_specs,
        scratch_shapes=[
            pltpu.VMEM(h.shape, BF16),
            pltpu.VMEM((cols, depth) if transposed else w.shape, BF16),
            *exchange_scratch(chips, rows, cols),
            pltpu.SemaphoreType.DMA,
            pltpu.SemaphoreType.DMA((chips, CORES)),
            *back_scratch,
        ],
        cost_estimate=pl.CostEstimate(flops=1_000_000_000, bytes_accessed=0, transcendentals=0),
        compiler_params=pltpu.CompilerParams(
            collective_id=ident, has_side_effects=True, vmem_limit_bytes=VMEM_LIMIT
        ),
    )(*operands)
    return result if len(out_shape) > 1 else result[0]


def gelu_slope(u):
    scale, cubic = math.sqrt(2.0 / math.pi), 0.044715
    square = u * u
    bend = jnp.tanh(scale * u * (1.0 + cubic * square))
    return 0.5 * (1.0 + bend) + 0.5 * u * (1.0 - bend * bend) * scale * (1.0 + 3.0 * cubic * square)


def hidden_back_kernel(
    chips, tile, g_ref, d_ref, p_ref, u_ref, a_ref, y_ref, unit_ref, inv_ref, gain_ref,
    o_ref, low_ref, sum_ref, s_ref, g_v, p_v, e_v, d_v, u_v, y_v, unit_v, *refs
):
    scratch, (w_sem, load_sem, a_sem, store_sem) = refs[:8], refs[8:]
    own_loads = [
        pltpu.make_async_copy(y_ref, y_v, w_sem.at[2]),
        pltpu.make_async_copy(unit_ref, unit_v, w_sem.at[3]),
    ]
    c, k = lax.axis_index("ctx"), lax.axis_index("core")
    rows = o_ref.shape[0]
    own, theirs = scratch[:2]
    d_load = pltpu.make_async_copy(core_window(d_ref, d_v.shape[1]), d_v, w_sem.at[0])
    u_load = pltpu.make_async_copy(core_window(u_ref, u_v.shape[1]), u_v, w_sem.at[1])
    d_load.start()
    loads, stores = {}, []
    for place, m in enumerate(block_order(chips)):
        if place == 1:
            u_load.start()
        for side, span in enumerate(block_rows(chips, rows, m)):
            for which, (source, target) in enumerate(((g_ref, g_v), (p_ref, p_v))):
                load = pltpu.make_async_copy(
                    source.at[span],
                    target.at[block_place(rows, m, side)],
                    load_sem.at[which, m, side],
                )
                load.start()
                loads.setdefault(m, []).append(load)
    greet(chips, c, k)
    d_load.wait()

    def compute(m):
        block = block_place(rows, m)
        for load in loads[m]:
            load.wait()

        def body(i, carry):
            cols = pl.ds(pl.multiple_of(i * tile, tile), tile)
            part = jnp.dot(g_v[block, :], d_v[:, cols], preferred_element_type=F32)
            e_v[block, cols] = (part * gelu_slope(p_v[block, cols])).astype(BF16)
            return carry

        lax.fori_loop(0, e_v.shape[1] // tile, body, 0)
        if m == block_order(chips)[0]:
            u_load.wait()
        product_terms(e_v[block, :], u_v, own, theirs, m, True, tile)

    a_loads = [
        pltpu.make_async_copy(
            a_ref.at[span], g_v.at[block_place(rows, m, side)], a_sem.at[m, side]
        )
        for m in range(chips)
        for side, span in enumerate(block_rows(chips, rows, m))
    ]

    def load_acts():
        for load in a_loads + own_loads:
            load.start()

    def await_acts():
        for load in a_loads:
            load.wait()

    def store(i, span):
        copy = pltpu.make_async_copy(d_v.at[span], s_ref.at[span], store_sem.at[i])
        copy.start()
        stores.append(copy)

    fillers = [load_acts, await_acts, *first_product_parts(g_v, e_v, d_v, tile, store)]
    exchange(chips, scratch, o_ref, compute, fillers)
    for load in own_loads:
        load.wait()
    total = [jnp.zeros((1, o_ref.shape[1]), F32)] * 2
    step = math.gcd(rows, 64)
    for first in range(0, rows, step):
        span = slice(first, first + step)
        grad, unit = o_ref[span, :], unit_v[span, :]
        total[0] += jnp.sum(grad * unit, axis=0, keepdims=True)
        total[1] += jnp.sum(grad, axis=0, keepdims=True)
        back = normalize_back(grad, unit, inv_ref[span, :], gain_ref[...])
        result = y_v[span, :].astype(F32) + back
        o_ref[span, :] = result
        low_ref[span, :] = result.astype(BF16)
    sum_ref[...] = jnp.concatenate(total)
    for copy in stores:
        copy.wait()


def hidden_back(grads, w_down, pre, w_up, acts, grad_y, unit, inv, gain, chips, ident):
    cols, width = w_up.shape[0], pre.shape[1]
    rows = grads.shape[0] // (CORES * chips)
    tile = 512
    in_place, in_vmem = pl.BlockSpec(memory_space=pl.ANY), pl.BlockSpec(memory_space=pltpu.VMEM)
    return pl.pallas_call(
        functools.partial(hidden_back_kernel, chips, tile),
        name="hidden_back",
        out_shape=[
            jax.ShapeDtypeStruct((rows, cols), F32),
            jax.ShapeDtypeStruct((rows, cols), BF16),
            jax.ShapeDtypeStruct((2, cols), F32),
            jax.ShapeDtypeStruct((cols, width), BF16),
        ],
        in_specs=[in_place] * 7 + [in_vmem] * 2,
        out_specs=[in_vmem] * 3 + [in_place],
        scratch_shapes=[
            pltpu.VMEM(grads.shape, BF16),
            pltpu.VMEM(pre.shape, pre.dtype),
            pltpu.VMEM(pre.shape, BF16),
            pltpu.VMEM((w_down.shape[0], width), BF16),
            pltpu.VMEM((cols, width), BF16),
            pltpu.VMEM((rows, cols), BF16),
            pltpu.VMEM((rows, cols), F32),
            *exchange_scratch(chips, rows, cols),
            pltpu.SemaphoreType.DMA((4,)),
            pltpu.SemaphoreType.DMA((2, chips, CORES)),
            pltpu.SemaphoreType.DMA((chips, CORES)),
            pltpu.SemaphoreType.DMA((cols // tile,)),
        ],
        cost_estimate=pl.CostEstimate(flops=1_000_000_000, bytes_accessed=0, transcendentals=0),
        compiler_params=pltpu.CompilerParams(
            collective_id=ident, has_side_effects=True, vmem_limit_bytes=VMEM_LIMIT
        ),
    )(grads, w_down, pre, w_up, acts, grad_y, unit, inv, gain)


def deal_kernel(chips, planes, b_ref, x_ref, landed, t_ref, heard, *sems):
    send_sem, recv_sem, sum_send, sum_recv = sems
    c, z, k = lax.axis_index("ctx"), lax.axis_index("z"), lax.axis_index("core")
    team, count, width = landed.shape
    peers = [{"ctx": c ^ m, "core": core} for m in range(1, chips) for core in (k, 1 - k)]
    peers.append({"core": 1 - k})
    lines = [{"z": z ^ mask} for mask in range(1, planes)]
    groups = [[{"ctx": c ^ m} for m in range(1, chips)], [{"core": 1 - k}], lines]
    barrier = pltpu.get_barrier_semaphore()
    for friend in peers + lines:
        pl.semaphore_signal(barrier, inc=1, device_id=friend, device_id_type=MESH)
    me = c * CORES + k
    landed[me] = b_ref[me]
    t_ref[...] = x_ref[...]
    pl.semaphore_wait(barrier, len(peers) + len(lines))
    copies = []
    for place, peer in enumerate(peers):
        target = peer.get("ctx", c) * CORES + peer["core"]
        copy = pltpu.make_async_remote_copy(
            src_ref=b_ref.at[target],
            dst_ref=landed.at[me],
            send_sem=send_sem.at[place],
            recv_sem=recv_sem.at[place],
            device_id=peer,
            device_id_type=MESH,
        )
        copies.append(copy)
    slot = 0
    for group in groups:
        sums = []
        for partner in group:
            sums.append(
                pltpu.make_async_remote_copy(
                    src_ref=t_ref,
                    dst_ref=heard.at[slot],
                    send_sem=sum_send.at[slot],
                    recv_sem=sum_recv.at[slot],
                    device_id=partner,
                    device_id_type=MESH,
                )
            )
            slot += 1
        for total in sums:
            total.start()
        if group is groups[0]:
            for copy in copies:
                copy.start()
        for total in sums:
            total.wait()
        for place in range(slot - len(sums), slot):
            t_ref[...] += heard[place]
    for copy in copies:
        copy.wait()


def columns_kernel(counts, *refs):
    blocks, targets = refs[: len(counts)], refs[len(counts) :]
    source = pl.program_id(0)
    for count, block, target in zip(counts, blocks, targets):
        piece = block.shape[2] // count
        whole = target.shape[1] // count
        for part in range(count):
            first = pl.multiple_of(part * whole + source * piece, piece) if count > 1 else 0
            target[:, pl.ds(first, piece)] = block[
                0, :, part * piece : (part + 1) * piece
            ].astype(F32)


def whole_columns(arrays, counts):
    team = arrays[0].shape[0]
    specs = []
    for array, count in zip(arrays, counts):
        rows, width = array.shape[1:]
        if count > 1:
            specs.append(pl.BlockSpec((rows, team * width), lambda i: (0, 0)))
        else:
            specs.append(pl.BlockSpec((rows, width), lambda i: (0, i)))
    return pl.pallas_call(
        functools.partial(columns_kernel, counts),
        name="whole_columns",
        grid=(team,),
        out_shape=[jax.ShapeDtypeStruct((a.shape[1], team * a.shape[2]), F32) for a in arrays],
        in_specs=[pl.BlockSpec((1, *a.shape[1:]), lambda i: (i, 0, 0)) for a in arrays],
        out_specs=specs,
    )(*arrays)


def deal(blocks, x, chips, planes, ident):
    team, count, width = blocks.shape
    in_vmem = pl.BlockSpec(memory_space=pltpu.VMEM)
    steps = chips - 1 + 1 + planes - 1
    return pl.pallas_call(
        functools.partial(deal_kernel, chips, planes),
        name="deal",
        out_shape=[
            jax.ShapeDtypeStruct(blocks.shape, BF16),
            jax.ShapeDtypeStruct(x.shape, F32),
        ],
        in_specs=[in_vmem] * 2,
        out_specs=[in_vmem] * 2,
        scratch_shapes=[
            pltpu.VMEM((steps, *x.shape), F32),
            pltpu.SemaphoreType.DMA((team - 1,)),
            pltpu.SemaphoreType.DMA((team - 1,)),
            pltpu.SemaphoreType.DMA((steps,)),
            pltpu.SemaphoreType.DMA((steps,)),
        ],
        compiler_params=pltpu.CompilerParams(collective_id=ident, has_side_effects=True),
    )(blocks, x)


def attend_kernel(heads, size, step, p_ref, key_blk, query_blk, o_ref, log_ref):
    length = p_ref.shape[0]
    scale = 1.0 / math.sqrt(size)
    key_block = key_blk[0]
    for head in range(heads):
        keys = p_ref[:, (heads + head) * size : (heads + head + 1) * size]
        values = p_ref[:, (2 * heads + head) * size : (2 * heads + head + 1) * size]
        values_t = values.T
        for first in range(0, length, step):
            span = slice(first, first + step)
            queries = p_ref[span, head * size : (head + 1) * size]
            scores = contract_last(keys, queries) * scale
            scores = jnp.where(key_block <= query_blk[0, :, span], scores, -jnp.inf)
            top = jnp.max(scores, axis=0, keepdims=True)
            weights = jnp.exp(scores - top)
            total = jnp.sum(weights, axis=0, keepdims=True)
            prob = (weights * (1.0 / total)).astype(BF16)
            out_t = jnp.dot(values_t, prob, preferred_element_type=F32)
            o_ref[span, head * size : (head + 1) * size] = out_t.T.astype(BF16)
            log_ref[0, head : head + 1, span] = top + jnp.log(total)


def attend_back_parts(
    heads, size, step, p_ref, g_ref, key_blk, query_blk, log_ref, d_ref, dk, dv
):
    length = key_blk.shape[1]
    scale = 1.0 / math.sqrt(size)

    def part(seq, head):
        whole = pl.ds(seq * length, length)
        at_query, at_key, at_value = [
            slice((j * heads + head) * size, (j * heads + head + 1) * size) for j in range(3)
        ]
        keys, values = p_ref[whole, at_key], p_ref[whole, at_value]
        keys_t = keys.T
        key_block = key_blk[seq]
        for first in range(0, length, step):
            here = slice(first, first + step)
            span = pl.ds(seq * length + first, step)
            queries, grads = p_ref[span, at_query], g_ref[span, at_query]
            scores = contract_last(keys, queries) * scale
            shifted = jnp.where(
                key_block <= query_blk[seq, :, here],
                scores - log_ref[seq, head : head + 1, here],
                -jnp.inf,
            )
            prob = jnp.exp(shifted)
            grad_prob = contract_last(values, grads)
            row_dot = jnp.sum(prob * grad_prob, axis=0, keepdims=True)
            grad_raw = (prob * (grad_prob - row_dot) * scale).astype(BF16)
            dk_part = jnp.dot(grad_raw, queries, preferred_element_type=F32)
            dv_part = jnp.dot(prob.astype(BF16), grads, preferred_element_type=F32)
            if first == 0:
                dk[...] = dk_part
                dv[...] = dv_part
            else:
                dk[...] += dk_part
                dv[...] += dv_part
            dq_t = jnp.dot(keys_t, grad_raw, preferred_element_type=F32)
            d_ref[span, at_query] = dq_t.T.astype(BF16)
        d_ref[whole, at_key] = dk[...].astype(BF16)
        d_ref[whole, at_value] = dv[...].astype(BF16)

    return [
        functools.partial(part, seq, head)
        for seq in range(key_blk.shape[0])
        for head in range(heads)
    ]


def attention_specs(length, width, heads):
    wide = pl.BlockSpec((length, 3 * width), lambda s: (s, 0))
    narrow = pl.BlockSpec((length, width), lambda s: (s, 0))
    column = pl.BlockSpec((1, length, 1), lambda s: (s, 0, 0))
    row = pl.BlockSpec((1, 1, length), lambda s: (s, 0, 0))
    logs = pl.BlockSpec((1, heads, length), lambda s: (s, 0, 0))
    return wide, narrow, column, row, logs


def attend(proj, blocks, heads, size):
    length = blocks.shape[1]
    width = heads * size
    wide, narrow, column, row, logs = attention_specs(length, width, heads)
    return pl.pallas_call(
        functools.partial(attend_kernel, heads, size, 256),
        name="attend",
        grid=(blocks.shape[0],),
        out_shape=(
            jax.ShapeDtypeStruct((proj.shape[0], width), BF16),
            jax.ShapeDtypeStruct((blocks.shape[0], heads, length), F32),
        ),
        in_specs=[wide, column, row],
        out_specs=(narrow, logs),
        cost_estimate=pl.CostEstimate(flops=1_000_000_000, bytes_accessed=0, transcendentals=0),
        compiler_params=pltpu.CompilerParams(vmem_limit_bytes=VMEM_LIMIT),
    )(proj, blocks[:, :, None], blocks[:, None, :])


def shards(
    tokens,
    block_ids,
    piece_order,
    norm1_gain,
    norm1_bias,
    w_qkv,
    w_out,
    norm2_gain,
    norm2_bias,
    w_up,
    w_down,
    grad_out,
):
    chips, depth = lax.axis_size("ctx"), lax.axis_size("z")
    c, k = lax.axis_index("ctx"), lax.axis_index("core")
    row_count, model_width = tokens.shape[1:]
    hidden_width = w_up.shape[1]
    size = model_width // HEADS
    team = CORES * chips
    heads = HEADS // team
    head_cols = heads * size
    ff_cols = hidden_width // team
    fsdp = ("z", "core")

    def core_cols(gathered, width, first=0):
        return lax.dynamic_slice_in_dim(gathered, first + k * width, width, 1)

    def across_z(w):
        return lax.all_gather(w, fsdp, axis=0, tiled=True)

    chip_heads = CORES * head_cols
    pieces = []
    for core in range(CORES):
        pieces += [
            (0, part * model_width + core * head_cols, chip_heads, head_cols) for part in range(3)
        ]
        pieces.append((1, core * head_cols, chip_heads, head_cols))
    attn_weights = across_z(pick_columns((w_qkv, w_out), pieces))
    inputs = tokens.reshape(row_count, model_width).astype(F32)
    grad_y = grad_out.reshape(row_count, model_width)
    normed_one, unit_one, inv_one = normalize(inputs, norm1_gain, norm1_bias)
    acts_one = plane_gather(normed_one.astype(BF16), chips, 1)
    acts_one, block_ids, grad_y, w_up, w_down = lax.optimization_barrier(
        (acts_one, block_ids, grad_y, w_up, w_down)
    )
    chip_ff = [(0, 0, CORES * ff_cols, CORES * ff_cols)]
    up_weights = across_z(pick_columns((w_up,), chip_ff))
    down_weights = across_z(pick_columns((w_down,), chip_ff))
    blocks = stored_blocks(block_ids, piece_order, row_count // 2)
    blocks = lax.all_gather(blocks, "core", axis=0, tiled=True)

    grads_y = plane_gather(grad_y, chips, 1)
    my_attn = core_cols(attn_weights, 4 * head_cols)
    out_blocks = my_attn[:, 3 * head_cols :]
    my_out = lax.all_to_all(out_blocks, ("ctx", "core"), split_axis=0, concat_axis=1, tiled=True)
    proj = jnp.dot(acts_one, my_attn[:, : 3 * head_cols], preferred_element_type=F32).astype(BF16)
    attended, logsums = attend(proj, blocks, heads, size)
    residual = inputs + product_scatter(attended, my_out, chips, 2, False)
    normed_two, unit_two, inv_two = normalize(residual, norm2_gain, norm2_bias)
    acts_two = plane_gather(normed_two.astype(BF16), chips, 1)
    up_weights, acts_two = lax.optimization_barrier((up_weights, acts_two))
    my_up = core_cols(up_weights, ff_cols)
    pre_act = jnp.dot(acts_two, my_up, preferred_element_type=F32)
    hidden = jax.nn.gelu(pre_act, approximate=True).astype(BF16)

    def sum_planes(grad):
        parts = grad.reshape(chips, -1, grad.shape[1])
        return lax.psum_scatter(parts, "z", scatter_dimension=1, tiled=True)

    def spread_rows(summed):
        summed = summed.reshape(team, -1, summed.shape[2])
        return lax.all_to_all(summed, ("ctx", "core"), split_axis=0, concat_axis=0, tiled=True)

    down_part = contract_first(grads_y, hidden).astype(BF16)
    down_weights, down_part = lax.optimization_barrier((down_weights, down_part))
    down_sum = sum_planes(down_part)
    grad_res, grad_res_low, norm_two, up_part = hidden_back(
        grads_y, down_weights, pre_act, up_weights, acts_two,
        grad_y, unit_two, inv_two, norm2_gain[None], chips, 3,
    )
    up_sum = sum_planes(up_part)
    grad_attended, out_part = attended_back(grad_res_low, my_out, attended, chips, 7)
    grad_attended, out_part, down_sum = lax.optimization_barrier(
        (grad_attended, out_part, down_sum)
    )
    down_parts = spread_rows(down_sum)
    mixed_sum, grad_proj, proj_part = product_scatter(
        hidden, down_weights, chips, 5, True,
        back=(proj, grad_attended, blocks, logsums, heads, size, acts_one),
    )
    grad_proj, proj_part, up_sum, out_part, down_parts = lax.optimization_barrier(
        (grad_proj, proj_part, up_sum, out_part, down_parts)
    )
    proj_sum = sum_planes(proj_part)
    out_part = out_part.reshape(depth // CORES, CORES, -1, model_width)
    kept, given = [
        lax.dynamic_index_in_dim(out_part, core, 1, keepdims=False) for core in (k, 1 - k)
    ]
    taken = lax.ppermute(given, "core", [(0, 1), (1, 0)])
    up_parts = spread_rows(up_sum)
    kept_first = k == 0
    out_mine = jnp.concatenate(
        [jnp.where(kept_first, kept, taken), jnp.where(kept_first, taken, kept)]
    )
    grad_act_one = product_scatter(grad_proj, attn_weights, chips, 4, True)
    grad_act_one, out_mine, up_parts, proj_sum = lax.optimization_barrier(
        (grad_act_one, out_mine, up_parts, proj_sum)
    )
    grad_wout = lax.psum_scatter(out_mine, "z", scatter_dimension=0, tiled=True)
    grad_wout = grad_wout.reshape(-1, model_width).astype(F32)
    mixed = residual + mixed_sum
    norm_parts = jnp.stack(
        [
            jnp.sum(grad_act_one * unit_one, axis=0),
            jnp.sum(grad_act_one, axis=0),
            norm_two[0],
            norm_two[1],
        ]
    ).reshape(8, -1)
    proj_parts, norm_sums = deal(
        proj_sum.reshape(team, -1, 3 * head_cols), norm_parts, chips, depth, 6
    )
    grad_qkv, grad_up, grad_down = whole_columns((proj_parts, up_parts, down_parts), (3, 1, 1))
    grad_inputs = grad_res + normalize_back(grad_act_one, unit_one, inv_one, norm1_gain)
    out_shape = (1, row_count, model_width)
    return (
        mixed.reshape(out_shape).astype(BF16),
        grad_inputs.reshape(out_shape).astype(BF16),
        grad_qkv,
        grad_wout,
        grad_up,
        grad_down,
        *norm_sums.reshape(4, model_width),
    )


def solution(mesh):
    chips, across = mesh.shape["ctx"], mesh.shape["fsdp"]
    devices = np.asarray(mesh.devices).reshape(chips, across // CORES, CORES)
    cube = Mesh(devices, ("ctx", "z", "core"))
    fsdp = ("z", "core")
    rows = P(fsdp, "ctx", None)
    weight = P(fsdp, None)
    grad = P(("ctx", "z", "core"), None)
    return jax.shard_map(
        shards,
        mesh=cube,
        in_specs=(rows, weight, P(), P(), P(), weight, weight, P(), P(), weight, weight, rows),
        out_specs=(rows, rows, grad, grad, grad, grad, P(), P(), P(), P()),
        check_vma=False,
    )
```

```python
import functools
import math

import jax
import jax.numpy as jnp
import numpy as np
from jax import lax
from jax.experimental import pallas as pl
from jax.experimental.pallas import tpu as pltpu
from jax.sharding import Mesh, PartitionSpec as P

HEADS = 16
CORES = 2
LANES = 2
MESH = pl.DeviceIdType.MESH
VMEM_LIMIT = 56 << 20
norm_eps = 1e-05
F32 = jnp.float32
BF16 = jnp.bfloat16


def stored_blocks(seq_blocks, piece_order, piece_len):
    pieces = seq_blocks.reshape(seq_blocks.shape[0], -1, piece_len)
    return jnp.take(pieces, piece_order, axis=1).reshape(seq_blocks.shape)


def normalize(values, norm_gain, norm_bias):
    center = values - jnp.mean(values, axis=-1, keepdims=True)
    variance = jnp.mean(center * center, axis=-1, keepdims=True)
    inv_std = lax.rsqrt(variance + norm_eps)
    unit_vals = center * inv_std
    return (unit_vals * norm_gain + norm_bias, unit_vals, inv_std)


def normalize_back(grad_normed, unit_vals, inv_std, norm_gain):
    grad_unit = grad_normed * norm_gain
    mean_first = jnp.mean(grad_unit, axis=-1, keepdims=True)
    mean_second = jnp.mean(grad_unit * unit_vals, axis=-1, keepdims=True)
    return inv_std * (grad_unit - mean_first - unit_vals * mean_second)


def contract_last(left_arr, right_arr):
    return lax.dot_general(
        left_arr, right_arr, (((1,), (1,)), ((), ())), preferred_element_type=F32
    )


def contract_first(left_arr, right_arr):
    return lax.dot_general(
        left_arr, right_arr, (((0,), (0,)), ((), ())), preferred_element_type=F32
    )


def chip_bits(chips):
    return [1 << i for i in range(chips.bit_length() - 1)]


def lane_orders(chips):
    bits = chip_bits(chips)
    return [bits[lane:] + bits[:lane] for lane in range(LANES)]


def greet(chips, me_chip, me_core, others=()):
    barrier = pltpu.get_barrier_semaphore()
    friends = [{"ctx": me_chip ^ bit} for bit in chip_bits(chips)] + [{"core": 1 - me_core}]
    friends += others
    for friend in friends:
        pl.semaphore_signal(barrier, inc=1, device_id=friend, device_id_type=MESH)
    pl.semaphore_wait(barrier, len(friends))


def gather_scratch(chips, pieces):
    bits = len(chip_bits(chips))
    return [
        pltpu.SemaphoreType.DMA((bits + 1, chips, LANES, pieces)),
        pltpu.SemaphoreType.DMA((2, chips, LANES, pieces)),
    ]


def gather(chips, pieces, sems, x_ref, o_ref, fillers=(), on_block=None):
    send_sem, recv_sem = sems
    c, k = lax.axis_index("ctx"), lax.axis_index("core")
    rows = x_ref.shape[0]
    piece_rows = rows // (LANES * pieces)
    bits, orders = chip_bits(chips), lane_orders(chips)
    fillers, started = list(fillers), []

    def place(core, chip, lane, piece):
        return pl.ds((core * chips + chip) * rows + (lane * pieces + piece) * piece_rows, piece_rows)

    def send(source, m, lane, piece, step):
        if step < len(bits):
            bit = orders[lane][step]
            device, kind, landing = {"ctx": c ^ bit}, 0, m ^ bit
        else:
            device, kind, landing = {"core": 1 - k}, 1, m
        copy = pltpu.make_async_remote_copy(
            src_ref=source,
            dst_ref=o_ref.at[place(k, c ^ m, lane, piece)],
            send_sem=send_sem.at[step, m, lane, piece],
            recv_sem=recv_sem.at[kind, landing, lane, piece],
            device_id=device,
            device_id_type=MESH,
        )
        copy.start()
        started.append(copy)

    def arrived(kind, m, lane, piece):
        ref = o_ref.at[place(k if kind == 0 else 1 - k, c ^ m, lane, piece)]
        pltpu.make_async_remote_copy(
            src_ref=ref,
            dst_ref=ref,
            send_sem=send_sem.at[0, m, lane, piece],
            recv_sem=recv_sem.at[kind, m, lane, piece],
            device_id={"core": 1 - k},
            device_id_type=MESH,
        ).wait_recv()

    def finish(m):
        if on_block is not None and m:
            on_block(k, m)
        for piece, lane in own:
            arrived(1, m, lane, piece)
        if on_block is not None:
            on_block(1 - k, m)

    own = [(p, l) for p in range(pieces) for l in range(LANES)]
    for piece, lane in own:
        source = x_ref.at[pl.ds((lane * pieces + piece) * piece_rows, piece_rows)]
        for step in range(len(bits)):
            send(source, 0, lane, piece, step)
    for piece, lane in own:
        source = x_ref.at[pl.ds((lane * pieces + piece) * piece_rows, piece_rows)]
        send(source, 0, lane, piece, len(bits))
    items = sorted(
        (max(i for i, b in enumerate(orders[lane]) if m & b), bin(m).count("1"), piece, lane, m)
        for m in range(1, chips)
        for piece, lane in own
    )
    left = {m: len(own) for m in range(1, chips)}
    if on_block is not None:
        on_block(k, 0)
    done = [0]
    for count, (step, _, piece, lane, m) in enumerate(items):
        if fillers and count % max(1, len(items) // len(fillers)) == 0:
            fillers.pop(0)()
        arrived(0, m, lane, piece)
        source = o_ref.at[place(k, c ^ m, lane, piece)]
        for later in range(step + 1, len(bits) + 1):
            send(source, m, lane, piece, later)
        left[m] -= 1
        if left[m] == 0:
            done.append(m)
            finish(done.pop(0))
    for filler in fillers:
        filler()
    for m in done:
        finish(m)
    for copy in started:
        copy.wait_send()


def gather_kernel(chips, pieces, x_ref, o_ref, own_sem, *sems):
    c, k = lax.axis_index("ctx"), lax.axis_index("core")
    rows = x_ref.shape[0]
    local = pltpu.make_async_copy(x_ref, o_ref.at[pl.ds((k * chips + c) * rows, rows)], own_sem)
    local.start()
    greet(chips, c, k)
    gather(chips, pieces, sems, x_ref, o_ref)
    local.wait()


def plane_gather(x, chips, ident, pieces=2):
    rows, cols = x.shape
    return pl.pallas_call(
        functools.partial(gather_kernel, chips, pieces),
        name="plane_gather",
        out_shape=jax.ShapeDtypeStruct((CORES * chips * rows, cols), x.dtype),
        in_specs=[pl.BlockSpec(memory_space=pl.ANY)],
        out_specs=pl.BlockSpec(memory_space=pl.ANY),
        scratch_shapes=[pltpu.SemaphoreType.DMA, *gather_scratch(chips, pieces)],
        cost_estimate=pl.CostEstimate(flops=1_000_000_000, bytes_accessed=0, transcendentals=0),
        compiler_params=pltpu.CompilerParams(collective_id=ident, has_side_effects=True),
    )(x)


def attended_back_kernel(
    chips, pieces, x_ref, w_ref, h_ref, g_ref, s_ref, x_v, own_sem, *sems
):
    c, k = lax.axis_index("ctx"), lax.axis_index("core")
    rows = x_ref.shape[0]

    def span_of(core, m):
        return pl.ds(pl.multiple_of((core * chips + (c ^ m)) * rows, rows), rows)

    local = pltpu.make_async_copy(x_ref, x_v.at[span_of(k, 0)], own_sem)
    local.start()
    greet(chips, c, k)
    local.wait()

    def on_block(core, m):
        span = span_of(core, m)
        g_ref[span, :] = contract_last(x_v[span, :], w_ref[...]).astype(BF16)

    gather(chips, pieces, sems, x_ref, x_v, (), on_block)
    tile = 512
    for i in range(x_v.shape[1] // tile):
        span = slice(i * tile, (i + 1) * tile)
        s_ref[:, span] = contract_first(h_ref[...], x_v[:, span]).astype(BF16)


def attended_back(x, w, attended, chips, ident, pieces=2):
    rows, cols = x.shape
    total = CORES * chips * rows
    in_place, in_vmem = pl.BlockSpec(memory_space=pl.ANY), pl.BlockSpec(memory_space=pltpu.VMEM)
    return pl.pallas_call(
        functools.partial(attended_back_kernel, chips, pieces),
        name="attended_back",
        out_shape=[
            jax.ShapeDtypeStruct((total, w.shape[0]), BF16),
            jax.ShapeDtypeStruct((attended.shape[1], cols), BF16),
        ],
        in_specs=[in_place] + [in_vmem] * 2,
        out_specs=[in_vmem] * 2,
        scratch_shapes=[
            pltpu.VMEM((total, cols), BF16),
            pltpu.SemaphoreType.DMA,
            *gather_scratch(chips, pieces),
        ],
        cost_estimate=pl.CostEstimate(flops=1_000_000_000, bytes_accessed=0, transcendentals=0),
        compiler_params=pltpu.CompilerParams(
            collective_id=ident, has_side_effects=True, vmem_limit_bytes=VMEM_LIMIT
        ),
    )(x, w, attended)


def pick_kernel(pieces, *refs):
    sources, (target, sem) = refs[:-2], refs[-2:]
    c = lax.axis_index("ctx")
    copies, landing = [], 0
    for place, (which, first, step, count) in enumerate(pieces):
        first = pl.multiple_of(first + c * step, 128)
        copy = pltpu.make_async_copy(
            sources[which].at[:, pl.ds(first, count)],
            target.at[:, pl.ds(landing, count)],
            sem.at[place],
        )
        copy.start()
        copies.append(copy)
        landing += count
    for copy in copies:
        copy.wait()


def pick_columns(weights, pieces):
    return pl.pallas_call(
        functools.partial(pick_kernel, pieces),
        name="pick_columns",
        out_shape=jax.ShapeDtypeStruct((weights[0].shape[0], sum(p[3] for p in pieces)), BF16),
        in_specs=[pl.BlockSpec(memory_space=pl.ANY)] * len(weights),
        out_specs=pl.BlockSpec(memory_space=pltpu.VMEM),
        scratch_shapes=[pltpu.SemaphoreType.DMA((len(pieces),))],
    )(*weights)


def scatter_plan(chips):
    orders = lane_orders(chips)
    slots, sends = {}, {}
    for lane in range(LANES):
        count = 0
        for step, bit in enumerate(orders[lane]):
            gone = sum(orders[lane][: step + 1])
            for m in range(chips):
                if m & gone == 0:
                    slots[lane, step, m] = count
                    count += 1
        for m in range(1, chips):
            sends[m, lane] = min(i for i, b in enumerate(orders[lane]) if m & b)
    return orders, slots, sends


def block_order(chips):
    return sorted(range(chips), key=lambda m: (-bin(m).count("1"), m))


def exchange_scratch(chips, rows, cols):
    half = rows // LANES
    return [
        pltpu.VMEM((chips, rows, cols), BF16),
        pltpu.VMEM((chips, rows, cols), BF16),
        pltpu.VMEM((chips, rows, cols), BF16),
        pltpu.VMEM((LANES, chips - 1, half, cols), BF16),
        pltpu.SemaphoreType.DMA((chips, LANES)),
        pltpu.SemaphoreType.DMA((chips, LANES)),
        pltpu.SemaphoreType.DMA((LANES, chips - 1)),
        pltpu.SemaphoreType.DMA((LANES, chips - 1)),
    ]


def exchange(chips, scratch, o_ref, compute, fillers=()):
    own, theirs, from_core, from_chip, core_send, core_recv, chip_send, chip_recv = scratch
    c, k = lax.axis_index("ctx"), lax.axis_index("core")
    half = o_ref.shape[0] // LANES
    orders, slots, sends = scatter_plan(chips)
    waits = []

    def share(m, lane):
        rows = pl.ds(lane * half, half)
        copy = pltpu.make_async_remote_copy(
            src_ref=theirs.at[m, rows],
            dst_ref=from_core.at[m, rows],
            send_sem=core_send.at[m, lane],
            recv_sem=core_recv.at[m, lane],
            device_id={"core": 1 - k},
            device_id_type=MESH,
        )
        copy.start()
        waits.append(copy)
        return copy

    def combine(m, lane, core_copy):
        rows = pl.ds(lane * half, half)
        core_copy.wait_recv()
        total = own[m, rows, :].astype(F32) + from_core[m, rows, :].astype(F32)
        last = sends.get((m, lane), len(orders[lane]))
        for step in range(last):
            slot = slots[lane, step, m]
            landed = from_chip.at[lane, slot]
            pltpu.make_async_remote_copy(
                src_ref=landed,
                dst_ref=landed,
                send_sem=chip_send.at[lane, slot],
                recv_sem=chip_recv.at[lane, slot],
                device_id={"core": 1 - k},
                device_id_type=MESH,
            ).wait_recv()
            total = total + from_chip[lane, slot].astype(F32)
        if m == 0:
            o_ref[rows, :] = total.astype(o_ref.dtype)
            return
        own[m, rows, :] = total.astype(BF16)
        bit = orders[lane][last]
        slot = slots[lane, last, m ^ bit]
        copy = pltpu.make_async_remote_copy(
            src_ref=own.at[m, rows],
            dst_ref=from_chip.at[lane, slot],
            send_sem=chip_send.at[lane, slot],
            recv_sem=chip_recv.at[lane, slot],
            device_id={"ctx": c ^ bit},
            device_id_type=MESH,
        )
        copy.start()
        waits.append(copy)

    fillers, pending, last = list(fillers), [], len(orders[0])

    def settle(level):
        for unit in [u for u in pending if sends.get(u[:2], last) <= level]:
            pending.remove(unit)
            combine(*unit)

    for m in block_order(chips):
        if m == 0:
            settle(0)
        compute(m)
        fresh = [(m, lane, share(m, lane)) for lane in range(LANES)]
        settle(0)
        pending += fresh
    settle(0)
    for level in range(1, last + 1):
        count = -(-len(fillers) // (last + 1 - level))
        for filler in fillers[:count]:
            filler()
        fillers = fillers[count:]
        settle(level)
    for copy in waits:
        copy.wait_send()


def block_rows(chips, rows, m):
    c, k = lax.axis_index("ctx"), lax.axis_index("core")
    starts = [(core * chips + (c ^ m)) * rows for core in (k, 1 - k)]
    return [pl.ds(pl.multiple_of(start, rows), rows) for start in starts]


def block_place(rows, m, side=None):
    if side is None:
        return slice(m * CORES * rows, (m + 1) * CORES * rows)
    return pl.ds((m * CORES + side) * rows, rows)


def product_terms(left, w_v, own, theirs, m, transposed, tile):
    rows, cols = own.shape[1:]

    def body(i, carry):
        span = pl.ds(pl.multiple_of(i * tile, tile), tile)
        if transposed:
            part = contract_last(left, w_v[span, :])
        else:
            part = jnp.dot(left, w_v[:, span], preferred_element_type=F32)
        own[m, :, span] = part[:rows].astype(BF16)
        theirs[m, :, span] = part[rows:].astype(BF16)
        return carry

    lax.fori_loop(0, cols // tile, body, 0)


def core_window(ref, width):
    stride = ref.shape[1] // CORES
    first = pl.multiple_of(lax.axis_index("core") * stride, 128)
    return ref.at[:, pl.ds(first, width)]


def product_scatter_kernel(chips, transposed, tile, back, *refs):
    refs = list(refs)
    take = lambda count: [refs.pop(0) for _ in range(count)]
    h_ref, w_ref = take(2)
    back_in = take(6) if back else None
    o_ref = take(1)[0]
    back_out = take(2) if back else None
    h_v, w_v = take(2)
    scratch = take(8)
    w_sem, h_sem = take(2)
    back_scratch = take(8) if back else None
    c, k = lax.axis_index("ctx"), lax.axis_index("core")
    rows = o_ref.shape[0]
    own, theirs = scratch[:2]
    if transposed:
        w_load = pltpu.make_async_copy(core_window(w_ref, w_v.shape[1]), w_v, w_sem)
    else:
        w_load = pltpu.make_async_copy(w_ref, w_v, w_sem)
    w_load.start()
    loads = {}
    for m in block_order(chips):
        for side, span in enumerate(block_rows(chips, rows, m)):
            load = pltpu.make_async_copy(
                h_ref.at[span], h_v.at[block_place(rows, m, side)], h_sem.at[m, side]
            )
            load.start()
            loads[m, side] = load
    fillers, stores = [], []
    if back:
        p_ref, g_ref, key_blk, query_blk, log_ref, a_ref = back_in
        p_v, g_v, a_v, d_v, q_v, dk, dv, back_sem = back_scratch
        copies = [
            pltpu.make_async_copy(source, target, back_sem.at[place])
            for place, (source, target) in enumerate(
                ((p_ref, p_v), (g_ref, g_v), (a_ref, a_v), (d_v, back_out[0]), (q_v, back_out[1]))
            )
        ]
        stores = copies[3:]
        for copy in copies[:3]:
            copy.start()
        parts = attend_back_parts(*back, p_v, g_v, key_blk, query_blk, log_ref, d_v, dk, dv)
        products = first_product_parts(a_v, d_v, q_v, tile)

        def first_part():
            copies[0].wait()
            copies[1].wait()
            parts[0]()

        def first_product():
            copies[2].wait()
            stores[0].start()
            products[0]()

        def last_product():
            products[-1]()
            stores[1].start()

        fillers = [first_part, *parts[1:], first_product, *products[1:-1], last_product]
    greet(chips, c, k)
    w_load.wait()

    def compute(m):
        for side in range(CORES):
            loads[m, side].wait()
        product_terms(h_v[block_place(rows, m), :], w_v, own, theirs, m, transposed, tile)

    exchange(chips, scratch, o_ref, compute, fillers)
    for store in stores:
        store.wait()


def first_product_parts(left, right, target, tile, after=None):
    def part(i):
        span = slice(i * tile, (i + 1) * tile)
        target[span, :] = contract_first(left[:, span], right[...]).astype(BF16)
        if after is not None:
            after(i, span)

    return [functools.partial(part, i) for i in range(left.shape[1] // tile)]


def product_scatter(h, w, chips, ident, transposed, back=None):
    depth = h.shape[1]
    cols = w.shape[0] if transposed else w.shape[1]
    rows = h.shape[0] // (CORES * chips)
    in_vmem = pl.BlockSpec(memory_space=pltpu.VMEM)
    in_place = pl.BlockSpec(memory_space=pl.ANY)
    operands, in_specs = [h, w], [in_place] * 2
    out_shape = [jax.ShapeDtypeStruct((rows, cols), F32)]
    out_specs, back_scratch, sizes = [in_vmem], [], None
    if back is not None:
        proj, grads, blocks, logsums, heads, size, acts = back
        operands += [proj, grads, blocks[:, :, None], blocks[:, None, :], logsums, acts]
        in_specs += [in_place] * 2 + [in_vmem] * 3 + [in_place]
        out_specs += [in_place] * 2
        out_shape.append(jax.ShapeDtypeStruct(proj.shape, BF16))
        out_shape.append(jax.ShapeDtypeStruct((acts.shape[1], proj.shape[1]), BF16))
        back_scratch = [
            pltpu.VMEM(proj.shape, BF16),
            pltpu.VMEM(grads.shape, BF16),
            pltpu.VMEM(acts.shape, BF16),
            pltpu.VMEM(proj.shape, BF16),
            pltpu.VMEM((acts.shape[1], proj.shape[1]), BF16),
            *[pltpu.VMEM((blocks.shape[1], size), F32)] * 2,
            pltpu.SemaphoreType.DMA((5,)),
        ]
        sizes = (heads, size, 256)
    result = pl.pallas_call(
        functools.partial(product_scatter_kernel, chips, transposed, 512, sizes),
        name="product_scatter",
        out_shape=out_shape,
        in_specs=in_specs,
        out_specs=out_specs,
        scratch_shapes=[
            pltpu.VMEM(h.shape, BF16),
            pltpu.VMEM((cols, depth) if transposed else w.shape, BF16),
            *exchange_scratch(chips, rows, cols),
            pltpu.SemaphoreType.DMA,
            pltpu.SemaphoreType.DMA((chips, CORES)),
            *back_scratch,
        ],
        cost_estimate=pl.CostEstimate(flops=1_000_000_000, bytes_accessed=0, transcendentals=0),
        compiler_params=pltpu.CompilerParams(
            collective_id=ident, has_side_effects=True, vmem_limit_bytes=VMEM_LIMIT
        ),
    )(*operands)
    return result if len(out_shape) > 1 else result[0]


def gelu_slope(u):
    scale, cubic = math.sqrt(2.0 / math.pi), 0.044715
    square = u * u
    bend = jnp.tanh(scale * u * (1.0 + cubic * square))
    return 0.5 * (1.0 + bend) + 0.5 * u * (1.0 - bend * bend) * scale * (1.0 + 3.0 * cubic * square)


def hidden_back_kernel(
    chips, tile, g_ref, d_ref, p_ref, u_ref, a_ref, unit_ref, inv_ref, gain_ref,
    o_ref, low_ref, sum_ref, s_ref, g_v, p_v, e_v, d_v, u_v, a_v, unit_v, *refs
):
    scratch, (w_sem, load_sem, a_sem, store_sem) = refs[:8], refs[8:]
    unit_load = pltpu.make_async_copy(unit_ref, unit_v, w_sem.at[2])
    c, k = lax.axis_index("ctx"), lax.axis_index("core")
    rows = o_ref.shape[0]
    own, theirs = scratch[:2]
    d_load = pltpu.make_async_copy(core_window(d_ref, d_v.shape[1]), d_v, w_sem.at[0])
    u_load = pltpu.make_async_copy(core_window(u_ref, u_v.shape[1]), u_v, w_sem.at[1])
    d_load.start()
    loads, stores = {}, []
    for place, m in enumerate(block_order(chips)):
        if place == 1:
            u_load.start()
        for side, span in enumerate(block_rows(chips, rows, m)):
            for which, (source, target) in enumerate(((g_ref, g_v), (p_ref, p_v))):
                load = pltpu.make_async_copy(
                    source.at[span],
                    target.at[block_place(rows, m, side)],
                    load_sem.at[which, m, side],
                )
                load.start()
                loads.setdefault(m, []).append(load)
    greet(chips, c, k)
    d_load.wait()

    def compute(m):
        block = block_place(rows, m)
        for load in loads[m]:
            load.wait()

        def body(i, carry):
            cols = pl.ds(pl.multiple_of(i * tile, tile), tile)
            part = jnp.dot(g_v[block, :], d_v[:, cols], preferred_element_type=F32)
            e_v[block, cols] = (part * gelu_slope(p_v[block, cols].astype(F32))).astype(BF16)
            return carry

        lax.fori_loop(0, e_v.shape[1] // tile, body, 0)
        if m == block_order(chips)[0]:
            u_load.wait()
        product_terms(e_v[block, :], u_v, own, theirs, m, True, tile)

    a_loads = [
        pltpu.make_async_copy(
            a_ref.at[span], a_v.at[block_place(rows, m, side)], a_sem.at[m, side]
        )
        for m in range(chips)
        for side, span in enumerate(block_rows(chips, rows, m))
    ]

    for load in a_loads + [unit_load]:
        load.start()

    def await_acts():
        for load in a_loads:
            load.wait()

    def store(i, span):
        copy = pltpu.make_async_copy(d_v.at[span], s_ref.at[span], store_sem.at[i])
        copy.start()
        stores.append(copy)

    fillers = [await_acts, *first_product_parts(a_v, e_v, d_v, tile, store)]
    exchange(chips, scratch, o_ref, compute, fillers)
    unit_load.wait()
    mine = block_place(rows, 0, 0).start
    total = [jnp.zeros((1, o_ref.shape[1]), F32)] * 2
    step = math.gcd(rows, 64)
    for first in range(0, rows, step):
        span = slice(first, first + step)
        grad, unit = o_ref[span, :], unit_v[span, :]
        total[0] += jnp.sum(grad * unit, axis=0, keepdims=True)
        total[1] += jnp.sum(grad, axis=0, keepdims=True)
        back = normalize_back(grad, unit, inv_ref[span, :], gain_ref[...])
        result = g_v[pl.ds(mine + first, step), :].astype(F32) + back
        o_ref[span, :] = result
        low_ref[span, :] = result.astype(BF16)
    sum_ref[...] = jnp.concatenate(total)
    for copy in stores:
        copy.wait()


def hidden_back(grads, w_down, pre, w_up, acts, unit, inv, gain, chips, ident):
    cols, width = w_up.shape[0], pre.shape[1]
    rows = grads.shape[0] // (CORES * chips)
    tile = 512
    in_place, in_vmem = pl.BlockSpec(memory_space=pl.ANY), pl.BlockSpec(memory_space=pltpu.VMEM)
    return pl.pallas_call(
        functools.partial(hidden_back_kernel, chips, tile),
        name="hidden_back",
        out_shape=[
            jax.ShapeDtypeStruct((rows, cols), F32),
            jax.ShapeDtypeStruct((rows, cols), BF16),
            jax.ShapeDtypeStruct((2, cols), F32),
            jax.ShapeDtypeStruct((cols, width), BF16),
        ],
        in_specs=[in_place] * 6 + [in_vmem] * 2,
        out_specs=[in_vmem] * 3 + [in_place],
        scratch_shapes=[
            pltpu.VMEM(grads.shape, BF16),
            pltpu.VMEM(pre.shape, pre.dtype),
            pltpu.VMEM(pre.shape, BF16),
            pltpu.VMEM((w_down.shape[0], width), BF16),
            pltpu.VMEM((cols, width), BF16),
            pltpu.VMEM(acts.shape, BF16),
            pltpu.VMEM((rows, cols), F32),
            *exchange_scratch(chips, rows, cols),
            pltpu.SemaphoreType.DMA((3,)),
            pltpu.SemaphoreType.DMA((2, chips, CORES)),
            pltpu.SemaphoreType.DMA((chips, CORES)),
            pltpu.SemaphoreType.DMA((cols // tile,)),
        ],
        cost_estimate=pl.CostEstimate(flops=1_000_000_000, bytes_accessed=0, transcendentals=0),
        compiler_params=pltpu.CompilerParams(
            collective_id=ident, has_side_effects=True, vmem_limit_bytes=VMEM_LIMIT
        ),
    )(grads, w_down, pre, w_up, acts, unit, inv, gain)


def deal_kernel(chips, planes, b_ref, x_ref, landed, t_ref, heard, *sems):
    send_sem, recv_sem, sum_send, sum_recv = sems
    c, z, k = lax.axis_index("ctx"), lax.axis_index("z"), lax.axis_index("core")
    team, count, width = landed.shape
    peers = [{"ctx": c ^ m, "core": core} for m in range(1, chips) for core in (k, 1 - k)]
    peers.append({"core": 1 - k})
    lines = [{"z": z ^ mask} for mask in range(1, planes)]
    groups = [[{"ctx": c ^ m} for m in range(1, chips)], [{"core": 1 - k}], lines]
    barrier = pltpu.get_barrier_semaphore()
    for friend in peers + lines:
        pl.semaphore_signal(barrier, inc=1, device_id=friend, device_id_type=MESH)
    me = c * CORES + k
    landed[me] = b_ref[me]
    t_ref[...] = x_ref[...]
    pl.semaphore_wait(barrier, len(peers) + len(lines))
    copies = []
    for place, peer in enumerate(peers):
        target = peer.get("ctx", c) * CORES + peer["core"]
        copy = pltpu.make_async_remote_copy(
            src_ref=b_ref.at[target],
            dst_ref=landed.at[me],
            send_sem=send_sem.at[place],
            recv_sem=recv_sem.at[place],
            device_id=peer,
            device_id_type=MESH,
        )
        copies.append(copy)
    slot = 0
    for group in groups:
        sums = []
        for partner in group:
            sums.append(
                pltpu.make_async_remote_copy(
                    src_ref=t_ref,
                    dst_ref=heard.at[slot],
                    send_sem=sum_send.at[slot],
                    recv_sem=sum_recv.at[slot],
                    device_id=partner,
                    device_id_type=MESH,
                )
            )
            slot += 1
        for total in sums:
            total.start()
        if group is groups[0]:
            for copy in copies:
                copy.start()
        for total in sums:
            total.wait()
        for place in range(slot - len(sums), slot):
            t_ref[...] += heard[place]
    for copy in copies:
        copy.wait()


def columns_kernel(counts, *refs):
    blocks, targets = refs[: len(counts)], refs[len(counts) :]
    source = pl.program_id(0)
    for count, block, target in zip(counts, blocks, targets):
        piece = block.shape[2] // count
        whole = target.shape[1] // count
        for part in range(count):
            first = pl.multiple_of(part * whole + source * piece, piece) if count > 1 else 0
            target[:, pl.ds(first, piece)] = block[
                0, :, part * piece : (part + 1) * piece
            ].astype(F32)


def whole_columns(arrays, counts):
    team = arrays[0].shape[0]
    specs = []
    for array, count in zip(arrays, counts):
        rows, width = array.shape[1:]
        if count > 1:
            specs.append(pl.BlockSpec((rows, team * width), lambda i: (0, 0)))
        else:
            specs.append(pl.BlockSpec((rows, width), lambda i: (0, i)))
    return pl.pallas_call(
        functools.partial(columns_kernel, counts),
        name="whole_columns",
        grid=(team,),
        out_shape=[jax.ShapeDtypeStruct((a.shape[1], team * a.shape[2]), F32) for a in arrays],
        in_specs=[pl.BlockSpec((1, *a.shape[1:]), lambda i: (i, 0, 0)) for a in arrays],
        out_specs=specs,
    )(*arrays)


def deal(blocks, x, chips, planes, ident):
    team, count, width = blocks.shape
    in_vmem = pl.BlockSpec(memory_space=pltpu.VMEM)
    steps = chips - 1 + 1 + planes - 1
    return pl.pallas_call(
        functools.partial(deal_kernel, chips, planes),
        name="deal",
        out_shape=[
            jax.ShapeDtypeStruct(blocks.shape, BF16),
            jax.ShapeDtypeStruct(x.shape, F32),
        ],
        in_specs=[in_vmem] * 2,
        out_specs=[in_vmem] * 2,
        scratch_shapes=[
            pltpu.VMEM((steps, *x.shape), F32),
            pltpu.SemaphoreType.DMA((team - 1,)),
            pltpu.SemaphoreType.DMA((team - 1,)),
            pltpu.SemaphoreType.DMA((steps,)),
            pltpu.SemaphoreType.DMA((steps,)),
        ],
        compiler_params=pltpu.CompilerParams(collective_id=ident, has_side_effects=True),
    )(blocks, x)


def attend_kernel(heads, size, step, p_ref, key_blk, query_blk, o_ref, log_ref):
    length = p_ref.shape[0]
    scale = 1.0 / math.sqrt(size)
    key_block = key_blk[0]
    for head in range(heads):
        keys = p_ref[:, (heads + head) * size : (heads + head + 1) * size]
        values = p_ref[:, (2 * heads + head) * size : (2 * heads + head + 1) * size]
        values_t = values.T
        for first in range(0, length, step):
            span = slice(first, first + step)
            queries = p_ref[span, head * size : (head + 1) * size]
            scores = contract_last(keys, queries) * scale
            scores = jnp.where(key_block <= query_blk[0, :, span], scores, -jnp.inf)
            top = jnp.max(scores, axis=0, keepdims=True)
            weights = jnp.exp(scores - top)
            total = jnp.sum(weights, axis=0, keepdims=True)
            prob = (weights * (1.0 / total)).astype(BF16)
            out_t = jnp.dot(values_t, prob, preferred_element_type=F32)
            o_ref[span, head * size : (head + 1) * size] = out_t.T.astype(BF16)
            log_ref[0, head : head + 1, span] = top + jnp.log(total)


def attend_back_parts(
    heads, size, step, p_ref, g_ref, key_blk, query_blk, log_ref, d_ref, dk, dv
):
    length = key_blk.shape[1]
    scale = 1.0 / math.sqrt(size)

    def part(seq, head):
        whole = pl.ds(seq * length, length)
        at_query, at_key, at_value = [
            slice((j * heads + head) * size, (j * heads + head + 1) * size) for j in range(3)
        ]
        keys, values = p_ref[whole, at_key], p_ref[whole, at_value]
        keys_t = keys.T
        key_block = key_blk[seq]
        for first in range(0, length, step):
            here = slice(first, first + step)
            span = pl.ds(seq * length + first, step)
            queries, grads = p_ref[span, at_query], g_ref[span, at_query]
            scores = contract_last(keys, queries) * scale
            shifted = jnp.where(
                key_block <= query_blk[seq, :, here],
                scores - log_ref[seq, head : head + 1, here],
                -jnp.inf,
            )
            prob = jnp.exp(shifted)
            grad_prob = contract_last(values, grads)
            row_dot = jnp.sum(prob * grad_prob, axis=0, keepdims=True)
            grad_raw = (prob * (grad_prob - row_dot) * scale).astype(BF16)
            dk_part = jnp.dot(grad_raw, queries, preferred_element_type=F32)
            dv_part = jnp.dot(prob.astype(BF16), grads, preferred_element_type=F32)
            if first == 0:
                dk[...] = dk_part
                dv[...] = dv_part
            else:
                dk[...] += dk_part
                dv[...] += dv_part
            dq_t = jnp.dot(keys_t, grad_raw, preferred_element_type=F32)
            d_ref[span, at_query] = dq_t.T.astype(BF16)
        d_ref[whole, at_key] = dk[...].astype(BF16)
        d_ref[whole, at_value] = dv[...].astype(BF16)

    return [
        functools.partial(part, seq, head)
        for seq in range(key_blk.shape[0])
        for head in range(heads)
    ]


def attention_specs(length, width, heads):
    wide = pl.BlockSpec((length, 3 * width), lambda s: (s, 0))
    narrow = pl.BlockSpec((length, width), lambda s: (s, 0))
    column = pl.BlockSpec((1, length, 1), lambda s: (s, 0, 0))
    row = pl.BlockSpec((1, 1, length), lambda s: (s, 0, 0))
    logs = pl.BlockSpec((1, heads, length), lambda s: (s, 0, 0))
    return wide, narrow, column, row, logs


def attend(proj, blocks, heads, size):
    length = blocks.shape[1]
    width = heads * size
    wide, narrow, column, row, logs = attention_specs(length, width, heads)
    return pl.pallas_call(
        functools.partial(attend_kernel, heads, size, 256),
        name="attend",
        grid=(blocks.shape[0],),
        out_shape=(
            jax.ShapeDtypeStruct((proj.shape[0], width), BF16),
            jax.ShapeDtypeStruct((blocks.shape[0], heads, length), F32),
        ),
        in_specs=[wide, column, row],
        out_specs=(narrow, logs),
        cost_estimate=pl.CostEstimate(flops=1_000_000_000, bytes_accessed=0, transcendentals=0),
        compiler_params=pltpu.CompilerParams(vmem_limit_bytes=VMEM_LIMIT),
    )(proj, blocks[:, :, None], blocks[:, None, :])


def shards(
    tokens,
    block_ids,
    piece_order,
    norm1_gain,
    norm1_bias,
    w_qkv,
    w_out,
    norm2_gain,
    norm2_bias,
    w_up,
    w_down,
    grad_out,
):
    chips, depth = lax.axis_size("ctx"), lax.axis_size("z")
    c, k = lax.axis_index("ctx"), lax.axis_index("core")
    row_count, model_width = tokens.shape[1:]
    hidden_width = w_up.shape[1]
    size = model_width // HEADS
    team = CORES * chips
    heads = HEADS // team
    head_cols = heads * size
    ff_cols = hidden_width // team
    fsdp = ("z", "core")

    def core_cols(gathered, width, first=0):
        return lax.dynamic_slice_in_dim(gathered, first + k * width, width, 1)

    def across_z(w):
        return lax.all_gather(w, fsdp, axis=0, tiled=True)

    chip_heads = CORES * head_cols
    pieces = []
    for core in range(CORES):
        pieces += [
            (0, part * model_width + core * head_cols, chip_heads, head_cols) for part in range(3)
        ]
        pieces.append((1, core * head_cols, chip_heads, head_cols))
    attn_weights = across_z(pick_columns((w_qkv, w_out), pieces))
    inputs = tokens.reshape(row_count, model_width).astype(F32)
    grad_y = grad_out.reshape(row_count, model_width)
    normed_one, unit_one, inv_one = normalize(inputs, norm1_gain, norm1_bias)
    acts_one = plane_gather(normed_one.astype(BF16), chips, 1)
    acts_one, block_ids, grad_y, w_up, w_down = lax.optimization_barrier(
        (acts_one, block_ids, grad_y, w_up, w_down)
    )
    chip_ff = [(0, 0, CORES * ff_cols, CORES * ff_cols)]
    up_weights = across_z(pick_columns((w_up,), chip_ff))
    down_weights = across_z(pick_columns((w_down,), chip_ff))
    blocks = stored_blocks(block_ids, piece_order, row_count // 2)
    blocks = lax.all_gather(blocks, "core", axis=0, tiled=True)

    grads_y = plane_gather(grad_y, chips, 1)
    my_attn = core_cols(attn_weights, 4 * head_cols)
    out_blocks = my_attn[:, 3 * head_cols :]
    my_out = lax.all_to_all(out_blocks, ("ctx", "core"), split_axis=0, concat_axis=1, tiled=True)
    proj = jnp.dot(acts_one, my_attn[:, : 3 * head_cols], preferred_element_type=F32).astype(BF16)
    attended, logsums = attend(proj, blocks, heads, size)
    residual = inputs + product_scatter(attended, my_out, chips, 2, False)
    normed_two, unit_two, inv_two = normalize(residual, norm2_gain, norm2_bias)
    acts_two = plane_gather(normed_two.astype(BF16), chips, 1)
    up_weights, acts_two = lax.optimization_barrier((up_weights, acts_two))
    my_up = core_cols(up_weights, ff_cols)
    pre_act = jnp.dot(acts_two, my_up, preferred_element_type=F32)
    hidden = jax.nn.gelu(pre_act, approximate=True).astype(BF16)

    def sum_planes(grad):
        parts = grad.reshape(chips, -1, grad.shape[1])
        return lax.psum_scatter(parts, "z", scatter_dimension=1, tiled=True)

    def spread_rows(summed):
        summed = summed.reshape(team, -1, summed.shape[2])
        return lax.all_to_all(summed, ("ctx", "core"), split_axis=0, concat_axis=0, tiled=True)

    down_part = contract_first(grads_y, hidden).astype(BF16)
    down_weights, down_part = lax.optimization_barrier((down_weights, down_part))
    down_sum = sum_planes(down_part)
    grad_res, grad_res_low, norm_two, up_part = hidden_back(
        grads_y, down_weights, pre_act.astype(BF16), up_weights, acts_two,
        unit_two, inv_two, norm2_gain[None], chips, 3,
    )
    up_sum = sum_planes(up_part)
    grad_attended, out_part = attended_back(grad_res_low, my_out, attended, chips, 7)
    grad_attended, out_part, down_sum = lax.optimization_barrier(
        (grad_attended, out_part, down_sum)
    )
    down_parts = spread_rows(down_sum)
    mixed_sum, grad_proj, proj_part = product_scatter(
        hidden, down_weights, chips, 5, True,
        back=(proj, grad_attended, blocks, logsums, heads, size, acts_one),
    )
    grad_proj, proj_part, up_sum, out_part, down_parts = lax.optimization_barrier(
        (grad_proj, proj_part, up_sum, out_part, down_parts)
    )
    proj_sum = sum_planes(proj_part)
    out_part = out_part.reshape(depth // CORES, CORES, -1, model_width)
    kept, given = [
        lax.dynamic_index_in_dim(out_part, core, 1, keepdims=False) for core in (k, 1 - k)
    ]
    taken = lax.ppermute(given, "core", [(0, 1), (1, 0)])
    up_parts = spread_rows(up_sum)
    kept_first = k == 0
    out_mine = jnp.concatenate(
        [jnp.where(kept_first, kept, taken), jnp.where(kept_first, taken, kept)]
    )
    grad_act_one = product_scatter(grad_proj, attn_weights, chips, 4, True)
    grad_act_one, out_mine, up_parts, proj_sum = lax.optimization_barrier(
        (grad_act_one, out_mine, up_parts, proj_sum)
    )
    grad_wout = lax.psum_scatter(out_mine, "z", scatter_dimension=0, tiled=True)
    grad_wout = grad_wout.reshape(-1, model_width).astype(F32)
    mixed = residual + mixed_sum
    norm_parts = jnp.stack(
        [
            jnp.sum(grad_act_one * unit_one, axis=0),
            jnp.sum(grad_act_one, axis=0),
            norm_two[0],
            norm_two[1],
        ]
    ).reshape(8, -1)
    proj_parts, norm_sums = deal(
        proj_sum.reshape(team, -1, 3 * head_cols), norm_parts, chips, depth, 6
    )
    grad_qkv, grad_up, grad_down = whole_columns((proj_parts, up_parts, down_parts), (3, 1, 1))
    grad_inputs = grad_res + normalize_back(grad_act_one, unit_one, inv_one, norm1_gain)
    out_shape = (1, row_count, model_width)
    return (
        mixed.reshape(out_shape).astype(BF16),
        grad_inputs.reshape(out_shape).astype(BF16),
        grad_qkv,
        grad_wout,
        grad_up,
        grad_down,
        *norm_sums.reshape(4, model_width),
    )


def solution(mesh):
    chips, across = mesh.shape["ctx"], mesh.shape["fsdp"]
    devices = np.asarray(mesh.devices).reshape(chips, across // CORES, CORES)
    cube = Mesh(devices, ("ctx", "z", "core"))
    fsdp = ("z", "core")
    rows = P(fsdp, "ctx", None)
    weight = P(fsdp, None)
    grad = P(("ctx", "z", "core"), None)
    return jax.shard_map(
        shards,
        mesh=cube,
        in_specs=(rows, weight, P(), P(), P(), weight, weight, P(), P(), weight, weight, rows),
        out_specs=(rows, rows, grad, grad, grad, grad, P(), P(), P(), P()),
        check_vma=False,
    )
```

```python
import functools
import math

import jax
import jax.numpy as jnp
import numpy as np
from jax import lax
from jax.experimental import pallas as pl
from jax.experimental.pallas import tpu as pltpu
from jax.sharding import Mesh, PartitionSpec as P

HEADS = 16
CORES = 2
LANES = 2
MESH = pl.DeviceIdType.MESH
VMEM_LIMIT = 56 << 20
norm_eps = 1e-05
F32 = jnp.float32
BF16 = jnp.bfloat16


def stored_blocks(seq_blocks, piece_order, piece_len):
    pieces = seq_blocks.reshape(seq_blocks.shape[0], -1, piece_len)
    return jnp.take(pieces, piece_order, axis=1).reshape(seq_blocks.shape)


def normalize(values, norm_gain, norm_bias):
    center = values - jnp.mean(values, axis=-1, keepdims=True)
    variance = jnp.mean(center * center, axis=-1, keepdims=True)
    inv_std = lax.rsqrt(variance + norm_eps)
    unit_vals = center * inv_std
    return (unit_vals * norm_gain + norm_bias, unit_vals, inv_std)


def normalize_back(grad_normed, unit_vals, inv_std, norm_gain):
    grad_unit = grad_normed * norm_gain
    mean_first = jnp.mean(grad_unit, axis=-1, keepdims=True)
    mean_second = jnp.mean(grad_unit * unit_vals, axis=-1, keepdims=True)
    return inv_std * (grad_unit - mean_first - unit_vals * mean_second)


def contract_last(left_arr, right_arr):
    return lax.dot_general(
        left_arr, right_arr, (((1,), (1,)), ((), ())), preferred_element_type=F32
    )


def contract_first(left_arr, right_arr):
    return lax.dot_general(
        left_arr, right_arr, (((0,), (0,)), ((), ())), preferred_element_type=F32
    )


def chip_bits(chips):
    return [1 << i for i in range(chips.bit_length() - 1)]


def lane_orders(chips):
    bits = chip_bits(chips)
    return [bits[lane:] + bits[:lane] for lane in range(LANES)]


def greet(chips, me_chip, me_core, others=()):
    barrier = pltpu.get_barrier_semaphore()
    friends = [{"ctx": me_chip ^ bit} for bit in chip_bits(chips)] + [{"core": 1 - me_core}]
    friends += others
    for friend in friends:
        pl.semaphore_signal(barrier, inc=1, device_id=friend, device_id_type=MESH)
    pl.semaphore_wait(barrier, len(friends))


def gather_scratch(chips, pieces):
    bits = len(chip_bits(chips))
    return [
        pltpu.SemaphoreType.DMA((bits + 1, chips, LANES, pieces)),
        pltpu.SemaphoreType.DMA((2, chips, LANES, pieces)),
    ]


def gather(chips, pieces, sems, x_ref, o_ref, fillers=(), on_block=None):
    send_sem, recv_sem = sems
    c, k = lax.axis_index("ctx"), lax.axis_index("core")
    rows = x_ref.shape[0]
    piece_rows = rows // (LANES * pieces)
    bits, orders = chip_bits(chips), lane_orders(chips)
    fillers, started = list(fillers), []

    def place(core, chip, lane, piece):
        return pl.ds((core * chips + chip) * rows + (lane * pieces + piece) * piece_rows, piece_rows)

    def send(source, m, lane, piece, step):
        if step < len(bits):
            bit = orders[lane][step]
            device, kind, landing = {"ctx": c ^ bit}, 0, m ^ bit
        else:
            device, kind, landing = {"core": 1 - k}, 1, m
        copy = pltpu.make_async_remote_copy(
            src_ref=source,
            dst_ref=o_ref.at[place(k, c ^ m, lane, piece)],
            send_sem=send_sem.at[step, m, lane, piece],
            recv_sem=recv_sem.at[kind, landing, lane, piece],
            device_id=device,
            device_id_type=MESH,
        )
        copy.start()
        started.append(copy)

    def arrived(kind, m, lane, piece):
        ref = o_ref.at[place(k if kind == 0 else 1 - k, c ^ m, lane, piece)]
        pltpu.make_async_remote_copy(
            src_ref=ref,
            dst_ref=ref,
            send_sem=send_sem.at[0, m, lane, piece],
            recv_sem=recv_sem.at[kind, m, lane, piece],
            device_id={"core": 1 - k},
            device_id_type=MESH,
        ).wait_recv()

    def finish(m):
        if on_block is not None and m:
            on_block(k, m)
        for piece, lane in own:
            arrived(1, m, lane, piece)
        if on_block is not None:
            on_block(1 - k, m)

    own = [(p, l) for p in range(pieces) for l in range(LANES)]
    for piece, lane in own:
        source = x_ref.at[pl.ds((lane * pieces + piece) * piece_rows, piece_rows)]
        for step in range(len(bits)):
            send(source, 0, lane, piece, step)
    for piece, lane in own:
        source = x_ref.at[pl.ds((lane * pieces + piece) * piece_rows, piece_rows)]
        send(source, 0, lane, piece, len(bits))
    items = sorted(
        (max(i for i, b in enumerate(orders[lane]) if m & b), bin(m).count("1"), piece, lane, m)
        for m in range(1, chips)
        for piece, lane in own
    )
    left = {m: len(own) for m in range(1, chips)}
    if on_block is not None:
        on_block(k, 0)
    done = [0]
    for count, (step, _, piece, lane, m) in enumerate(items):
        if fillers and count % max(1, len(items) // len(fillers)) == 0:
            fillers.pop(0)()
        arrived(0, m, lane, piece)
        source = o_ref.at[place(k, c ^ m, lane, piece)]
        for later in range(step + 1, len(bits) + 1):
            send(source, m, lane, piece, later)
        left[m] -= 1
        if left[m] == 0:
            done.append(m)
            finish(done.pop(0))
    for filler in fillers:
        filler()
    for m in done:
        finish(m)
    for copy in started:
        copy.wait_send()


def gather_kernel(chips, pieces, x_ref, o_ref, own_sem, *sems):
    c, k = lax.axis_index("ctx"), lax.axis_index("core")
    rows = x_ref.shape[0]
    local = pltpu.make_async_copy(x_ref, o_ref.at[pl.ds((k * chips + c) * rows, rows)], own_sem)
    local.start()
    greet(chips, c, k)
    gather(chips, pieces, sems, x_ref, o_ref)
    local.wait()


def plane_gather(x, chips, ident, pieces=2):
    rows, cols = x.shape
    return pl.pallas_call(
        functools.partial(gather_kernel, chips, pieces),
        name="plane_gather",
        out_shape=jax.ShapeDtypeStruct((CORES * chips * rows, cols), x.dtype),
        in_specs=[pl.BlockSpec(memory_space=pl.ANY)],
        out_specs=pl.BlockSpec(memory_space=pl.ANY),
        scratch_shapes=[pltpu.SemaphoreType.DMA, *gather_scratch(chips, pieces)],
        cost_estimate=pl.CostEstimate(flops=1_000_000_000, bytes_accessed=0, transcendentals=0),
        compiler_params=pltpu.CompilerParams(collective_id=ident, has_side_effects=True),
    )(x)


def attended_back_kernel(
    chips, pieces, x_ref, w_ref, h_ref, g_ref, s_ref, x_v, total, own_sem, *sems
):
    c, k = lax.axis_index("ctx"), lax.axis_index("core")
    rows = x_ref.shape[0]

    def span_of(core, m):
        return pl.ds(pl.multiple_of((core * chips + (c ^ m)) * rows, rows), rows)

    local = pltpu.make_async_copy(x_ref, x_v.at[span_of(k, 0)], own_sem)
    local.start()
    greet(chips, c, k)
    local.wait()

    def on_block(core, m):
        span = span_of(core, m)
        g_ref[span, :] = contract_last(x_v[span, :], w_ref[...]).astype(BF16)
        total[...] += contract_first(h_ref[span, :], x_v[span, :])

    total[...] = jnp.zeros_like(total)
    gather(chips, pieces, sems, x_ref, x_v, (), on_block)
    s_ref[...] = total[...].astype(BF16)


def attended_back(x, w, attended, chips, ident, pieces=2):
    rows, cols = x.shape
    total = CORES * chips * rows
    in_place, in_vmem = pl.BlockSpec(memory_space=pl.ANY), pl.BlockSpec(memory_space=pltpu.VMEM)
    return pl.pallas_call(
        functools.partial(attended_back_kernel, chips, pieces),
        name="attended_back",
        out_shape=[
            jax.ShapeDtypeStruct((total, w.shape[0]), BF16),
            jax.ShapeDtypeStruct((attended.shape[1], cols), BF16),
        ],
        in_specs=[in_place] + [in_vmem] * 2,
        out_specs=[in_vmem] * 2,
        scratch_shapes=[
            pltpu.VMEM((total, cols), BF16),
            pltpu.VMEM((attended.shape[1], cols), F32),
            pltpu.SemaphoreType.DMA,
            *gather_scratch(chips, pieces),
        ],
        cost_estimate=pl.CostEstimate(flops=1_000_000_000, bytes_accessed=0, transcendentals=0),
        compiler_params=pltpu.CompilerParams(
            collective_id=ident, has_side_effects=True, vmem_limit_bytes=VMEM_LIMIT
        ),
    )(x, w, attended)


def pick_kernel(pieces, *refs):
    sources, (target, sem) = refs[:-2], refs[-2:]
    c = lax.axis_index("ctx")
    copies, landing = [], 0
    for place, (which, first, step, count) in enumerate(pieces):
        first = pl.multiple_of(first + c * step, 128)
        copy = pltpu.make_async_copy(
            sources[which].at[:, pl.ds(first, count)],
            target.at[:, pl.ds(landing, count)],
            sem.at[place],
        )
        copy.start()
        copies.append(copy)
        landing += count
    for copy in copies:
        copy.wait()


def pick_columns(weights, pieces):
    return pl.pallas_call(
        functools.partial(pick_kernel, pieces),
        name="pick_columns",
        out_shape=jax.ShapeDtypeStruct((weights[0].shape[0], sum(p[3] for p in pieces)), BF16),
        in_specs=[pl.BlockSpec(memory_space=pl.ANY)] * len(weights),
        out_specs=pl.BlockSpec(memory_space=pltpu.VMEM),
        scratch_shapes=[pltpu.SemaphoreType.DMA((len(pieces),))],
    )(*weights)


def scatter_plan(chips):
    orders = lane_orders(chips)
    slots, sends = {}, {}
    for lane in range(LANES):
        count = 0
        for step, bit in enumerate(orders[lane]):
            gone = sum(orders[lane][: step + 1])
            for m in range(chips):
                if m & gone == 0:
                    slots[lane, step, m] = count
                    count += 1
        for m in range(1, chips):
            sends[m, lane] = min(i for i, b in enumerate(orders[lane]) if m & b)
    return orders, slots, sends


def block_order(chips):
    return sorted(range(chips), key=lambda m: (-bin(m).count("1"), m))


def exchange_scratch(chips, rows, cols):
    half = rows // LANES
    return [
        pltpu.VMEM((chips, rows, cols), BF16),
        pltpu.VMEM((chips, rows, cols), BF16),
        pltpu.VMEM((chips, rows, cols), BF16),
        pltpu.VMEM((LANES, chips - 1, half, cols), BF16),
        pltpu.SemaphoreType.DMA((chips, LANES)),
        pltpu.SemaphoreType.DMA((chips, LANES)),
        pltpu.SemaphoreType.DMA((LANES, chips - 1)),
        pltpu.SemaphoreType.DMA((LANES, chips - 1)),
    ]


def exchange(chips, scratch, o_ref, compute, fillers=()):
    own, theirs, from_core, from_chip, core_send, core_recv, chip_send, chip_recv = scratch
    c, k = lax.axis_index("ctx"), lax.axis_index("core")
    half = o_ref.shape[0] // LANES
    orders, slots, sends = scatter_plan(chips)
    waits = []

    def share(m, lane):
        rows = pl.ds(lane * half, half)
        copy = pltpu.make_async_remote_copy(
            src_ref=theirs.at[m, rows],
            dst_ref=from_core.at[m, rows],
            send_sem=core_send.at[m, lane],
            recv_sem=core_recv.at[m, lane],
            device_id={"core": 1 - k},
            device_id_type=MESH,
        )
        copy.start()
        waits.append(copy)
        return copy

    def combine(m, lane, core_copy):
        rows = pl.ds(lane * half, half)
        core_copy.wait_recv()
        total = own[m, rows, :].astype(F32) + from_core[m, rows, :].astype(F32)
        last = sends.get((m, lane), len(orders[lane]))
        for step in range(last):
            slot = slots[lane, step, m]
            landed = from_chip.at[lane, slot]
            pltpu.make_async_remote_copy(
                src_ref=landed,
                dst_ref=landed,
                send_sem=chip_send.at[lane, slot],
                recv_sem=chip_recv.at[lane, slot],
                device_id={"core": 1 - k},
                device_id_type=MESH,
            ).wait_recv()
            total = total + from_chip[lane, slot].astype(F32)
        if m == 0:
            o_ref[rows, :] = total.astype(o_ref.dtype)
            return
        own[m, rows, :] = total.astype(BF16)
        bit = orders[lane][last]
        slot = slots[lane, last, m ^ bit]
        copy = pltpu.make_async_remote_copy(
            src_ref=own.at[m, rows],
            dst_ref=from_chip.at[lane, slot],
            send_sem=chip_send.at[lane, slot],
            recv_sem=chip_recv.at[lane, slot],
            device_id={"ctx": c ^ bit},
            device_id_type=MESH,
        )
        copy.start()
        waits.append(copy)

    fillers, pending, last = list(fillers), [], len(orders[0])

    def settle(level):
        for unit in [u for u in pending if sends.get(u[:2], last) <= level]:
            pending.remove(unit)
            combine(*unit)

    for m in block_order(chips):
        if m == 0:
            settle(0)
        compute(m)
        fresh = [(m, lane, share(m, lane)) for lane in range(LANES)]
        settle(0)
        pending += fresh
    settle(0)
    for level in range(1, last + 1):
        count = -(-len(fillers) // (last + 1 - level))
        for filler in fillers[:count]:
            filler()
        fillers = fillers[count:]
        settle(level)
    for copy in waits:
        copy.wait_send()


def block_rows(chips, rows, m):
    c, k = lax.axis_index("ctx"), lax.axis_index("core")
    starts = [(core * chips + (c ^ m)) * rows for core in (k, 1 - k)]
    return [pl.ds(pl.multiple_of(start, rows), rows) for start in starts]


def block_place(rows, m, side=None):
    if side is None:
        return slice(m * CORES * rows, (m + 1) * CORES * rows)
    return pl.ds((m * CORES + side) * rows, rows)


def product_terms(left, w_v, own, theirs, m, transposed, tile):
    rows, cols = own.shape[1:]

    def body(i, carry):
        span = pl.ds(pl.multiple_of(i * tile, tile), tile)
        if transposed:
            part = contract_last(left, w_v[span, :])
        else:
            part = jnp.dot(left, w_v[:, span], preferred_element_type=F32)
        own[m, :, span] = part[:rows].astype(BF16)
        theirs[m, :, span] = part[rows:].astype(BF16)
        return carry

    lax.fori_loop(0, cols // tile, body, 0)


def core_window(ref, width):
    stride = ref.shape[1] // CORES
    first = pl.multiple_of(lax.axis_index("core") * stride, 128)
    return ref.at[:, pl.ds(first, width)]


def product_scatter_kernel(chips, transposed, tile, back, *refs):
    refs = list(refs)
    take = lambda count: [refs.pop(0) for _ in range(count)]
    h_ref, w_ref = take(2)
    back_in = take(6) if back else None
    o_ref = take(1)[0]
    back_out = take(2) if back else None
    h_v, w_v = take(2)
    scratch = take(8)
    w_sem, h_sem = take(2)
    back_scratch = take(8) if back else None
    c, k = lax.axis_index("ctx"), lax.axis_index("core")
    rows = o_ref.shape[0]
    own, theirs = scratch[:2]
    if transposed:
        w_load = pltpu.make_async_copy(core_window(w_ref, w_v.shape[1]), w_v, w_sem)
    else:
        w_load = pltpu.make_async_copy(w_ref, w_v, w_sem)
    w_load.start()
    loads = {}
    for m in block_order(chips):
        for side, span in enumerate(block_rows(chips, rows, m)):
            load = pltpu.make_async_copy(
                h_ref.at[span], h_v.at[block_place(rows, m, side)], h_sem.at[m, side]
            )
            load.start()
            loads[m, side] = load
    fillers, stores = [], []
    if back:
        p_ref, g_ref, key_blk, query_blk, log_ref, a_ref = back_in
        p_v, g_v, a_v, d_v, q_v, dk, dv, back_sem = back_scratch
        copies = [
            pltpu.make_async_copy(source, target, back_sem.at[place])
            for place, (source, target) in enumerate(
                ((p_ref, p_v), (g_ref, g_v), (a_ref, a_v), (d_v, back_out[0]), (q_v, back_out[1]))
            )
        ]
        stores = copies[3:]
        for copy in copies[:3]:
            copy.start()
        parts = attend_back_parts(*back, p_v, g_v, key_blk, query_blk, log_ref, d_v, dk, dv)
        products = first_product_parts(a_v, d_v, q_v, tile)

        def first_part():
            copies[0].wait()
            copies[1].wait()
            parts[0]()

        def first_product():
            copies[2].wait()
            stores[0].start()
            products[0]()

        def last_product():
            products[-1]()
            stores[1].start()

        fillers = [first_part, *parts[1:], first_product, *products[1:-1], last_product]
    greet(chips, c, k)
    w_load.wait()

    def compute(m):
        for side in range(CORES):
            loads[m, side].wait()
        product_terms(h_v[block_place(rows, m), :], w_v, own, theirs, m, transposed, tile)

    exchange(chips, scratch, o_ref, compute, fillers)
    for store in stores:
        store.wait()


def first_product_parts(left, right, target, tile, after=None):
    def part(i):
        span = slice(i * tile, (i + 1) * tile)
        target[span, :] = contract_first(left[:, span], right[...]).astype(BF16)
        if after is not None:
            after(i, span)

    return [functools.partial(part, i) for i in range(left.shape[1] // tile)]


def product_scatter(h, w, chips, ident, transposed, back=None):
    depth = h.shape[1]
    cols = w.shape[0] if transposed else w.shape[1]
    rows = h.shape[0] // (CORES * chips)
    in_vmem = pl.BlockSpec(memory_space=pltpu.VMEM)
    in_place = pl.BlockSpec(memory_space=pl.ANY)
    operands, in_specs = [h, w], [in_place] * 2
    out_shape = [jax.ShapeDtypeStruct((rows, cols), F32)]
    out_specs, back_scratch, sizes = [in_vmem], [], None
    if back is not None:
        proj, grads, blocks, logsums, heads, size, acts = back
        operands += [proj, grads, blocks[:, :, None], blocks[:, None, :], logsums, acts]
        in_specs += [in_place] * 2 + [in_vmem] * 3 + [in_place]
        out_specs += [in_place] * 2
        out_shape.append(jax.ShapeDtypeStruct(proj.shape, BF16))
        out_shape.append(jax.ShapeDtypeStruct((acts.shape[1], proj.shape[1]), BF16))
        back_scratch = [
            pltpu.VMEM(proj.shape, BF16),
            pltpu.VMEM(grads.shape, BF16),
            pltpu.VMEM(acts.shape, BF16),
            pltpu.VMEM(proj.shape, BF16),
            pltpu.VMEM((acts.shape[1], proj.shape[1]), BF16),
            *[pltpu.VMEM((blocks.shape[1], size), F32)] * 2,
            pltpu.SemaphoreType.DMA((5,)),
        ]
        sizes = (heads, size, 256)
    result = pl.pallas_call(
        functools.partial(product_scatter_kernel, chips, transposed, 512, sizes),
        name="product_scatter",
        out_shape=out_shape,
        in_specs=in_specs,
        out_specs=out_specs,
        scratch_shapes=[
            pltpu.VMEM(h.shape, BF16),
            pltpu.VMEM((cols, depth) if transposed else w.shape, BF16),
            *exchange_scratch(chips, rows, cols),
            pltpu.SemaphoreType.DMA,
            pltpu.SemaphoreType.DMA((chips, CORES)),
            *back_scratch,
        ],
        cost_estimate=pl.CostEstimate(flops=1_000_000_000, bytes_accessed=0, transcendentals=0),
        compiler_params=pltpu.CompilerParams(
            collective_id=ident, has_side_effects=True, vmem_limit_bytes=VMEM_LIMIT
        ),
    )(*operands)
    return result if len(out_shape) > 1 else result[0]


def gelu_slope(u):
    scale, cubic = math.sqrt(2.0 / math.pi), 0.044715
    square = u * u
    bend = jnp.tanh(scale * u * (1.0 + cubic * square))
    return 0.5 * (1.0 + bend) + 0.5 * u * (1.0 - bend * bend) * scale * (1.0 + 3.0 * cubic * square)


def hidden_back_kernel(
    chips, tile, g_ref, d_ref, p_ref, u_ref, a_ref, unit_ref, inv_ref, gain_ref,
    o_ref, low_ref, sum_ref, s_ref, g_v, p_v, e_v, d_v, u_v, a_v, unit_v, *refs
):
    scratch, (w_sem, load_sem, a_sem, store_sem) = refs[:8], refs[8:]
    unit_load = pltpu.make_async_copy(unit_ref, unit_v, w_sem.at[2])
    c, k = lax.axis_index("ctx"), lax.axis_index("core")
    rows = o_ref.shape[0]
    own, theirs = scratch[:2]
    d_load = pltpu.make_async_copy(core_window(d_ref, d_v.shape[1]), d_v, w_sem.at[0])
    u_load = pltpu.make_async_copy(core_window(u_ref, u_v.shape[1]), u_v, w_sem.at[1])
    d_load.start()
    loads, stores = {}, []
    for place, m in enumerate(block_order(chips)):
        if place == 1:
            u_load.start()
        for side, span in enumerate(block_rows(chips, rows, m)):
            for which, (source, target) in enumerate(((g_ref, g_v), (p_ref, p_v))):
                load = pltpu.make_async_copy(
                    source.at[span],
                    target.at[block_place(rows, m, side)],
                    load_sem.at[which, m, side],
                )
                load.start()
                loads.setdefault(m, []).append(load)
    greet(chips, c, k)
    d_load.wait()

    def compute(m):
        block = block_place(rows, m)
        for load in loads[m]:
            load.wait()

        def body(i, carry):
            cols = pl.ds(pl.multiple_of(i * tile, tile), tile)
            part = jnp.dot(g_v[block, :], d_v[:, cols], preferred_element_type=F32)
            e_v[block, cols] = (part * gelu_slope(p_v[block, cols].astype(F32))).astype(BF16)
            return carry

        lax.fori_loop(0, e_v.shape[1] // tile, body, 0)
        if m == block_order(chips)[0]:
            u_load.wait()
        product_terms(e_v[block, :], u_v, own, theirs, m, True, tile)

    a_loads = [
        pltpu.make_async_copy(
            a_ref.at[span], a_v.at[block_place(rows, m, side)], a_sem.at[m, side]
        )
        for m in range(chips)
        for side, span in enumerate(block_rows(chips, rows, m))
    ]

    for load in a_loads + [unit_load]:
        load.start()

    def await_acts():
        for load in a_loads:
            load.wait()

    def store(i, span):
        copy = pltpu.make_async_copy(d_v.at[span], s_ref.at[span], store_sem.at[i])
        copy.start()
        stores.append(copy)

    fillers = [await_acts, *first_product_parts(a_v, e_v, d_v, tile, store)]
    exchange(chips, scratch, o_ref, compute, fillers)
    unit_load.wait()
    mine = block_place(rows, 0, 0).start
    total = [jnp.zeros((1, o_ref.shape[1]), F32)] * 2
    step = math.gcd(rows, 64)
    for first in range(0, rows, step):
        span = slice(first, first + step)
        grad, unit = o_ref[span, :], unit_v[span, :]
        total[0] += jnp.sum(grad * unit, axis=0, keepdims=True)
        total[1] += jnp.sum(grad, axis=0, keepdims=True)
        back = normalize_back(grad, unit, inv_ref[span, :], gain_ref[...])
        result = g_v[pl.ds(mine + first, step), :].astype(F32) + back
        o_ref[span, :] = result
        low_ref[span, :] = result.astype(BF16)
    sum_ref[...] = jnp.concatenate(total)
    for copy in stores:
        copy.wait()


def hidden_back(grads, w_down, pre, w_up, acts, unit, inv, gain, chips, ident):
    cols, width = w_up.shape[0], pre.shape[1]
    rows = grads.shape[0] // (CORES * chips)
    tile = 512
    in_place, in_vmem = pl.BlockSpec(memory_space=pl.ANY), pl.BlockSpec(memory_space=pltpu.VMEM)
    return pl.pallas_call(
        functools.partial(hidden_back_kernel, chips, tile),
        name="hidden_back",
        out_shape=[
            jax.ShapeDtypeStruct((rows, cols), F32),
            jax.ShapeDtypeStruct((rows, cols), BF16),
            jax.ShapeDtypeStruct((2, cols), F32),
            jax.ShapeDtypeStruct((cols, width), BF16),
        ],
        in_specs=[in_place] * 6 + [in_vmem] * 2,
        out_specs=[in_vmem] * 3 + [in_place],
        scratch_shapes=[
            pltpu.VMEM(grads.shape, BF16),
            pltpu.VMEM(pre.shape, pre.dtype),
            pltpu.VMEM(pre.shape, BF16),
            pltpu.VMEM((w_down.shape[0], width), BF16),
            pltpu.VMEM((cols, width), BF16),
            pltpu.VMEM(acts.shape, BF16),
            pltpu.VMEM((rows, cols), F32),
            *exchange_scratch(chips, rows, cols),
            pltpu.SemaphoreType.DMA((3,)),
            pltpu.SemaphoreType.DMA((2, chips, CORES)),
            pltpu.SemaphoreType.DMA((chips, CORES)),
            pltpu.SemaphoreType.DMA((cols // tile,)),
        ],
        cost_estimate=pl.CostEstimate(flops=1_000_000_000, bytes_accessed=0, transcendentals=0),
        compiler_params=pltpu.CompilerParams(
            collective_id=ident, has_side_effects=True, vmem_limit_bytes=VMEM_LIMIT
        ),
    )(grads, w_down, pre, w_up, acts, unit, inv, gain)


def deal_kernel(chips, planes, b_ref, x_ref, landed, t_ref, heard, *sems):
    send_sem, recv_sem, sum_send, sum_recv = sems
    c, z, k = lax.axis_index("ctx"), lax.axis_index("z"), lax.axis_index("core")
    team, count, width = landed.shape
    peers = [{"ctx": c ^ m, "core": core} for m in range(1, chips) for core in (k, 1 - k)]
    peers.append({"core": 1 - k})
    lines = [{"z": z ^ mask} for mask in range(1, planes)]
    groups = [[{"ctx": c ^ m} for m in range(1, chips)], [{"core": 1 - k}], lines]
    barrier = pltpu.get_barrier_semaphore()
    for friend in peers + lines:
        pl.semaphore_signal(barrier, inc=1, device_id=friend, device_id_type=MESH)
    me = c * CORES + k
    landed[me] = b_ref[me]
    t_ref[...] = x_ref[...]
    pl.semaphore_wait(barrier, len(peers) + len(lines))
    copies = []
    for place, peer in enumerate(peers):
        target = peer.get("ctx", c) * CORES + peer["core"]
        copy = pltpu.make_async_remote_copy(
            src_ref=b_ref.at[target],
            dst_ref=landed.at[me],
            send_sem=send_sem.at[place],
            recv_sem=recv_sem.at[place],
            device_id=peer,
            device_id_type=MESH,
        )
        copies.append(copy)
    slot = 0
    for group in groups:
        sums = []
        for partner in group:
            sums.append(
                pltpu.make_async_remote_copy(
                    src_ref=t_ref,
                    dst_ref=heard.at[slot],
                    send_sem=sum_send.at[slot],
                    recv_sem=sum_recv.at[slot],
                    device_id=partner,
                    device_id_type=MESH,
                )
            )
            slot += 1
        for total in sums:
            total.start()
        if group is groups[0]:
            for copy in copies:
                copy.start()
        for total in sums:
            total.wait()
        for place in range(slot - len(sums), slot):
            t_ref[...] += heard[place]
    for copy in copies:
        copy.wait()


def columns_kernel(counts, *refs):
    blocks, targets = refs[: len(counts)], refs[len(counts) :]
    source = pl.program_id(0)
    for count, block, target in zip(counts, blocks, targets):
        piece = block.shape[2] // count
        whole = target.shape[1] // count
        for part in range(count):
            first = pl.multiple_of(part * whole + source * piece, piece) if count > 1 else 0
            target[:, pl.ds(first, piece)] = block[
                0, :, part * piece : (part + 1) * piece
            ].astype(F32)


def whole_columns(arrays, counts):
    team = arrays[0].shape[0]
    specs = []
    for array, count in zip(arrays, counts):
        rows, width = array.shape[1:]
        if count > 1:
            specs.append(pl.BlockSpec((rows, team * width), lambda i: (0, 0)))
        else:
            specs.append(pl.BlockSpec((rows, width), lambda i: (0, i)))
    return pl.pallas_call(
        functools.partial(columns_kernel, counts),
        name="whole_columns",
        grid=(team,),
        out_shape=[jax.ShapeDtypeStruct((a.shape[1], team * a.shape[2]), F32) for a in arrays],
        in_specs=[pl.BlockSpec((1, *a.shape[1:]), lambda i: (i, 0, 0)) for a in arrays],
        out_specs=specs,
    )(*arrays)


def deal(blocks, x, chips, planes, ident):
    team, count, width = blocks.shape
    in_vmem = pl.BlockSpec(memory_space=pltpu.VMEM)
    steps = chips - 1 + 1 + planes - 1
    return pl.pallas_call(
        functools.partial(deal_kernel, chips, planes),
        name="deal",
        out_shape=[
            jax.ShapeDtypeStruct(blocks.shape, BF16),
            jax.ShapeDtypeStruct(x.shape, F32),
        ],
        in_specs=[in_vmem] * 2,
        out_specs=[in_vmem] * 2,
        scratch_shapes=[
            pltpu.VMEM((steps, *x.shape), F32),
            pltpu.SemaphoreType.DMA((team - 1,)),
            pltpu.SemaphoreType.DMA((team - 1,)),
            pltpu.SemaphoreType.DMA((steps,)),
            pltpu.SemaphoreType.DMA((steps,)),
        ],
        compiler_params=pltpu.CompilerParams(collective_id=ident, has_side_effects=True),
    )(blocks, x)


def attend_kernel(heads, size, step, p_ref, key_blk, query_blk, o_ref, log_ref):
    length = p_ref.shape[0]
    scale = 1.0 / math.sqrt(size)
    key_block = key_blk[0]
    for head in range(heads):
        keys = p_ref[:, (heads + head) * size : (heads + head + 1) * size]
        values = p_ref[:, (2 * heads + head) * size : (2 * heads + head + 1) * size]
        values_t = values.T
        for first in range(0, length, step):
            span = slice(first, first + step)
            queries = p_ref[span, head * size : (head + 1) * size]
            scores = contract_last(keys, queries) * scale
            scores = jnp.where(key_block <= query_blk[0, :, span], scores, -jnp.inf)
            top = jnp.max(scores, axis=0, keepdims=True)
            weights = jnp.exp(scores - top)
            total = jnp.sum(weights, axis=0, keepdims=True)
            prob = (weights * (1.0 / total)).astype(BF16)
            out_t = jnp.dot(values_t, prob, preferred_element_type=F32)
            o_ref[span, head * size : (head + 1) * size] = out_t.T.astype(BF16)
            log_ref[0, head : head + 1, span] = top + jnp.log(total)


def attend_back_parts(
    heads, size, step, p_ref, g_ref, key_blk, query_blk, log_ref, d_ref, dk, dv
):
    length = key_blk.shape[1]
    scale = 1.0 / math.sqrt(size)

    def part(seq, head):
        whole = pl.ds(seq * length, length)
        at_query, at_key, at_value = [
            slice((j * heads + head) * size, (j * heads + head + 1) * size) for j in range(3)
        ]
        keys, values = p_ref[whole, at_key], p_ref[whole, at_value]
        keys_t = keys.T
        key_block = key_blk[seq]
        for first in range(0, length, step):
            here = slice(first, first + step)
            span = pl.ds(seq * length + first, step)
            queries, grads = p_ref[span, at_query], g_ref[span, at_query]
            scores = contract_last(keys, queries) * scale
            shifted = jnp.where(
                key_block <= query_blk[seq, :, here],
                scores - log_ref[seq, head : head + 1, here],
                -jnp.inf,
            )
            prob = jnp.exp(shifted)
            grad_prob = contract_last(values, grads)
            row_dot = jnp.sum(prob * grad_prob, axis=0, keepdims=True)
            grad_raw = (prob * (grad_prob - row_dot) * scale).astype(BF16)
            dk_part = jnp.dot(grad_raw, queries, preferred_element_type=F32)
            dv_part = jnp.dot(prob.astype(BF16), grads, preferred_element_type=F32)
            if first == 0:
                dk[...] = dk_part
                dv[...] = dv_part
            else:
                dk[...] += dk_part
                dv[...] += dv_part
            dq_t = jnp.dot(keys_t, grad_raw, preferred_element_type=F32)
            d_ref[span, at_query] = dq_t.T.astype(BF16)
        d_ref[whole, at_key] = dk[...].astype(BF16)
        d_ref[whole, at_value] = dv[...].astype(BF16)

    return [
        functools.partial(part, seq, head)
        for seq in range(key_blk.shape[0])
        for head in range(heads)
    ]


def attention_specs(length, width, heads):
    wide = pl.BlockSpec((length, 3 * width), lambda s: (s, 0))
    narrow = pl.BlockSpec((length, width), lambda s: (s, 0))
    column = pl.BlockSpec((1, length, 1), lambda s: (s, 0, 0))
    row = pl.BlockSpec((1, 1, length), lambda s: (s, 0, 0))
    logs = pl.BlockSpec((1, heads, length), lambda s: (s, 0, 0))
    return wide, narrow, column, row, logs


def attend(proj, blocks, heads, size):
    length = blocks.shape[1]
    width = heads * size
    wide, narrow, column, row, logs = attention_specs(length, width, heads)
    return pl.pallas_call(
        functools.partial(attend_kernel, heads, size, 256),
        name="attend",
        grid=(blocks.shape[0],),
        out_shape=(
            jax.ShapeDtypeStruct((proj.shape[0], width), BF16),
            jax.ShapeDtypeStruct((blocks.shape[0], heads, length), F32),
        ),
        in_specs=[wide, column, row],
        out_specs=(narrow, logs),
        cost_estimate=pl.CostEstimate(flops=1_000_000_000, bytes_accessed=0, transcendentals=0),
        compiler_params=pltpu.CompilerParams(vmem_limit_bytes=VMEM_LIMIT),
    )(proj, blocks[:, :, None], blocks[:, None, :])


def shards(
    tokens,
    block_ids,
    piece_order,
    norm1_gain,
    norm1_bias,
    w_qkv,
    w_out,
    norm2_gain,
    norm2_bias,
    w_up,
    w_down,
    grad_out,
):
    chips, depth = lax.axis_size("ctx"), lax.axis_size("z")
    c, k = lax.axis_index("ctx"), lax.axis_index("core")
    row_count, model_width = tokens.shape[1:]
    hidden_width = w_up.shape[1]
    size = model_width // HEADS
    team = CORES * chips
    heads = HEADS // team
    head_cols = heads * size
    ff_cols = hidden_width // team
    fsdp = ("z", "core")

    def core_cols(gathered, width, first=0):
        return lax.dynamic_slice_in_dim(gathered, first + k * width, width, 1)

    def across_z(w):
        return lax.all_gather(w, fsdp, axis=0, tiled=True)

    chip_heads = CORES * head_cols
    pieces = []
    for core in range(CORES):
        pieces += [
            (0, part * model_width + core * head_cols, chip_heads, head_cols) for part in range(3)
        ]
        pieces.append((1, core * head_cols, chip_heads, head_cols))
    attn_weights = across_z(pick_columns((w_qkv, w_out), pieces))
    inputs = tokens.reshape(row_count, model_width).astype(F32)
    grad_y = grad_out.reshape(row_count, model_width)
    normed_one, unit_one, inv_one = normalize(inputs, norm1_gain, norm1_bias)
    acts_one = plane_gather(normed_one.astype(BF16), chips, 1)
    acts_one, block_ids, grad_y, w_up, w_down = lax.optimization_barrier(
        (acts_one, block_ids, grad_y, w_up, w_down)
    )
    chip_ff = [(0, 0, CORES * ff_cols, CORES * ff_cols)]
    up_weights = across_z(pick_columns((w_up,), chip_ff))
    down_weights = across_z(pick_columns((w_down,), chip_ff))
    blocks = stored_blocks(block_ids, piece_order, row_count // 2)
    blocks = lax.all_gather(blocks, "core", axis=0, tiled=True)

    grads_y = plane_gather(grad_y, chips, 1)
    my_attn = core_cols(attn_weights, 4 * head_cols)
    out_blocks = my_attn[:, 3 * head_cols :]
    my_out = lax.all_to_all(out_blocks, ("ctx", "core"), split_axis=0, concat_axis=1, tiled=True)
    proj = jnp.dot(acts_one, my_attn[:, : 3 * head_cols], preferred_element_type=F32).astype(BF16)
    attended, logsums = attend(proj, blocks, heads, size)
    residual = inputs + product_scatter(attended, my_out, chips, 2, False)
    normed_two, unit_two, inv_two = normalize(residual, norm2_gain, norm2_bias)
    acts_two = plane_gather(normed_two.astype(BF16), chips, 1)
    up_weights, acts_two = lax.optimization_barrier((up_weights, acts_two))
    my_up = core_cols(up_weights, ff_cols)
    pre_act = jnp.dot(acts_two, my_up, preferred_element_type=F32)
    hidden = jax.nn.gelu(pre_act, approximate=True).astype(BF16)

    def sum_planes(grad):
        parts = grad.reshape(chips, -1, grad.shape[1])
        return lax.psum_scatter(parts, "z", scatter_dimension=1, tiled=True)

    def spread_rows(summed):
        summed = summed.reshape(team, -1, summed.shape[2])
        return lax.all_to_all(summed, ("ctx", "core"), split_axis=0, concat_axis=0, tiled=True)

    down_part = contract_first(grads_y, hidden).astype(BF16)
    down_weights, down_part = lax.optimization_barrier((down_weights, down_part))
    down_sum = sum_planes(down_part)
    grad_res, grad_res_low, norm_two, up_part = hidden_back(
        grads_y, down_weights, pre_act.astype(BF16), up_weights, acts_two,
        unit_two, inv_two, norm2_gain[None], chips, 3,
    )
    up_sum = sum_planes(up_part)
    grad_attended, out_part = attended_back(grad_res_low, my_out, attended, chips, 7)
    grad_attended, out_part, down_sum = lax.optimization_barrier(
        (grad_attended, out_part, down_sum)
    )
    down_parts = spread_rows(down_sum)
    mixed_sum, grad_proj, proj_part = product_scatter(
        hidden, down_weights, chips, 5, True,
        back=(proj, grad_attended, blocks, logsums, heads, size, acts_one),
    )
    grad_proj, proj_part, up_sum, out_part, down_parts = lax.optimization_barrier(
        (grad_proj, proj_part, up_sum, out_part, down_parts)
    )
    proj_sum = sum_planes(proj_part)
    out_part = out_part.reshape(depth // CORES, CORES, -1, model_width)
    kept, given = [
        lax.dynamic_index_in_dim(out_part, core, 1, keepdims=False) for core in (k, 1 - k)
    ]
    taken = lax.ppermute(given, "core", [(0, 1), (1, 0)])
    up_parts = spread_rows(up_sum)
    kept_first = k == 0
    out_mine = jnp.concatenate(
        [jnp.where(kept_first, kept, taken), jnp.where(kept_first, taken, kept)]
    )
    grad_act_one = product_scatter(grad_proj, attn_weights, chips, 4, True)
    grad_act_one, out_mine, up_parts, proj_sum = lax.optimization_barrier(
        (grad_act_one, out_mine, up_parts, proj_sum)
    )
    grad_wout = lax.psum_scatter(out_mine, "z", scatter_dimension=0, tiled=True)
    grad_wout = grad_wout.reshape(-1, model_width).astype(F32)
    mixed = residual + mixed_sum
    norm_parts = jnp.stack(
        [
            jnp.sum(grad_act_one * unit_one, axis=0),
            jnp.sum(grad_act_one, axis=0),
            norm_two[0],
            norm_two[1],
        ]
    ).reshape(8, -1)
    proj_parts, norm_sums = deal(
        proj_sum.reshape(team, -1, 3 * head_cols), norm_parts, chips, depth, 6
    )
    grad_qkv, grad_up, grad_down = whole_columns((proj_parts, up_parts, down_parts), (3, 1, 1))
    grad_inputs = grad_res + normalize_back(grad_act_one, unit_one, inv_one, norm1_gain)
    out_shape = (1, row_count, model_width)
    return (
        mixed.reshape(out_shape).astype(BF16),
        grad_inputs.reshape(out_shape).astype(BF16),
        grad_qkv,
        grad_wout,
        grad_up,
        grad_down,
        *norm_sums.reshape(4, model_width),
    )


def solution(mesh):
    chips, across = mesh.shape["ctx"], mesh.shape["fsdp"]
    devices = np.asarray(mesh.devices).reshape(chips, across // CORES, CORES)
    cube = Mesh(devices, ("ctx", "z", "core"))
    fsdp = ("z", "core")
    rows = P(fsdp, "ctx", None)
    weight = P(fsdp, None)
    grad = P(("ctx", "z", "core"), None)
    return jax.shard_map(
        shards,
        mesh=cube,
        in_specs=(rows, weight, P(), P(), P(), weight, weight, P(), P(), weight, weight, rows),
        out_specs=(rows, rows, grad, grad, grad, grad, P(), P(), P(), P()),
        check_vma=False,
    )
```
